256 devices in a mesh: band: 64 (over x, y_lo, z), comp: 2 (over y_hi), tile: 2 (over core).
Axes of the slice: x: 4, y: 4 (y_hi: 2, y_lo: 2; y = y_hi * 2 + y_lo), z: 8, core: 2. Of those that a mesh axis runs over, the one named last changes fastest.
Arguments:
- atmosphere: bfloat16 [192, 384, 768], P('band', None, ('comp', 'tile')), may hold values from -6 to 6
- spec_weight: float32 [2, 2, 2, 768, 96], P(None, None, None, ('comp', 'tile')), may hold values from -0.625 to 0.625
- spec_bias: float32 [2, 2, 2, 768], P(None, None, None, ('comp', 'tile')), may hold values from -4 to 4
- norm_gain: float32 [2, 2, 768], replicated, may hold values from 0.25 to 1.75
- norm_shift: float32 [2, 2, 768], replicated, may hold values from -3 to 3
- fc_in: bfloat16 [2, 768, 3072], P(None, None, ('comp', 'tile')), may hold values from -0.21875 to 0.21875
- fc_out: bfloat16 [2, 3072, 768], P(None, ('comp', 'tile')), may hold values from -0.109375 to 0.109375
- flux_head: bfloat16 [768, 8], P(('comp', 'tile')), may hold values from -0.21875 to 0.21875
- flux_embed: float32 [8, 256], replicated, may hold values from -2 to 2
- ocean_state: bfloat16 [384, 768, 256], P('band', ('comp', 'tile')), may hold values from -6 to 6
- sea_mask: int32 [384, 768], P('band', ('comp', 'tile')), may hold values 0 or 1
- depth_kernel: float32 [7, 7, 256], replicated, may hold values from -0.875 to 0.875
- ocean_gain: float32 [256], replicated, may hold values from 0.25 to 1.75
- ocean_shift: float32 [256], replicated, may hold values from -3 to 3
- ocean_in: bfloat16 [256, 1024], replicated, may hold values from -0.375 to 0.375
- ocean_out: bfloat16 [1024, 256], replicated, may hold values from -0.1875 to 0.1875
- layer_scale: float32 [256], replicated, may hold values from 0.3 to 1
- field_head: float32 [256, 4], replicated, may hold values from -0.375 to 0.375
- patch_embed: float32 [16, 768], P(None, ('comp', 'tile')), may hold values from -1.5 to 1.5
Outputs:
- atmosphere_next: bfloat16 [192, 384, 768], P('band', None, ('comp', 'tile'))
- ocean_next: bfloat16 [384, 768, 256], P('band', ('comp', 'tile'))
- surface_fields: float32 [384, 768, 4], P('band', ('comp', 'tile'))
The draws below stay inside these ranges and needn't reach their ends.
All inputs are finite; a program needn't handle non-finite values. No bound on the sum of `sea_mask` on one device may be relied on, other than what follows from the above.
Results may differ from the reference program's by a relative error of at most 0.0095.
Values may be sent and summed in bfloat16 or wider, within the bound.
A program may use at most 128 MiB of HBM per device.

```python
import math
import jax
import jax.numpy as jnp
from jax import lax

LAT = 192
LON = 384
D = 768
FFH = 3072
OC = 256
OFF = 1024
FLUX = 8
FIELDS = 4
BS = 96
KLON = 192
OLAT = 384
OLON = 768
PATCH = 16


def touch_ends(array, rng, least, high):
    index_at = [jax.random.randint(jax.random.fold_in(rng, axis), (), 0, length) for axis, length in enumerate(array.shape)]
    longest = array.shape.index(max(array.shape))
    next_to = index_at[:longest] + [(index_at[longest] + 1) % array.shape[longest]] + index_at[longest + 1:]
    return array.at[tuple(index_at)].set(least).at[tuple(next_to)].set(high)


def block_levels(key, extent, cuts, low, largest):
    gain = 1.0
    for dim, blocks in cuts:
        heights = jax.random.uniform(jax.random.fold_in(jax.random.fold_in(key, 6), dim), (blocks,), jnp.float32, low / len(cuts), largest / len(cuts))
        gain = gain * jnp.repeat(jnp.exp(heights), extent[dim] // blocks).reshape((-1,) + (1,) * (len(extent) - 1 - dim))
    return gain


def centred(stream_key, shape, deviation, reach, split=(), dtype=jnp.bfloat16):
    drawn = jax.random.normal(stream_key, shape, jnp.float32) * deviation
    if len(split) > 0:
        drawn = block_levels(stream_key, shape, split, -0.22, 0.18) * drawn
    return jnp.clip(drawn, min=-reach, max=reach).astype(dtype)


def setup_inputs(seed: int = 0) -> dict:
    keys = jax.random.split(jax.random.key(seed), 20)
    return {
        "atmosphere": centred(keys[0], (LAT, LON, D), 1.0, 6.0, ((0, 64), (2, 4))),
        "spec_weight": centred(keys[1], (2, 2, 2, D, BS), BS ** -0.5, 0.625, ((3, 4),), jnp.float32),
        "spec_bias": centred(keys[2], (2, 2, 2, D), 0.3, 4.0, ((3, 4),), jnp.float32),
        "norm_gain": jnp.clip(1.0 + 0.15 * jax.random.normal(keys[3], (2, 2, D), jnp.float32), 0.25, 1.75),
        "norm_shift": centred(keys[4], (2, 2, D), 0.2, 3.0, (), jnp.float32),
        "fc_in": centred(keys[5], (2, D, FFH), D ** -0.5, 0.21875, ((2, 4),)),
        "fc_out": centred(keys[6], (2, FFH, D), FFH ** -0.5, 0.109375, ((1, 4),)),
        "flux_head": centred(keys[7], (D, FLUX), D ** -0.5, 0.21875, ((0, 4),)),
        "flux_embed": centred(keys[8], (FLUX, OC), FLUX ** -0.5, 2.0, (), jnp.float32),
        "ocean_state": centred(keys[9], (OLAT, OLON, OC), 1.0, 6.0, ((0, 64), (1, 4))),
        "sea_mask": touch_ends((jax.random.randint(keys[10], (OLAT, OLON), 0, 10) < 7).astype(jnp.int32), jax.random.fold_in(keys[10], 1), 0, 1),
        "depth_kernel": centred(keys[11], (7, 7, OC), 49 ** -0.5, 0.875, (), jnp.float32),
        "ocean_gain": jnp.clip(1.0 + 0.15 * jax.random.normal(keys[12], (OC,), jnp.float32), 0.25, 1.75),
        "ocean_shift": centred(keys[13], (OC,), 0.2, 3.0, (), jnp.float32),
        "ocean_in": centred(keys[14], (OC, OFF), OC ** -0.5, 0.375),
        "ocean_out": centred(keys[15], (OFF, OC), OFF ** -0.5, 0.1875),
        "layer_scale": jnp.clip(jnp.exp(jax.random.uniform(keys[16], (OC,), jnp.float32, math.log(0.3), math.log(1.0))), 0.3, 1.0),
        "field_head": centred(keys[17], (OC, FIELDS), OC ** -0.5, 0.375, (), jnp.float32),
        "patch_embed": centred(keys[18], (PATCH, D), PATCH ** -0.5, 1.5, ((1, 4),), jnp.float32),
    }


full_precision = lax.Precision.HIGHEST
eps_norm = 1e-06
shrink_level = 0.01

def layer_norm(values, scaling, offset):
    average = lax.optimization_barrier(jnp.mean(values, axis=-1, keepdims=True))
    squares = lax.optimization_barrier(jnp.mean(values * values, axis=-1, keepdims=True))
    variance = squares - average * average
    return (values - average) * lax.rsqrt(variance + eps_norm) * scaling + offset

def soft_shrink(values):
    zeros = jnp.zeros_like(values)
    return jnp.where(values > shrink_level, values - shrink_level, jnp.where(values < -shrink_level, values + shrink_level, zeros))

def group_product(values, matrix):
    return jnp.einsum('...gi,gio->...go', values, matrix, precision=full_precision)

def mix_modes(real_part, imag_part, weights, biases):
    full_shape = real_part.shape
    group_width = weights.shape[-1]
    groups = weights.shape[-2] // group_width
    real_part = real_part.reshape(full_shape[:-1] + (groups, group_width))
    imag_part = imag_part.reshape(full_shape[:-1] + (groups, group_width))
    for sublayer in range(2):
        w_real = weights[sublayer, 0].reshape(groups, group_width, group_width)
        w_imag = weights[sublayer, 1].reshape(groups, group_width, group_width)
        b_real = biases[sublayer, 0].reshape(groups, group_width)
        b_imag = biases[sublayer, 1].reshape(groups, group_width)
        new_real = group_product(real_part, w_real) - group_product(imag_part, w_imag) + b_real
        new_imag = group_product(imag_part, w_real) + group_product(real_part, w_imag) + b_imag
        if sublayer == 0:
            new_real = jnp.maximum(new_real, 0.0)
            new_imag = jnp.maximum(new_imag, 0.0)
        real_part, imag_part = (new_real, new_imag)
    return (soft_shrink(real_part).reshape(full_shape), soft_shrink(imag_part).reshape(full_shape))

def mlp_row(normed_row, w_in, w_out):
    hidden = jax.nn.gelu(jnp.dot(normed_row, w_in, preferred_element_type=jnp.float32), approximate=False).astype(jnp.bfloat16)
    return jnp.dot(hidden, w_out, preferred_element_type=jnp.float32)

def afno_block(stream, scaling, offset, weights, biases, w_in, w_out):
    values = stream.astype(jnp.float32)
    normed = layer_norm(values, scaling[0], offset[0])
    spectrum = jnp.fft.rfft(normed, axis=1, norm='ortho')[:, :KLON]
    spectrum = jnp.fft.fft(spectrum, axis=0, norm='ortho')
    real_part, imag_part = mix_modes(jnp.real(spectrum), jnp.imag(spectrum), weights, biases)
    spectrum = jnp.fft.ifft(lax.complex(real_part, imag_part), axis=0, norm='ortho')
    spectrum = jnp.pad(spectrum, ((0, 0), (0, LON // 2 + 1 - KLON), (0, 0)))
    restored = jnp.fft.irfft(spectrum, n=LON, axis=1, norm='ortho')
    after_filter = (values + restored + normed).astype(jnp.bfloat16)
    filtered = after_filter.astype(jnp.float32)
    second = layer_norm(filtered, scaling[1], offset[1]).astype(jnp.bfloat16)
    mixed = lax.map(lambda row_block: mlp_row(row_block, w_in, w_out), second)
    return (filtered + mixed).astype(jnp.bfloat16)

def reference(atmosphere, spec_weight, spec_bias, norm_gain, norm_shift, fc_in, fc_out, flux_head, flux_embed, ocean_state, sea_mask, depth_kernel, ocean_gain, ocean_shift, ocean_in, ocean_out, layer_scale, field_head, patch_embed):
    after_one = afno_block(atmosphere, norm_gain[0], norm_shift[0], spec_weight[0], spec_bias[0], fc_in[0], fc_out[0])
    fluxes = jnp.dot(after_one.reshape(-1, D), flux_head, preferred_element_type=jnp.float32).reshape(LAT, LON, FLUX)
    upsampled = jnp.repeat(jnp.repeat(fluxes, 2, axis=0), 2, axis=1)
    sea_cells = sea_mask.astype(jnp.float32)[..., None]
    forcing = jnp.einsum('ijf,fc->ijc', upsampled, flux_embed, precision=full_precision)
    start = (ocean_state.astype(jnp.float32) + sea_cells * forcing).astype(jnp.bfloat16)
    padded = jnp.pad(start.astype(jnp.float32), ((0, 0), (3, 3), (0, 0)), mode='wrap')
    padded = jnp.pad(padded, ((3, 3), (0, 0), (0, 0)))
    convolved = jnp.zeros((OLAT, OLON, OC), jnp.float32)
    for row_step in range(7):
        for col_step in range(7):
            convolved = convolved + padded[row_step:row_step + OLAT, col_step:col_step + OLON] * depth_kernel[row_step, col_step]
    normed = layer_norm(convolved, ocean_gain, ocean_shift).astype(jnp.bfloat16)
    update = lax.map(lambda row_block: mlp_row(row_block, ocean_in, ocean_out), normed)
    ocean_next = (start.astype(jnp.float32) + sea_cells * layer_scale * update).astype(jnp.bfloat16)
    surface = sea_cells * jnp.einsum('ijc,cf->ijf', ocean_next.astype(jnp.float32), field_head, precision=full_precision)
    patches = surface.reshape(LAT, 2, LON, 2, FIELDS).transpose(0, 2, 4, 1, 3).reshape(LAT, LON, PATCH)
    embedding = jnp.einsum('pqk,kd->pqd', patches, patch_embed, precision=full_precision)
    middle = (after_one.astype(jnp.float32) + embedding).astype(jnp.bfloat16)
    atmosphere_next = afno_block(middle, norm_gain[1], norm_shift[1], spec_weight[1], spec_bias[1], fc_in[1], fc_out[1])
    return (atmosphere_next, ocean_next, surface)
```

```python
import math

import jax
import jax.numpy as jnp
import numpy as np
from jax import lax
from jax.sharding import PartitionSpec as P

full_precision = lax.Precision.HIGHEST
eps_norm = 1e-06
shrink_level = 0.01


def with_halo(cells, sides, width, closed):
    for axis, dim in sides:
        count = lax.axis_size(axis)
        ends = count if closed else count - 1
        head = lax.slice_in_dim(cells, 0, width, axis=dim)
        tail = lax.slice_in_dim(cells, cells.shape[dim] - width, cells.shape[dim], axis=dim)
        cells = jnp.concatenate(
            [
                lax.ppermute(tail, axis, [(i, (i + 1) % count) for i in range(ends)]),
                cells,
                lax.ppermute(head, axis, [((i + 1) % count, i) for i in range(ends)]),
            ],
            axis=dim,
        )
    return cells


def layer_norm(values, scaling, offset):
    average = jnp.mean(values, axis=-1, keepdims=True)
    squares = jnp.mean(values * values, axis=-1, keepdims=True)
    variance = squares - average * average
    return (values - average) * lax.rsqrt(variance + eps_norm) * scaling + offset


def soft_shrink(values):
    zeros = jnp.zeros_like(values)
    return jnp.where(
        values > shrink_level,
        values - shrink_level,
        jnp.where(values < -shrink_level, values + shrink_level, zeros),
    )


def dft_angles(first, second, length):
    turns = np.outer(np.arange(first), np.arange(second)) % length
    return turns * (2.0 * math.pi / length)


def dot32(subscripts, left, right):
    return jnp.einsum(
        subscripts,
        left.astype(jnp.bfloat16),
        right.astype(jnp.bfloat16),
        preferred_element_type=jnp.float32,
    )


def complex_weights(weights, biases):
    width = weights.shape[-1]
    groups = weights.shape[-2] // width
    w = weights.reshape(2, 2, groups, width, width)
    top = jnp.stack([w[:, 0], w[:, 1]], axis=3)
    bottom = jnp.stack([-w[:, 1], w[:, 0]], axis=3)
    return jnp.stack([top, bottom], axis=2), biases.reshape(2, 2, groups, width)


def channel_mlp(tokens, layer_index, norm_gain, norm_shift, w_in, w_out):
    flat_tokens = tokens.reshape(-1, tokens.shape[-1]).astype(jnp.float32)
    second = layer_norm(flat_tokens, norm_gain[layer_index, 1], norm_shift[layer_index, 1]).astype(
        jnp.bfloat16
    )
    hidden = jax.nn.gelu(
        jnp.dot(second, w_in, preferred_element_type=jnp.float32), approximate=False
    ).astype(jnp.bfloat16)
    summed = jnp.dot(hidden, w_out, preferred_element_type=jnp.float32)
    return (flat_tokens + summed).astype(jnp.bfloat16).reshape(tokens.shape)


def spectral_filter(values, average, inverse, gain, shift, weights, biases):
    normed = (values - average) * inverse * gain + shift
    rows, longitudes, slot = values.shape
    kept = longitudes // 2
    bands = lax.axis_size("band")
    latitudes = rows * bands
    each = kept // bands
    lon = dft_angles(kept, longitudes, longitudes)
    forward = np.stack([np.cos(lon), -np.sin(lon)], axis=1) / math.sqrt(longitudes)
    lat = dft_angles(latitudes, latitudes, latitudes) / 1.0
    cos_lat = np.cos(lat) / math.sqrt(latitudes)
    sin_lat = np.sin(lat) / math.sqrt(latitudes)
    lat_forward = np.stack([np.stack([cos_lat, sin_lat], 1), np.stack([-sin_lat, cos_lat], 1)], 0)
    lat_back = np.stack([np.stack([cos_lat, -sin_lat], 1), np.stack([sin_lat, cos_lat], 1)], 0)
    forward, lat_forward, lat_back = (
        jnp.asarray(m, jnp.bfloat16) for m in (forward, lat_forward, lat_back)
    )
    spectrum = dot32("krn,lnc->krlc", forward, normed).astype(jnp.bfloat16)
    chunk = each * 2 * rows * slot
    sent = spectrum.reshape(bands, chunk // 128, 128)
    got = lax.all_to_all(sent, "band", split_axis=0, concat_axis=0, tiled=True)
    got = got.reshape(bands, each, 2, rows, slot)
    got = got.transpose(1, 2, 0, 3, 4).reshape(each, 2, latitudes, slot)
    spec = dot32("sqrl,krlc->kqsc", lat_forward, got)
    groups = weights.shape[1]
    width = slot // groups
    mixed = spec.reshape(each, latitudes, 2, groups, width)
    for sublayer in range(2):
        mixed = dot32("kqrgi,grisj->kqsgj", mixed, weights[sublayer]) + biases[sublayer]
        if sublayer == 0:
            mixed = jnp.maximum(mixed, 0.0)
    mixed = soft_shrink(mixed).reshape(each, latitudes, 2, slot)
    back = dot32("sqrl,klrc->kqsc", lat_back, mixed).astype(jnp.bfloat16)
    back = back.reshape(each, bands, rows, 2, slot).transpose(1, 0, 3, 2, 4)
    sent = back.reshape(bands, chunk // 128, 128)
    got = lax.all_to_all(sent, "band", split_axis=0, concat_axis=0, tiled=True)
    got = got.reshape(kept, 2, rows, slot)
    inverse_lon = np.stack([np.cos(lon), -np.sin(lon)], axis=1) * np.where(
        np.arange(kept) == 0, 1.0, 2.0
    )[:, None, None] / math.sqrt(longitudes)
    restored = dot32("krn,krlc->lnc", jnp.asarray(inverse_lon, jnp.bfloat16), got)
    return (values + restored + normed).astype(jnp.bfloat16)


def on_device(
    atmosphere,
    spec_weight,
    spec_bias,
    norm_gain,
    norm_shift,
    fc_in,
    fc_out,
    flux_head,
    flux_embed,
    ocean_state,
    sea_mask,
    depth_kernel,
    ocean_gain,
    ocean_shift,
    ocean_in,
    ocean_out,
    layer_scale,
    field_head,
    patch_embed,
):
    column_index = lax.axis_index(("comp", "tile"))
    team = ("comp", "tile")
    slot = atmosphere.shape[-1]
    w_in = [lax.all_gather(fc_in[b], team, axis=1, tiled=True) for b in range(2)]
    w_out = [lax.all_gather(fc_out[b], team, axis=0, tiled=True) for b in range(2)]
    head = lax.all_gather(flux_head, team, axis=0, tiled=True)
    embed = lax.all_gather(patch_embed, team, axis=1, tiled=True)

    def filtered(values, average, inverse, block):
        gain = lax.dynamic_slice_in_dim(norm_gain[block, 0], column_index * slot, slot)
        shift = lax.dynamic_slice_in_dim(norm_shift[block, 0], column_index * slot, slot)
        weights, biases = complex_weights(spec_weight[block], spec_bias[block])
        return spectral_filter(
            values, average[..., None], inverse[..., None], gain, shift, weights, biases
        )

    values = atmosphere.astype(jnp.float32)
    width_full = slot * lax.axis_size(team)
    totals, squares = lax.psum(
        (jnp.sum(values, axis=-1), jnp.sum(values * values, axis=-1)), team
    )
    average = totals / width_full
    inverse = lax.rsqrt(squares / width_full - average * average + eps_norm)
    after_filter = filtered(values, average, inverse, 0)
    tokens = lax.all_to_all(after_filter, team, split_axis=1, concat_axis=2, tiled=True)
    after_one = channel_mlp(tokens, 0, norm_gain, norm_shift, w_in[0], w_out[0])
    fluxes = jnp.einsum("lnc,cf->lnf", after_one, head, preferred_element_type=jnp.float32)
    upsampled = jnp.repeat(jnp.repeat(fluxes, 2, axis=0), 2, axis=1)
    sea_cells = sea_mask.astype(jnp.float32)[..., None]
    forcing = jnp.einsum("ijf,fc->ijc", upsampled, flux_embed, precision=full_precision)
    start = (ocean_state.astype(jnp.float32) + sea_cells * forcing).astype(jnp.bfloat16)
    widened = with_halo(start, ((("comp", "tile"), 1),), 3, True)
    extended = with_halo(widened, (("band", 0),), 3, False).astype(jnp.float32)
    tile_rows = start.shape[0]
    tile_columns = start.shape[1]
    convolved = jnp.zeros(start.shape, jnp.float32)
    for row_step in range(7):
        for col_step in range(7):
            convolved = (
                convolved
                + extended[row_step : row_step + tile_rows, col_step : col_step + tile_columns]
                * depth_kernel[row_step, col_step]
            )
    normed = layer_norm(convolved, ocean_gain, ocean_shift).astype(jnp.bfloat16)
    flat_cells = normed.reshape(-1, normed.shape[-1])
    hidden = jax.nn.gelu(
        jnp.dot(flat_cells, ocean_in, preferred_element_type=jnp.float32), approximate=False
    ).astype(jnp.bfloat16)
    update = jnp.dot(hidden, ocean_out, preferred_element_type=jnp.float32).reshape(start.shape)
    ocean_next = (start.astype(jnp.float32) + sea_cells * layer_scale * update).astype(jnp.bfloat16)
    surface = sea_cells * jnp.einsum(
        "ijc,cf->ijf", ocean_next.astype(jnp.float32), field_head, precision=full_precision
    )
    half_rows = tile_rows // 2
    half_columns = tile_columns // 2
    patches = (
        surface.reshape(half_rows, 2, half_columns, 2, surface.shape[2])
        .transpose(0, 2, 4, 1, 3)
        .reshape(half_rows, half_columns, -1)
    )
    embedding = jnp.einsum("pqk,kd->pqd", patches, embed, precision=full_precision)
    middle = (after_one.astype(jnp.float32) + embedding).astype(jnp.bfloat16)
    values = middle.astype(jnp.float32)
    average = jnp.mean(values, axis=-1)
    inverse = lax.rsqrt(jnp.mean(values * values, axis=-1) - average * average + eps_norm)
    stats = lax.all_gather(jnp.stack([average, inverse]), team, axis=2, tiled=True)
    values = lax.all_to_all(middle, team, split_axis=2, concat_axis=1, tiled=True)
    after_filter = filtered(values.astype(jnp.float32), stats[0], stats[1], 1)
    tokens = lax.all_to_all(after_filter, team, split_axis=1, concat_axis=2, tiled=True)
    result = channel_mlp(tokens, 1, norm_gain, norm_shift, w_in[1], w_out[1])
    atmosphere_next = lax.all_to_all(result, team, split_axis=2, concat_axis=1, tiled=True)
    return (atmosphere_next, ocean_next, surface)


def solution(mesh):
    placed = (
        P("band", None, ("comp", "tile")),
        P(None, None, None, ("comp", "tile"), None),
        P(None, None, None, ("comp", "tile")),
        P(),
        P(),
        P(None, None, ("comp", "tile")),
        P(None, ("comp", "tile"), None),
        P(("comp", "tile"), None),
        P(),
        P("band", ("comp", "tile"), None),
        P("band", ("comp", "tile")),
        P(),
        P(),
        P(),
        P(),
        P(),
        P(),
        P(),
        P(None, ("comp", "tile")),
    )
    return jax.shard_map(
        on_device,
        mesh=mesh,
        in_specs=placed,
        out_specs=(
            P("band", None, ("comp", "tile")),
            P("band", ("comp", "tile"), None),
            P("band", ("comp", "tile"), None),
        ),
        check_vma=False,
    )
```

```python
import functools
import math

import jax
import jax.numpy as jnp
import numpy as np
from jax import lax
from jax.experimental import pallas as pl
from jax.experimental.pallas import tpu as pltpu
from jax.sharding import PartitionSpec as P

MESH = pl.DeviceIdType.MESH
full_precision = lax.Precision.HIGHEST
eps_norm = 1e-06
shrink_level = 0.01


def with_halo(cells, sides, width, closed):
    for axis, dim in sides:
        count = lax.axis_size(axis)
        ends = count if closed else count - 1
        head = lax.slice_in_dim(cells, 0, width, axis=dim)
        tail = lax.slice_in_dim(cells, cells.shape[dim] - width, cells.shape[dim], axis=dim)
        cells = jnp.concatenate(
            [
                lax.ppermute(tail, axis, [(i, (i + 1) % count) for i in range(ends)]),
                cells,
                lax.ppermute(head, axis, [((i + 1) % count, i) for i in range(ends)]),
            ],
            axis=dim,
        )
    return cells


def layer_norm(values, scaling, offset):
    average = jnp.mean(values, axis=-1, keepdims=True)
    squares = jnp.mean(values * values, axis=-1, keepdims=True)
    variance = squares - average * average
    return (values - average) * lax.rsqrt(variance + eps_norm) * scaling + offset


def soft_shrink(values):
    zeros = jnp.zeros_like(values)
    return jnp.where(
        values > shrink_level,
        values - shrink_level,
        jnp.where(values < -shrink_level, values + shrink_level, zeros),
    )


def channel_mlp(tokens, layer_index, norm_gain, norm_shift, w_in, w_out):
    flat_tokens = tokens.reshape(-1, tokens.shape[-1]).astype(jnp.float32)
    second = layer_norm(flat_tokens, norm_gain[layer_index, 1], norm_shift[layer_index, 1]).astype(
        jnp.bfloat16
    )
    hidden = jax.nn.gelu(
        jnp.dot(second, w_in, preferred_element_type=jnp.float32), approximate=False
    ).astype(jnp.bfloat16)
    summed = jnp.dot(hidden, w_out, preferred_element_type=jnp.float32)
    return (flat_tokens + summed).astype(jnp.bfloat16).reshape(tokens.shape)


def split_bf16(array):
    high = array.astype(jnp.bfloat16)
    return high, (array - high.astype(jnp.float32)).astype(jnp.bfloat16)


def host_split(array):
    whole = np.asarray(array, np.float32)
    high = whole.astype(jnp.bfloat16)
    low = (whole - high.astype(np.float32)).astype(jnp.bfloat16)
    return jnp.asarray(np.stack([high, low]))


def transforms(latitudes, longitudes, bands):
    kept = longitudes // 2
    each, rows = kept // bands, latitudes // bands
    waves = np.arange(kept).reshape(bands, each).T.reshape(-1)
    lats = np.arange(latitudes).reshape(bands, rows).T.reshape(-1)
    lon = np.outer(waves, np.arange(longitudes)) % longitudes * (2.0 * math.pi / longitudes)
    lat = np.outer(np.arange(latitudes), lats) % latitudes * (2.0 * math.pi / latitudes)
    forward = np.concatenate([np.cos(lon), -np.sin(lon)], 0) / math.sqrt(longitudes)
    across = np.stack([np.cos(lat), np.sin(lat)], 0) / math.sqrt(latitudes)
    weight = np.where(waves == 0, 1.0, 2.0)[:, None]
    inverse = np.concatenate([np.cos(lon) * weight, -np.sin(lon) * weight], 0).T
    return (
        host_split(forward),
        host_split(across.reshape(2 * latitudes, latitudes)),
        host_split(across.transpose(0, 2, 1).reshape(2 * latitudes, latitudes)),
        host_split(inverse / math.sqrt(longitudes)),
    )


def mix_matrices(weights, biases):
    slot, width = weights.shape[-2:]
    groups = slot // width
    eye = jnp.eye(groups, dtype=weights.dtype)
    full = weights.reshape(2, 2, groups, width, 1, width) * eye[None, None, :, None, :, None]
    full = full.reshape(2, 2, slot, slot)
    whole = jnp.concatenate(
        [
            jnp.concatenate([full[:, 0], full[:, 1]], axis=2),
            jnp.concatenate([-full[:, 1], full[:, 0]], axis=2),
        ],
        axis=1,
    )
    def lanes(array, axis):
        part = [lax.slice_in_dim(array, a, b, axis=axis) for a, b in
                ((0, 128), (slot, slot + 128), (128, slot), (slot + 128, 2 * slot))]
        return jnp.concatenate(part, axis=axis)
    whole = lanes(lanes(whole, 1), 2)
    high, low = split_bf16(whole)
    offsets = lanes(biases.reshape(2, 2 * slot), 1)
    return jnp.stack([high, low], axis=1), jnp.concatenate([offsets, jnp.zeros((6, 2 * slot))], 0)


def product(left, right):
    total = None
    for a, b in ((0, 0), (1, 0), (0, 1)):
        if a < len(left) and b < len(right):
            term = jnp.dot(left[a], right[b], preferred_element_type=jnp.float32)
            total = term if total is None else total + term
    return total


def filter_kernel(
    bands, exchanged, x_ref, affine_ref, forward_ref, across_ref, back_ref, inverse_ref, mix_ref,
    offset_ref, out_ref, *scratch
):
    if exchanged:
        held, scratch = scratch[0], scratch[1:]
    (
        normed, after, stage, landed, sums, all_sums, send_a, got_a, send_b, got_b,
        sent_team, came_team, sent_sum, came_sum, sent_a, came_a, sent_b, came_b, sent_out, came_out,
    ) = scratch
    rows, quarter, slot = out_ref.shape[1:]
    longitudes = 4 * quarter
    latitudes = rows * bands
    each = longitudes // 2 // bands
    me = lax.axis_index("band")
    mine = lax.axis_index("comp") * 2 + lax.axis_index("tile")

    def member(step):
        return lax.rem(mine + step, 4)

    def team_id(index):
        return {"comp": lax.div(index, 2), "tile": lax.rem(index, 2)}

    barrier = pltpu.get_barrier_semaphore()

    def greet(step, carry):
        pl.semaphore_signal(
            barrier, inc=1, device_id={"band": lax.rem(me + step, bands)}, device_id_type=MESH
        )
        return carry

    for step in range(1, 4):
        pl.semaphore_signal(barrier, inc=1, device_id=team_id(member(step)), device_id_type=MESH)
    lax.fori_loop(1, bands, greet, 0)

    def team_copy(source, target, sent, came, step, whole=False):
        index = member(step)
        return pltpu.make_async_remote_copy(
            src_ref=source if whole else source.at[index],
            dst_ref=target.at[mine],
            send_sem=sent.at[index],
            recv_sem=came.at[mine],
            device_id=team_id(index),
            device_id_type=MESH,
        )

    def team_landing(source, target, sent, came, step, whole=False):
        index = member(step)
        return pltpu.make_async_remote_copy(
            src_ref=source if whole else source.at[index],
            dst_ref=target.at[index],
            send_sem=sent.at[index],
            recv_sem=came.at[index],
            device_id=team_id(index),
            device_id_type=MESH,
        )

    def team_exchange(*args):
        for step in range(1, 4):
            team_copy(*args[:4], step, *args[4:]).start()

    def team_finish(*args):
        for step in range(1, 4):
            team_landing(*args[:4], step, *args[4:]).wait()

    if exchanged:
        pl.semaphore_wait(barrier, bands - 1 + 3)
        team_exchange(x_ref, held, sent_team, came_team)
        held[mine] = x_ref[mine]
        team_finish(x_ref, held, sent_team, came_team)

    def tokens(lat):
        if exchanged:
            return jnp.concatenate([held[s, lat] for s in range(4)], axis=0)
        return x_ref[lat]

    ones = jnp.ones((8, slot), jnp.bfloat16)
    which = lax.broadcasted_iota(jnp.int32, (8, longitudes), 0)
    turned = (((1,), (1,)), ((), ()))

    def row_sum(values):
        return lax.dot_general(ones, values, turned, preferred_element_type=jnp.float32)

    total = jnp.zeros((8, longitudes), jnp.float32)
    for lat in range(rows):
        values = tokens(lat)
        wide = values.astype(jnp.float32)
        high, low = split_bf16(wide * wide)
        total = total + jnp.where(which == lat, row_sum(values), 0.0)
        total = total + jnp.where(which == rows + lat, row_sum(high) + row_sum(low), 0.0)
    sums[...] = total
    if not exchanged:
        pl.semaphore_wait(barrier, bands - 1 + 3)
    team_exchange(sums, all_sums, sent_sum, came_sum, True)
    all_sums[mine] = total
    team_finish(sums, all_sums, sent_sum, came_sum, True)
    total = (all_sums[0] + all_sums[1] + all_sums[2] + all_sums[3]) * (1.0 / (4 * slot))
    columns = jnp.concatenate([total, jnp.zeros((120, longitudes), jnp.float32)], axis=0).T

    lane = lax.broadcasted_iota(jnp.int32, (1, 128), 1)
    first_half = lane < slot - 128
    sign = jnp.where(first_half, 1.0, -1.0)
    half = longitudes // 2

    def spread(lat, wave, part, values):
        stage[pl.ds(part * 9 + lat * 3 + wave, bands, stride=32), :] = values

    def collect(lat, wave, part):
        return landed[pl.ds(part * 9 + lat * 3 + wave, bands, stride=32), :]

    for lat in range(rows):
        values = tokens(lat).astype(jnp.float32)
        average = columns[:, lat : lat + 1]
        second = columns[:, rows + lat : rows + lat + 1]
        scaled = (values - average) * lax.rsqrt(second - average * average + eps_norm)
        scaled = scaled * affine_ref[0:1, :] + affine_ref[1:2, :]
        normed[lat] = scaled
        tail = scaled[:, 128:]
        wide = jnp.concatenate([scaled[:, :128], tail, tail], axis=1)
        spectrum = product((forward_ref[0], forward_ref[1]), split_bf16(wide))
        upper, lower = spectrum[:half], spectrum[half:]
        parts = (upper[:, :128], lower[:, :128], jnp.where(first_half, upper[:, 128:], lower[:, 128:]))
        for part in range(3):
            for wave in range(each):
                spread(lat, wave, part, parts[part][wave * bands : (wave + 1) * bands])

    def band_copy(source, target, sent, came, step, landing):
        index = lax.rem(me + step, bands)
        return pltpu.make_async_remote_copy(
            src_ref=source.at[index],
            dst_ref=target.at[index if landing else me],
            send_sem=sent.at[index],
            recv_sem=came.at[index if landing else me],
            device_id={"band": index},
            device_id_type=MESH,
        )

    def band_exchange(source, target, sent, came):
        source[...] = stage[...].astype(jnp.bfloat16).reshape(source.shape)

        def go(step, carry):
            band_copy(source, target, sent, came, step, False).start()
            return carry

        lax.fori_loop(1, bands, go, 0)
        target[me] = source[me]

        def come(step, carry):
            band_copy(source, target, sent, came, step, True).wait()
            return carry

        lax.fori_loop(1, bands, come, 0)
        landed[...] = target[...].astype(jnp.float32).reshape(landed.shape)

    band_exchange(send_a, got_a, sent_a, came_a)
    pieces = []
    for wave in range(each):
        for part in range(3):
            pieces.append(
                jnp.concatenate([collect(lat, wave, part) for lat in range(rows)], axis=0)
            )
    spectrum = jnp.concatenate(pieces, axis=1).astype(jnp.bfloat16)
    turned_all = product((across_ref[0], across_ref[1]), (spectrum,))

    def combine(both, wave, direction):
        base = wave * 384
        cosine, sine = both[:latitudes, base : base + 384], both[latitudes:, base : base + 384]
        real = cosine[:, :128] + direction * sine[:, 128:256]
        imag = cosine[:, 128:256] - direction * sine[:, :128]
        rest = cosine[:, 256:] + (direction * sign) * pltpu.roll(sine[:, 256:], 64, 1)
        return real, imag, rest

    rows_in = jnp.concatenate(
        [jnp.concatenate(combine(turned_all, wave, 1.0), axis=1) for wave in range(each)], axis=0
    )
    hidden = product(split_bf16(rows_in), (mix_ref[0, 0], mix_ref[0, 1])) + offset_ref[0:1, :]
    hidden = jnp.maximum(hidden, 0.0)
    mixed = product(split_bf16(hidden), (mix_ref[1, 0], mix_ref[1, 1])) + offset_ref[1:2, :]
    mixed = soft_shrink(mixed)
    columns_back = jnp.concatenate(
        [mixed[wave * latitudes : (wave + 1) * latitudes] for wave in range(each)], axis=1
    )
    turned_back = product((back_ref[0], back_ref[1]), split_bf16(columns_back))
    for wave in range(each):
        parts = combine(turned_back, wave, -1.0)
        for part in range(3):
            for lat in range(rows):
                spread(lat, wave, part, parts[part][lat * bands : (lat + 1) * bands])
    band_exchange(send_b, got_b, sent_b, came_b)
    for lat in range(rows):
        real, imag, rest = (
            jnp.concatenate([collect(lat, wave, part) for wave in range(each)], axis=0)
            for part in range(3)
        )
        right = jnp.concatenate(
            [
                jnp.concatenate([real, rest], axis=1),
                jnp.concatenate([imag, pltpu.roll(rest, 64, 1)], axis=1),
            ],
            axis=0,
        ).astype(jnp.bfloat16)
        restored = product((inverse_ref[0], inverse_ref[1]), (right,))
        result = tokens(lat).astype(jnp.float32) + restored[:, :slot] + normed[lat]
        result = result.astype(jnp.bfloat16)
        for s in range(4):
            after[s, lat] = result[s * quarter : (s + 1) * quarter]
    team_exchange(after, out_ref, sent_out, came_out)
    out_ref[mine] = after[mine]
    team_finish(after, out_ref, sent_out, came_out)


def spectral_filter(values, gain, shift, weights, biases, bands, exchanged):
    if exchanged:
        quarter, slot = values.shape[2:]
        rows, longitudes = values.shape[1], 4 * quarter
    else:
        rows, longitudes, slot = values.shape
        quarter = longitudes // 4
    latitudes = rows * bands
    mats = transforms(latitudes, longitudes, bands)
    mix, offsets = mix_matrices(weights, biases)
    affine = jnp.concatenate([gain[None], shift[None], jnp.zeros((6, slot))], 0)
    team = pltpu.VMEM((4, rows, quarter, slot), jnp.bfloat16)
    chunks = pltpu.VMEM((bands, 32, 128), jnp.bfloat16)
    four = pltpu.SemaphoreType.DMA((4,))
    many = pltpu.SemaphoreType.DMA((bands,))
    scratch = [team] if exchanged else []
    scratch += [
        pltpu.VMEM((rows, longitudes, slot), jnp.float32),
        team,
        pltpu.VMEM((bands * 32, 128), jnp.float32),
        pltpu.VMEM((bands * 32, 128), jnp.float32),
        pltpu.VMEM((8, longitudes), jnp.float32),
        pltpu.VMEM((4, 8, longitudes), jnp.float32),
        chunks, chunks, chunks, chunks,
        four, four, four, four, many, many, many, many, four, four,
    ]
    return pl.pallas_call(
        functools.partial(filter_kernel, bands, exchanged),
        out_shape=jax.ShapeDtypeStruct((4, rows, quarter, slot), jnp.bfloat16),
        in_specs=[pl.BlockSpec(memory_space=pltpu.VMEM)] * 8,
        out_specs=pl.BlockSpec(memory_space=pltpu.VMEM),
        scratch_shapes=scratch,
        compiler_params=pltpu.CompilerParams(
            collective_id=1 if exchanged else 0, has_side_effects=True, vmem_limit_bytes=60 << 20
        ),
    )(values, affine, *mats, mix, offsets)


def on_device(
    atmosphere,
    spec_weight,
    spec_bias,
    norm_gain,
    norm_shift,
    fc_in,
    fc_out,
    flux_head,
    flux_embed,
    ocean_state,
    sea_mask,
    depth_kernel,
    ocean_gain,
    ocean_shift,
    ocean_in,
    ocean_out,
    layer_scale,
    field_head,
    patch_embed,
):
    column_index = lax.axis_index(("comp", "tile"))
    team = ("comp", "tile")
    slot = atmosphere.shape[-1]
    w_in = [lax.all_gather(fc_in[b], team, axis=1, tiled=True) for b in range(2)]
    w_out = [lax.all_gather(fc_out[b], team, axis=0, tiled=True) for b in range(2)]
    head = lax.all_gather(flux_head, team, axis=0, tiled=True)
    embed = lax.all_gather(patch_embed, team, axis=1, tiled=True)

    bands = lax.axis_size("band")

    def filtered(values, block):
        gain = lax.dynamic_slice_in_dim(norm_gain[block, 0], column_index * slot, slot)
        shift = lax.dynamic_slice_in_dim(norm_shift[block, 0], column_index * slot, slot)
        pieces = spectral_filter(
            values, gain, shift, spec_weight[block], spec_bias[block], bands, block == 1
        )
        return pieces.transpose(1, 2, 0, 3).reshape(pieces.shape[1], pieces.shape[2], -1)

    tokens = filtered(atmosphere, 0)
    after_one = channel_mlp(tokens, 0, norm_gain, norm_shift, w_in[0], w_out[0])
    fluxes = jnp.einsum("lnc,cf->lnf", after_one, head, preferred_element_type=jnp.float32)
    upsampled = jnp.repeat(jnp.repeat(fluxes, 2, axis=0), 2, axis=1)
    sea_cells = sea_mask.astype(jnp.float32)[..., None]
    forcing = jnp.einsum("ijf,fc->ijc", upsampled, flux_embed, precision=full_precision)
    start = (ocean_state.astype(jnp.float32) + sea_cells * forcing).astype(jnp.bfloat16)
    widened = with_halo(start, ((("comp", "tile"), 1),), 3, True)
    extended = with_halo(widened, (("band", 0),), 3, False).astype(jnp.float32)
    tile_rows = start.shape[0]
    tile_columns = start.shape[1]
    convolved = jnp.zeros(start.shape, jnp.float32)
    for row_step in range(7):
        for col_step in range(7):
            convolved = (
                convolved
                + extended[row_step : row_step + tile_rows, col_step : col_step + tile_columns]
                * depth_kernel[row_step, col_step]
            )
    normed = layer_norm(convolved, ocean_gain, ocean_shift).astype(jnp.bfloat16)
    flat_cells = normed.reshape(-1, normed.shape[-1])
    hidden = jax.nn.gelu(
        jnp.dot(flat_cells, ocean_in, preferred_element_type=jnp.float32), approximate=False
    ).astype(jnp.bfloat16)
    update = jnp.dot(hidden, ocean_out, preferred_element_type=jnp.float32).reshape(start.shape)
    ocean_next = (start.astype(jnp.float32) + sea_cells * layer_scale * update).astype(jnp.bfloat16)
    surface = sea_cells * jnp.einsum(
        "ijc,cf->ijf", ocean_next.astype(jnp.float32), field_head, precision=full_precision
    )
    half_rows = tile_rows // 2
    half_columns = tile_columns // 2
    patches = (
        surface.reshape(half_rows, 2, half_columns, 2, surface.shape[2])
        .transpose(0, 2, 4, 1, 3)
        .reshape(half_rows, half_columns, -1)
    )
    embedding = jnp.einsum("pqk,kd->pqd", patches, embed, precision=full_precision)
    middle = (after_one.astype(jnp.float32) + embedding).astype(jnp.bfloat16)
    pieces = middle.reshape(middle.shape[0], middle.shape[1], 4, slot).transpose(2, 0, 1, 3)
    tokens = filtered(pieces, 1)
    result = channel_mlp(tokens, 1, norm_gain, norm_shift, w_in[1], w_out[1])
    atmosphere_next = lax.all_to_all(result, team, split_axis=2, concat_axis=1, tiled=True)
    return (atmosphere_next, ocean_next, surface)


def solution(mesh):
    placed = (
        P("band", None, ("comp", "tile")),
        P(None, None, None, ("comp", "tile"), None),
        P(None, None, None, ("comp", "tile")),
        P(),
        P(),
        P(None, None, ("comp", "tile")),
        P(None, ("comp", "tile"), None),
        P(("comp", "tile"), None),
        P(),
        P("band", ("comp", "tile"), None),
        P("band", ("comp", "tile")),
        P(),
        P(),
        P(),
        P(),
        P(),
        P(),
        P(),
        P(None, ("comp", "tile")),
    )
    return jax.shard_map(
        on_device,
        mesh=mesh,
        in_specs=placed,
        out_specs=(
            P("band", None, ("comp", "tile")),
            P("band", ("comp", "tile"), None),
            P("band", ("comp", "tile"), None),
        ),
        check_vma=False,
    )
```

```python
import functools
import math

import jax
import jax.numpy as jnp
import numpy as np
from jax import lax
from jax.experimental import pallas as pl
from jax.experimental.pallas import tpu as pltpu
from jax.sharding import PartitionSpec as P

MESH = pl.DeviceIdType.MESH
full_precision = lax.Precision.HIGHEST
eps_norm = 1e-06
shrink_level = 0.01


def with_halo(cells, sides, width, closed):
    for axis, dim in sides:
        count = lax.axis_size(axis)
        ends = count if closed else count - 1
        head = lax.slice_in_dim(cells, 0, width, axis=dim)
        tail = lax.slice_in_dim(cells, cells.shape[dim] - width, cells.shape[dim], axis=dim)
        cells = jnp.concatenate(
            [
                lax.ppermute(tail, axis, [(i, (i + 1) % count) for i in range(ends)]),
                cells,
                lax.ppermute(head, axis, [((i + 1) % count, i) for i in range(ends)]),
            ],
            axis=dim,
        )
    return cells


def layer_norm(values, scaling, offset):
    average = jnp.mean(values, axis=-1, keepdims=True)
    squares = jnp.mean(values * values, axis=-1, keepdims=True)
    variance = squares - average * average
    return (values - average) * lax.rsqrt(variance + eps_norm) * scaling + offset


def soft_shrink(values):
    zeros = jnp.zeros_like(values)
    return jnp.where(
        values > shrink_level,
        values - shrink_level,
        jnp.where(values < -shrink_level, values + shrink_level, zeros),
    )


def split_bf16(array):
    high = array.astype(jnp.bfloat16)
    return high, (array - high.astype(jnp.float32)).astype(jnp.bfloat16)


def host_split(array):
    whole = np.asarray(array, np.float32)
    high = whole.astype(jnp.bfloat16)
    low = (whole - high.astype(np.float32)).astype(jnp.bfloat16)
    return jnp.asarray(np.stack([high, low]))


def transforms(latitudes, longitudes, bands):
    kept = longitudes // 2
    each, rows = kept // bands, latitudes // bands
    waves = np.arange(kept).reshape(bands, each).T.reshape(-1)
    lats = np.arange(latitudes).reshape(bands, rows).T.reshape(-1)
    lon = np.outer(waves, np.arange(longitudes)) % longitudes * (2.0 * math.pi / longitudes)
    lat = np.outer(np.arange(latitudes), lats) % latitudes * (2.0 * math.pi / latitudes)
    forward = np.concatenate([np.cos(lon), -np.sin(lon)], 0) / math.sqrt(longitudes)
    across = np.stack([np.cos(lat), np.sin(lat)], 0) / math.sqrt(latitudes)
    weight = np.where(waves == 0, 1.0, 2.0)[:, None]
    inverse = np.concatenate([np.cos(lon) * weight, -np.sin(lon) * weight], 0).T
    return (
        host_split(forward),
        host_split(across.reshape(2 * latitudes, latitudes)),
        host_split(across.transpose(0, 2, 1).reshape(2 * latitudes, latitudes)),
        host_split(inverse / math.sqrt(longitudes)),
    )


def mix_matrices(weights, biases):
    slot, width = weights.shape[-2:]
    groups = slot // width
    eye = jnp.eye(groups, dtype=weights.dtype)
    full = weights.reshape(2, 2, groups, width, 1, width) * eye[None, None, :, None, :, None]
    full = full.reshape(2, 2, slot, slot)
    whole = jnp.concatenate(
        [
            jnp.concatenate([full[:, 0], full[:, 1]], axis=2),
            jnp.concatenate([-full[:, 1], full[:, 0]], axis=2),
        ],
        axis=1,
    )
    def lanes(array, axis):
        part = [lax.slice_in_dim(array, a, b, axis=axis) for a, b in
                ((0, 128), (slot, slot + 128), (128, slot), (slot + 128, 2 * slot))]
        return jnp.concatenate(part, axis=axis)
    whole = lanes(lanes(whole, 1), 2)
    high, low = split_bf16(whole)
    offsets = lanes(biases.reshape(2, 2 * slot), 1)
    return jnp.stack([high, low], axis=1), jnp.concatenate([offsets, jnp.zeros((6, 2 * slot))], 0)


def product(left, right):
    total = None
    for a, b in ((0, 0), (1, 0), (0, 1)):
        if a < len(left) and b < len(right):
            term = jnp.dot(left[a], right[b], preferred_element_type=jnp.float32)
            total = term if total is None else total + term
    return total


def block_kernel(
    bands, block, x_ref, affine_ref, forward_ref, across_ref, back_ref, inverse_ref, mix_ref,
    offset_ref, second_ref, fc_in_ref, fc_out_ref, *scratch
):
    exchanged = block == 1
    if exchanged:
        out_ref, held, scratch = scratch[0], scratch[1], scratch[2:]
    else:
        share_ref, out_ref, shared_ref, scratch = scratch[0], scratch[1], scratch[2], scratch[3:]
        sent_share, came_share, scratch = scratch[0], scratch[1], scratch[2:]
    (
        normed, after, token, stage, landed, sums, all_sums, send_a, got_a, send_b, got_b,
        w_in, w_out, stream, hidden_ref, part_out, part_in,
        sent_team, came_team, sent_sum, came_sum, sent_a, came_a, sent_b, came_b, sent_out, came_out,
        sent_part, came_part, load, sent_load, came_load,
    ) = scratch
    if exchanged:
        quarter, slot = x_ref.shape[2:]
        rows, longitudes = x_ref.shape[1], 4 * quarter
    else:
        rows, longitudes, slot = x_ref.shape
        quarter = longitudes // 4
    packed = quarter * slot // 128
    comp, tile = lax.axis_index("comp"), lax.axis_index("tile")
    latitudes = rows * bands
    each = longitudes // 2 // bands
    me = lax.axis_index("band")
    mine = lax.axis_index("comp") * 2 + lax.axis_index("tile")

    def member(step):
        return lax.rem(mine + step, 4)

    def team_id(index):
        return {"comp": lax.div(index, 2), "tile": lax.rem(index, 2)}

    own_loads = [
        pltpu.make_async_copy(fc_in_ref.at[block], w_in.at[0], load.at[0]),
        pltpu.make_async_copy(fc_out_ref.at[block], w_out.at[0], load.at[1]),
    ]
    sibling_loads = [
        pltpu.make_async_remote_copy(
            src_ref=source.at[block],
            dst_ref=target.at[1],
            send_sem=sent_load.at[i],
            recv_sem=came_load.at[i],
            device_id={"tile": 1 - tile},
            device_id_type=MESH,
        )
        for i, (source, target) in enumerate(((fc_in_ref, w_in), (fc_out_ref, w_out)))
    ]
    for copy in own_loads:
        copy.start()
    barrier = pltpu.get_barrier_semaphore()

    def greet(step, carry):
        pl.semaphore_signal(
            barrier, inc=1, device_id={"band": lax.rem(me + step, bands)}, device_id_type=MESH
        )
        return carry

    for step in range(1, 4):
        pl.semaphore_signal(barrier, inc=1, device_id=team_id(member(step)), device_id_type=MESH)
    lax.fori_loop(1, bands, greet, 0)

    def team_copy(source, target, sent, came, step, whole=False, halves=False):
        index = member(step)
        return pltpu.make_async_remote_copy(
            src_ref=source if whole else source.at[lax.rem(index, 2) if halves else index],
            dst_ref=target.at[mine],
            send_sem=sent.at[index],
            recv_sem=came.at[mine],
            device_id=team_id(index),
            device_id_type=MESH,
        )

    def team_landing(source, target, sent, came, step, whole=False, halves=False):
        index = member(step)
        return pltpu.make_async_remote_copy(
            src_ref=source if whole else source.at[lax.rem(index, 2) if halves else index],
            dst_ref=target.at[index],
            send_sem=sent.at[index],
            recv_sem=came.at[index],
            device_id=team_id(index),
            device_id_type=MESH,
        )

    def team_exchange(*args):
        for step in range(1, 4):
            team_copy(*args[:4], step, *args[4:]).start()

    def team_finish(*args):
        for step in range(1, 4):
            team_landing(*args[:4], step, *args[4:]).wait()

    if exchanged:
        pl.semaphore_wait(barrier, bands - 1 + 3)
        team_exchange(x_ref, held, sent_team, came_team)
        held[mine] = x_ref[mine]
        team_finish(x_ref, held, sent_team, came_team)

    def tokens(lat):
        if exchanged:
            return jnp.concatenate([held[s, lat] for s in range(4)], axis=0)
        return x_ref[lat]

    ones = jnp.ones((8, slot), jnp.bfloat16)
    which = lax.broadcasted_iota(jnp.int32, (8, longitudes), 0)
    turned = (((1,), (1,)), ((), ()))

    def row_sum(values):
        return lax.dot_general(ones, values, turned, preferred_element_type=jnp.float32)

    total = jnp.zeros((8, longitudes), jnp.float32)
    for lat in range(rows):
        values = tokens(lat)
        wide = values.astype(jnp.float32)
        high, low = split_bf16(wide * wide)
        total = total + jnp.where(which == lat, row_sum(values), 0.0)
        total = total + jnp.where(which == rows + lat, row_sum(high) + row_sum(low), 0.0)
    sums[...] = total
    if not exchanged:
        pl.semaphore_wait(barrier, bands - 1 + 3)
    for copy in sibling_loads:
        copy.start()
    team_exchange(sums, all_sums, sent_sum, came_sum, True)
    if not exchanged:
        team_exchange(share_ref, shared_ref, sent_share, came_share, True)
        shared_ref[mine] = share_ref[...]
    all_sums[mine] = total
    team_finish(sums, all_sums, sent_sum, came_sum, True)
    total = (all_sums[0] + all_sums[1] + all_sums[2] + all_sums[3]) * (1.0 / (4 * slot))
    columns = jnp.concatenate([total, jnp.zeros((120, longitudes), jnp.float32)], axis=0).T

    lane = lax.broadcasted_iota(jnp.int32, (1, 128), 1)
    first_half = lane < slot - 128
    sign = jnp.where(first_half, 1.0, -1.0)
    half = longitudes // 2

    def spread(lat, wave, part, values):
        stage[pl.ds(part * 9 + lat * 3 + wave, bands, stride=32), :] = values

    def collect(lat, wave, part):
        return landed[pl.ds(part * 9 + lat * 3 + wave, bands, stride=32), :]

    for lat in range(rows):
        values = tokens(lat).astype(jnp.float32)
        average = columns[:, lat : lat + 1]
        second = columns[:, rows + lat : rows + lat + 1]
        scaled = (values - average) * lax.rsqrt(second - average * average + eps_norm)
        scaled = scaled * affine_ref[0:1, :] + affine_ref[1:2, :]
        normed[lat] = scaled
        tail = scaled[:, 128:]
        wide = jnp.concatenate([scaled[:, :128], tail, tail], axis=1)
        spectrum = product((forward_ref[0], forward_ref[1]), split_bf16(wide))
        upper, lower = spectrum[:half], spectrum[half:]
        parts = (upper[:, :128], lower[:, :128], jnp.where(first_half, upper[:, 128:], lower[:, 128:]))
        for part in range(3):
            for wave in range(each):
                spread(lat, wave, part, parts[part][wave * bands : (wave + 1) * bands])

    def band_copy(source, target, sent, came, step, landing):
        index = lax.rem(me + step, bands)
        return pltpu.make_async_remote_copy(
            src_ref=source.at[index],
            dst_ref=target.at[index if landing else me],
            send_sem=sent.at[index],
            recv_sem=came.at[index if landing else me],
            device_id={"band": index},
            device_id_type=MESH,
        )

    def band_exchange(source, target, sent, came):
        source[...] = stage[...].astype(jnp.bfloat16).reshape(source.shape)

        def go(step, carry):
            band_copy(source, target, sent, came, step, False).start()
            return carry

        lax.fori_loop(1, bands, go, 0)
        target[me] = source[me]

        def come(step, carry):
            band_copy(source, target, sent, came, step, True).wait()
            return carry

        lax.fori_loop(1, bands, come, 0)
        landed[...] = target[...].astype(jnp.float32).reshape(landed.shape)

    band_exchange(send_a, got_a, sent_a, came_a)
    pieces = []
    for wave in range(each):
        for part in range(3):
            pieces.append(
                jnp.concatenate([collect(lat, wave, part) for lat in range(rows)], axis=0)
            )
    spectrum = jnp.concatenate(pieces, axis=1).astype(jnp.bfloat16)
    turned_all = product((across_ref[0], across_ref[1]), (spectrum,))

    def combine(both, wave, direction):
        base = wave * 384
        cosine, sine = both[:latitudes, base : base + 384], both[latitudes:, base : base + 384]
        real = cosine[:, :128] + direction * sine[:, 128:256]
        imag = cosine[:, 128:256] - direction * sine[:, :128]
        rest = cosine[:, 256:] + (direction * sign) * pltpu.roll(sine[:, 256:], 64, 1)
        return real, imag, rest

    rows_in = jnp.concatenate(
        [jnp.concatenate(combine(turned_all, wave, 1.0), axis=1) for wave in range(each)], axis=0
    )
    hidden = product(split_bf16(rows_in), (mix_ref[0, 0], mix_ref[0, 1])) + offset_ref[0:1, :]
    hidden = jnp.maximum(hidden, 0.0)
    mixed = product(split_bf16(hidden), (mix_ref[1, 0], mix_ref[1, 1])) + offset_ref[1:2, :]
    mixed = soft_shrink(mixed)
    columns_back = jnp.concatenate(
        [mixed[wave * latitudes : (wave + 1) * latitudes] for wave in range(each)], axis=1
    )
    turned_back = product((back_ref[0], back_ref[1]), split_bf16(columns_back))
    for wave in range(each):
        parts = combine(turned_back, wave, -1.0)
        for part in range(3):
            for lat in range(rows):
                spread(lat, wave, part, parts[part][lat * bands : (lat + 1) * bands])
    band_exchange(send_b, got_b, sent_b, came_b)
    for lat in range(rows):
        real, imag, rest = (
            jnp.concatenate([collect(lat, wave, part) for wave in range(each)], axis=0)
            for part in range(3)
        )
        right = jnp.concatenate(
            [
                jnp.concatenate([real, rest], axis=1),
                jnp.concatenate([imag, pltpu.roll(rest, 64, 1)], axis=1),
            ],
            axis=0,
        ).astype(jnp.bfloat16)
        restored = product((inverse_ref[0], inverse_ref[1]), (right,))
        result = tokens(lat).astype(jnp.float32) + restored[:, :slot] + normed[lat]
        for s in range(4):
            piece = result[s * quarter : (s + 1) * quarter]
            tail = piece[:, 128:]
            tail = jnp.concatenate([tail[: quarter // 2], tail[quarter // 2 :]], axis=1)
            after[s % 2, s // 2, lat, :quarter] = piece[:, :128].astype(jnp.bfloat16)
            after[s % 2, s // 2, lat, quarter:] = tail.astype(jnp.bfloat16)
    team_exchange(after, token, sent_out, came_out, False, True)
    token[mine] = after[tile]
    team_finish(after, token, sent_out, came_out, False, True)
    for copy in own_loads:
        copy.wait()
    for copy in sibling_loads:
        copy.wait()
    if not exchanged:
        team_finish(share_ref, shared_ref, sent_share, came_share, True)

    def swap(values):
        return pltpu.roll(values, 64, 1)

    count = rows * quarter
    middle = quarter // 2

    def pair(left, right):
        return jnp.concatenate(
            [jnp.where(first_half, left, swap(right)), jnp.where(first_half, swap(left), right)], 0
        )

    def unpair(both):
        top, low = both[:middle], both[middle:]
        return jnp.where(first_half, top, swap(low)), jnp.where(first_half, swap(top), low)

    def lanes_of(slices):
        heads = [p[:quarter] for p in slices]
        tails = [p[quarter:] for p in slices]
        return jnp.concatenate(heads + [pair(*tails[:2]), pair(*tails[2:])], axis=1)

    def gather_rows(weight):
        heads = [weight[s * slot : s * slot + 128] for s in range(4)]
        tails = [weight[s * slot + 128 : (s + 1) * slot] for s in range(4)]
        return jnp.concatenate(heads + tails, axis=0)

    def reorder(values):
        t = [values[:, i * 128 : (i + 1) * 128] for i in range(6)]
        def inner(a, b):
            return jnp.where(first_half, swap(a), swap(b)), jnp.where(first_half, a, b)
        one, tails_a = inner(t[1], t[2])
        three, tails_b = inner(t[4], t[5])
        return jnp.concatenate([t[0], one, t[3], three, tails_a, tails_b], axis=1)

    def mlp(which_quarter):
        for lat in range(rows):
            slices = [token[s, which_quarter, lat].astype(jnp.float32) for s in range(4)]
            stream[lat * quarter : (lat + 1) * quarter] = lanes_of(slices)
        values = stream[...]
        normal = layer_norm(values, second_ref[0:1, :], second_ref[1:2, :]).astype(jnp.bfloat16)
        wide = w_in.shape[2]
        for part in range(2):
            weight = gather_rows(w_in[part])
            for start in range(0, wide, 256):
                z = jnp.dot(normal, weight[:, start : start + 256], preferred_element_type=jnp.float32)
                z = 0.5 * z * (1.0 + lax.erf(z * math.sqrt(0.5)))
                at = part * wide + start
                hidden_ref[:, at : at + 256] = z.astype(jnp.bfloat16)
        total = jnp.dot(hidden_ref[:, :wide], w_out[0], preferred_element_type=jnp.float32)
        total = total + jnp.dot(hidden_ref[:, wide:], w_out[1], preferred_element_type=jnp.float32)
        return reorder(total)

    if not exchanged:
        part_out[...] = mlp(1 - comp).astype(jnp.bfloat16)
        copy = pltpu.make_async_remote_copy(
            src_ref=part_out,
            dst_ref=part_in,
            send_sem=sent_part.at[0],
            recv_sem=came_part.at[0],
            device_id={"comp": 1 - comp},
            device_id_type=MESH,
        )
        copy.start()
        total = mlp(comp)
        copy.wait()
        result = stream[...] + total + part_in[...].astype(jnp.float32)
        out_ref[...] = result.astype(jnp.bfloat16)
        return

    for which_quarter in range(2):
        total = mlp(which_quarter)
        for lat in range(rows):
            block_rows = total[lat * quarter : (lat + 1) * quarter]
            tails = unpair(block_rows[:, 512:640]) + unpair(block_rows[:, 640:])
            for s in range(4):
                head = block_rows[:, s * 128 : (s + 1) * 128]
                part_out[which_quarter, s, lat, :quarter] = head.astype(jnp.bfloat16)
                part_out[which_quarter, s, lat, quarter:] = tails[s].astype(jnp.bfloat16)
        team_exchange(
            part_out.at[which_quarter], part_in.at[which_quarter],
            sent_part.at[which_quarter], came_part.at[which_quarter],
        )
        part_in[which_quarter, mine] = part_out[which_quarter, mine]
    for which_quarter in range(2):
        team_finish(
            part_out.at[which_quarter], part_in.at[which_quarter],
            sent_part.at[which_quarter], came_part.at[which_quarter],
        )
        for half_of in range(2):
            for lat in range(rows):
                piece = after[half_of, which_quarter, lat].astype(jnp.float32)
                piece = piece + part_in[which_quarter, half_of, lat].astype(jnp.float32)
                piece = piece + part_in[which_quarter, 2 + half_of, lat].astype(jnp.float32)
                tail = piece[quarter:]
                at = (2 * which_quarter + half_of) * quarter
                tail = jnp.concatenate([tail, swap(tail)], axis=0)
                out_ref[lat, at : at + quarter, :128] = piece[:quarter].astype(jnp.bfloat16)
                out_ref[lat, at : at + quarter, 128:] = tail[:, : slot - 128].astype(jnp.bfloat16)


def block_call(values, gain, shift, weights, biases, second, fc_in, fc_out, share, bands, block):
    exchanged = block == 1
    if exchanged:
        quarter, slot = values.shape[2:]
        rows, longitudes = values.shape[1], 4 * quarter
    else:
        rows, longitudes, slot = values.shape
        quarter = longitudes // 4
    latitudes = rows * bands
    channels, wide = fc_in.shape[1:]
    packed = quarter * slot // 128
    count = rows * quarter
    mats = transforms(latitudes, longitudes, bands)
    mix, offsets = mix_matrices(weights, biases)
    affine = jnp.concatenate([gain[None], shift[None], jnp.zeros((6, slot))], 0)
    chunks = pltpu.VMEM((bands, 32, 128), jnp.bfloat16)
    four, two = pltpu.SemaphoreType.DMA((4,)), pltpu.SemaphoreType.DMA((2,))
    both = pltpu.SemaphoreType.DMA((2, 4))
    many = pltpu.SemaphoreType.DMA((bands,))
    inside, outside = pl.BlockSpec(memory_space=pltpu.VMEM), pl.BlockSpec(memory_space=pl.ANY)
    arguments = [values, affine, *mats, mix, offsets, second, fc_in, fc_out]
    specs = [inside] * 9 + [outside] * 2
    if exchanged:
        shapes = jax.ShapeDtypeStruct((rows, longitudes, slot), jnp.bfloat16)
        out_specs = inside
        scratch = [pltpu.VMEM((4, rows, quarter, slot), jnp.bfloat16)]
        part = pltpu.VMEM((2, 4, rows, packed, 128), jnp.bfloat16)
        part_sems = both
    else:
        arguments.append(share)
        specs.append(inside)
        shapes = (
            jax.ShapeDtypeStruct((count, channels), jnp.bfloat16),
            jax.ShapeDtypeStruct((4,) + share.shape, share.dtype),
        )
        out_specs = (inside, inside)
        scratch = [four, four]
        part = pltpu.VMEM((count, channels), jnp.bfloat16)
        part_sems = two
    scratch += [
        pltpu.VMEM((rows, longitudes, slot), jnp.float32),
        pltpu.VMEM((2, 2, rows, packed, 128), jnp.bfloat16),
        pltpu.VMEM((4, 2, rows, packed, 128), jnp.bfloat16),
        pltpu.VMEM((bands * 32, 128), jnp.float32),
        pltpu.VMEM((bands * 32, 128), jnp.float32),
        pltpu.VMEM((8, longitudes), jnp.float32),
        pltpu.VMEM((4, 8, longitudes), jnp.float32),
        chunks, chunks, chunks, chunks,
        pltpu.VMEM((2, channels, wide), jnp.bfloat16),
        pltpu.VMEM((2, wide, channels), jnp.bfloat16),
        pltpu.VMEM((count, channels), jnp.float32),
        pltpu.VMEM((count, 2 * wide), jnp.bfloat16),
        part, part,
        four, four, four, four, many, many, many, many, four, four,
        part_sems, part_sems, two, two, two,
    ]
    return pl.pallas_call(
        functools.partial(block_kernel, bands, block),
        out_shape=shapes,
        in_specs=specs,
        out_specs=out_specs,
        scratch_shapes=scratch,
        compiler_params=pltpu.CompilerParams(
            collective_id=block, has_side_effects=True, vmem_limit_bytes=60 << 20
        ),
    )(*arguments)


def on_device(
    atmosphere,
    spec_weight,
    spec_bias,
    norm_gain,
    norm_shift,
    fc_in,
    fc_out,
    flux_head,
    flux_embed,
    ocean_state,
    sea_mask,
    depth_kernel,
    ocean_gain,
    ocean_shift,
    ocean_in,
    ocean_out,
    layer_scale,
    field_head,
    patch_embed,
):
    column_index = lax.axis_index(("comp", "tile"))
    team = ("comp", "tile")
    slot = atmosphere.shape[-1]
    bands = lax.axis_size("band")

    def heads_first(array):
        split = array.reshape(array.shape[:-1] + (4, slot))
        lead = array.shape[:-1]
        return jnp.concatenate(
            [split[..., :128].reshape(lead + (-1,)), split[..., 128:].reshape(lead + (-1,))], axis=-1
        )

    def run_block(values, block, share):
        gain = lax.dynamic_slice_in_dim(norm_gain[block, 0], column_index * slot, slot)
        shift = lax.dynamic_slice_in_dim(norm_shift[block, 0], column_index * slot, slot)
        second = jnp.stack([norm_gain[block, 1], norm_shift[block, 1]])
        second = jnp.concatenate([heads_first(second), jnp.zeros((6, 4 * slot))], axis=0)
        return block_call(
            values, gain, shift, spec_weight[block], spec_bias[block], second,
            fc_in, fc_out, share, bands, block,
        )

    share = jnp.concatenate([flux_head.astype(jnp.float32).T, patch_embed], axis=0)
    share = jnp.pad(share, ((0, 0), (0, 256 - slot)))
    after_one, shared = run_block(atmosphere, 0, share)
    after_one = after_one.reshape(atmosphere.shape[0], -1, 4 * slot)
    whole = heads_first(shared[:, :, :slot].transpose(1, 0, 2).reshape(share.shape[0], -1))
    head, embed = whole[:8], whole[8:]
    fluxes = jnp.einsum(
        "lnc,fc->lnf", after_one, head.astype(jnp.bfloat16), preferred_element_type=jnp.float32
    )
    upsampled = jnp.repeat(jnp.repeat(fluxes, 2, axis=0), 2, axis=1)
    sea_cells = sea_mask.astype(jnp.float32)[..., None]
    forcing = jnp.einsum("ijf,fc->ijc", upsampled, flux_embed, precision=full_precision)
    start = (ocean_state.astype(jnp.float32) + sea_cells * forcing).astype(jnp.bfloat16)
    widened = with_halo(start, ((("comp", "tile"), 1),), 3, True)
    extended = with_halo(widened, (("band", 0),), 3, False).astype(jnp.float32)
    tile_rows = start.shape[0]
    tile_columns = start.shape[1]
    convolved = jnp.zeros(start.shape, jnp.float32)
    for row_step in range(7):
        for col_step in range(7):
            convolved = (
                convolved
                + extended[row_step : row_step + tile_rows, col_step : col_step + tile_columns]
                * depth_kernel[row_step, col_step]
            )
    normed = layer_norm(convolved, ocean_gain, ocean_shift).astype(jnp.bfloat16)
    flat_cells = normed.reshape(-1, normed.shape[-1])
    hidden = jax.nn.gelu(
        jnp.dot(flat_cells, ocean_in, preferred_element_type=jnp.float32), approximate=False
    ).astype(jnp.bfloat16)
    update = jnp.dot(hidden, ocean_out, preferred_element_type=jnp.float32).reshape(start.shape)
    ocean_next = (start.astype(jnp.float32) + sea_cells * layer_scale * update).astype(jnp.bfloat16)
    surface = sea_cells * jnp.einsum(
        "ijc,cf->ijf", ocean_next.astype(jnp.float32), field_head, precision=full_precision
    )
    half_rows = tile_rows // 2
    half_columns = tile_columns // 2
    patches = (
        surface.reshape(half_rows, 2, half_columns, 2, surface.shape[2])
        .transpose(0, 2, 4, 1, 3)
        .reshape(half_rows, half_columns, -1)
    )
    embedding = jnp.einsum("pqk,kd->pqd", patches, embed, precision=full_precision)
    middle = (after_one.astype(jnp.float32) + embedding).astype(jnp.bfloat16)
    lead = middle.shape[:2]
    pieces = jnp.concatenate(
        [middle[..., :512].reshape(lead + (4, 128)), middle[..., 512:].reshape(lead + (4, slot - 128))],
        axis=-1,
    ).transpose(2, 0, 1, 3)
    atmosphere_next = run_block(pieces, 1, None)
    return (atmosphere_next, ocean_next, surface)


def solution(mesh):
    placed = (
        P("band", None, ("comp", "tile")),
        P(None, None, None, ("comp", "tile"), None),
        P(None, None, None, ("comp", "tile")),
        P(),
        P(),
        P(None, None, ("comp", "tile")),
        P(None, ("comp", "tile"), None),
        P(("comp", "tile"), None),
        P(),
        P("band", ("comp", "tile"), None),
        P("band", ("comp", "tile")),
        P(),
        P(),
        P(),
        P(),
        P(),
        P(),
        P(),
        P(None, ("comp", "tile")),
    )
    return jax.shard_map(
        on_device,
        mesh=mesh,
        in_specs=placed,
        out_specs=(
            P("band", None, ("comp", "tile")),
            P("band", ("comp", "tile"), None),
            P("band", ("comp", "tile"), None),
        ),
        check_vma=False,
    )
```

```python
import functools
import math

import jax
import jax.numpy as jnp
import numpy as np
from jax import lax
from jax.experimental import pallas as pl
from jax.experimental.pallas import tpu as pltpu
from jax.sharding import PartitionSpec as P

MESH = pl.DeviceIdType.MESH
full_precision = lax.Precision.HIGHEST
eps_norm = 1e-06
shrink_level = 0.01


def layer_norm(values, scaling, offset):
    average = jnp.mean(values, axis=-1, keepdims=True)
    squares = jnp.mean(values * values, axis=-1, keepdims=True)
    variance = squares - average * average
    return (values - average) * lax.rsqrt(variance + eps_norm) * scaling + offset


def soft_shrink(values):
    zeros = jnp.zeros_like(values)
    return jnp.where(
        values > shrink_level,
        values - shrink_level,
        jnp.where(values < -shrink_level, values + shrink_level, zeros),
    )


def split_bf16(array):
    high = array.astype(jnp.bfloat16)
    return high, (array - high.astype(jnp.float32)).astype(jnp.bfloat16)


def host_split(array):
    whole = np.asarray(array, np.float32)
    high = whole.astype(jnp.bfloat16)
    low = (whole - high.astype(np.float32)).astype(jnp.bfloat16)
    return jnp.asarray(np.stack([high, low]))


def transforms(latitudes, longitudes, bands):
    kept = longitudes // 2
    each, rows = kept // bands, latitudes // bands
    waves = np.arange(kept).reshape(bands, each).T.reshape(-1)
    lats = np.arange(latitudes).reshape(bands, rows).T.reshape(-1)
    lon = np.outer(waves, np.arange(longitudes)) % longitudes * (2.0 * math.pi / longitudes)
    lat = np.outer(np.arange(latitudes), lats) % latitudes * (2.0 * math.pi / latitudes)
    forward = np.concatenate([np.cos(lon), -np.sin(lon)], 0) / math.sqrt(longitudes)
    across = np.stack([np.cos(lat), np.sin(lat)], 0) / math.sqrt(latitudes)
    weight = np.where(waves == 0, 1.0, 2.0)[:, None]
    inverse = np.concatenate([np.cos(lon) * weight, -np.sin(lon) * weight], 0).T
    return (
        host_split(forward),
        host_split(across.reshape(2 * latitudes, latitudes)),
        host_split(across.transpose(0, 2, 1).reshape(2 * latitudes, latitudes)),
        host_split(inverse / math.sqrt(longitudes)),
    )


def mix_matrices(weights, biases):
    slot, width = weights.shape[-2:]
    groups = slot // width
    eye = jnp.eye(groups, dtype=weights.dtype)
    full = weights.reshape(2, 2, groups, width, 1, width) * eye[None, None, :, None, :, None]
    full = full.reshape(2, 2, slot, slot)
    whole = jnp.concatenate(
        [
            jnp.concatenate([full[:, 0], full[:, 1]], axis=2),
            jnp.concatenate([-full[:, 1], full[:, 0]], axis=2),
        ],
        axis=1,
    )
    def lanes(array, axis):
        part = [lax.slice_in_dim(array, a, b, axis=axis) for a, b in
                ((0, 128), (slot, slot + 128), (128, slot), (slot + 128, 2 * slot))]
        return jnp.concatenate(part, axis=axis)
    whole = lanes(lanes(whole, 1), 2)
    high, low = split_bf16(whole)
    offsets = lanes(biases.reshape(2, 2 * slot), 1)
    return jnp.stack([high, low], axis=1), jnp.concatenate([offsets, jnp.zeros((6, 2 * slot))], 0)


def product(left, right):
    total = None
    for a, b in ((0, 0), (1, 0), (0, 1)):
        if a < len(left) and b < len(right):
            term = jnp.dot(left[a], right[b], preferred_element_type=jnp.float32)
            total = term if total is None else total + term
    return total


directions = [(b, c) for b in (-1, 0, 1) for c in (-1, 0, 1) if (b, c) != (0, 0)]


def ocean_selectors(quarter):
    columns = np.arange(-8, 2 * quarter + 8)
    pick = np.zeros((len(columns), 384), np.float32)
    seen = np.zeros((len(columns), 512), np.float32)
    for i, column in enumerate(columns):
        if not -3 <= column < 2 * quarter + 3:
            continue
        token = column // 2
        side = 0 if token < 0 else 2 if token >= quarter else 1
        pick[i, side * 128 + token % quarter] = 1
        inner = column % (2 * quarter)
        seen[i, inner - 128 if column < 0 else 384 + inner if column >= 2 * quarter else 128 + inner] = 1
    split = np.zeros((2 * quarter, 2 * quarter), np.float32)
    for e in range(2):
        split[e * quarter + np.arange(quarter), 2 * np.arange(quarter) + e] = 1
    return (jnp.asarray(m, jnp.bfloat16) for m in (pick, seen, split))


def thirds(array):
    high = array.astype(jnp.bfloat16)
    rest = array - high.astype(jnp.float32)
    middle = rest.astype(jnp.bfloat16)
    return high, middle, (rest - middle.astype(jnp.float32)).astype(jnp.bfloat16)


def gelu(z):
    return 0.5 * z * (1.0 + lax.erf(z * math.sqrt(0.5)))


def step_kernel(bands, *refs):
    (
        x_ref, affine_ref, forward_ref, across_ref, back_ref, inverse_ref, mix_ref, offset_ref,
        second_ref, fc_in_ref, fc_out_ref, share_ref, ocean_ref, mask_ref, spread_ref, depth_ref,
        ocean_affine_ref, ocean_in_ref, ocean_out_ref, field_ref, pick_ref, seen_ref, split_ref,
        atmosphere_ref, next_ref, surface_ref,
        normed, after, token, stage, landed, sums, all_sums, send_a, got_a, send_b, got_b,
        w_in, w_out, stream, hidden_ref, half_out, half_in, part_out, part_in, shared_ref,
        rows_in, cols_in, corner_in, masks_in, flux_ref, flux_in, tile_ref, conv_ref, wave_ref,
        middle_out, middle_in,
        sent_sum, came_sum, sent_a, came_a, sent_b, came_b, sent_out, came_out,
        sent_half, came_half, sent_part, came_part, load, sent_load, came_load,
        sent_share, came_share, sent_cells, came_cells, sent_mask, came_mask, sent_flux, came_flux,
        sent_middle, came_middle,
    ) = refs
    rows, longitudes, slot = x_ref.shape
    quarter = longitudes // 4
    middle = quarter // 2
    latitudes = rows * bands
    each = longitudes // 2 // bands
    cells = ocean_ref.shape[1]
    me = lax.axis_index("band")
    comp, tile = lax.axis_index("comp"), lax.axis_index("tile")
    mine = comp * 2 + tile

    def member(step):
        return lax.rem(mine + step, 4)

    def team_id(index):
        return {"comp": lax.div(index, 2), "tile": lax.rem(index, 2)}

    def near_id(b, c):
        index = lax.rem(mine + c + 4, 4)
        return {"band": lax.rem(me + b + bands, bands), **team_id(index)}

    own_loads = [
        pltpu.make_async_copy(source.at[block], target.at[block, 0], load.at[block, i])
        for block in range(2)
        for i, (source, target) in enumerate(((fc_in_ref, w_in), (fc_out_ref, w_out)))
    ]
    sibling_loads = [
        pltpu.make_async_remote_copy(
            src_ref=source.at[block],
            dst_ref=target.at[block, 1],
            send_sem=sent_load.at[block, i],
            recv_sem=came_load.at[block, i],
            device_id={"tile": 1 - tile},
            device_id_type=MESH,
        )
        for block in range(2)
        for i, (source, target) in enumerate(((fc_in_ref, w_in), (fc_out_ref, w_out)))
    ]
    barrier = pltpu.get_barrier_semaphore()

    def greet(step, carry):
        pl.semaphore_signal(
            barrier, inc=1, device_id={"band": lax.rem(me + step, bands)}, device_id_type=MESH
        )
        return carry

    for step in range(1, 4):
        pl.semaphore_signal(barrier, inc=1, device_id=team_id(member(step)), device_id_type=MESH)
    for b, c in directions:
        if b and c:
            pl.semaphore_signal(barrier, inc=1, device_id=near_id(b, c), device_id_type=MESH)
    lax.fori_loop(1, bands, greet, 0)
    for copy in own_loads:
        copy.start()

    def near_copies(source_of, target_of, sent, came):
        copies = []
        for d, (b, c) in enumerate(directions):
            copies.append(
                pltpu.make_async_remote_copy(
                    src_ref=source_of(b, c),
                    dst_ref=target_of(-b, -c),
                    send_sem=sent.at[d],
                    recv_sem=came.at[directions.index((-b, -c))],
                    device_id=near_id(b, c),
                    device_id_type=MESH,
                )
            )
        return copies

    def near_landings(source_of, target_of, sent, came):
        copies = []
        for d, (b, c) in enumerate(directions):
            copies.append(
                pltpu.make_async_remote_copy(
                    src_ref=source_of(b, c),
                    dst_ref=target_of(b, c),
                    send_sem=sent.at[d],
                    recv_sem=came.at[d],
                    device_id=near_id(b, c),
                    device_id_type=MESH,
                )
            )
        return copies

    def cells_from(b, c):
        row = pl.ds(0, 2 * rows) if b == 0 else pl.ds(2 * rows - 3 if b > 0 else 0, 3)
        column = pl.ds(0, cells) if c == 0 else pl.ds(cells - 16 if c > 0 else 0, 16)
        return ocean_ref.at[row, column]

    def cells_to(b, c):
        if c == 0:
            return rows_in.at[0 if b < 0 else 1]
        if b == 0:
            return cols_in.at[0 if c < 0 else 1]
        return corner_in.at[0 if b < 0 else 1, 0 if c < 0 else 1]

    cell_args = (cells_from, cells_to, sent_cells, came_cells)
    mask_args = (
        lambda b, c: mask_ref, lambda b, c: masks_in.at[directions.index((b, c))], sent_mask, came_mask
    )
    flux_args = (
        lambda b, c: flux_ref, lambda b, c: flux_in.at[directions.index((b, c))], sent_flux, came_flux
    )

    def team_copy(source, target, sent, came, step, pick, landing):
        index = member(step)
        chosen = {"whole": lambda: source, "half": lambda: source.at[lax.rem(index, 2)],
                  "each": lambda: source.at[index]}[pick]()
        place = index if landing else mine
        return pltpu.make_async_remote_copy(
            src_ref=chosen,
            dst_ref=target.at[place],
            send_sem=sent.at[index],
            recv_sem=came.at[place],
            device_id=team_id(index),
            device_id_type=MESH,
        )

    def team_exchange(source, target, sent, came, pick):
        for step in range(1, 4):
            team_copy(source, target, sent, came, step, pick, False).start()

    def team_finish(source, target, sent, came, pick):
        for step in range(1, 4):
            team_copy(source, target, sent, came, step, pick, True).wait()

    def band_copy(source, target, sent, came, step, landing):
        index = lax.rem(me + step, bands)
        return pltpu.make_async_remote_copy(
            src_ref=source.at[index],
            dst_ref=target.at[index if landing else me],
            send_sem=sent.at[index],
            recv_sem=came.at[index if landing else me],
            device_id={"band": index},
            device_id_type=MESH,
        )

    def band_exchange(source, target, sent, came):
        source[...] = stage[...].astype(jnp.bfloat16).reshape(source.shape)

        def go(step, carry):
            band_copy(source, target, sent, came, step, False).start()
            return carry

        lax.fori_loop(1, bands, go, 0)
        target[me] = source[me]

        def come(step, carry):
            band_copy(source, target, sent, came, step, True).wait()
            return carry

        lax.fori_loop(1, bands, come, 0)
        landed[...] = target[...].astype(jnp.float32).reshape(landed.shape)

    lane = lax.broadcasted_iota(jnp.int32, (1, 128), 1)
    first_half = lane < slot - 128
    sign = jnp.where(first_half, 1.0, -1.0)
    half = longitudes // 2
    counted = jnp.where(lax.broadcasted_iota(jnp.int32, (8, 256), 1) < slot, 1.0, 0.0)
    counted = counted.astype(jnp.bfloat16)
    which = lax.broadcasted_iota(jnp.int32, (8, longitudes), 0)
    turned = (((1,), (1,)), ((), ()))

    def across_rows(left, right):
        return lax.dot_general(left, right, turned, preferred_element_type=jnp.float32)

    def swap(values):
        return pltpu.roll(values, 64, 1)

    def doubled(tails):
        top = jnp.where(first_half, tails, swap(tails))
        low = jnp.where(first_half, swap(tails), tails)
        return jnp.concatenate([top, low], axis=0)

    def tokens(block, lat):
        if block == 0:
            values = x_ref[lat].astype(jnp.float32)
            return jnp.concatenate([values, values[:, 128:]], axis=1)
        pieces = [middle_in[s, lat].astype(jnp.float32) for s in range(4)]
        return jnp.concatenate(
            [jnp.concatenate([p[:quarter], doubled(p[quarter:])], axis=1) for p in pieces], axis=0
        )

    def spread(lat, wave, part, values):
        stage[pl.ds(part * 9 + lat * 3 + wave, bands, stride=32), :] = values

    def collect(lat, wave, part):
        return landed[pl.ds(part * 9 + lat * 3 + wave, bands, stride=32), :]

    def spectral_filter(block):
        total = jnp.zeros((8, longitudes), jnp.float32)
        for lat in range(rows):
            values = tokens(block, lat)
            high, low = split_bf16(values * values)
            total = total + jnp.where(
                which == lat, across_rows(counted, values.astype(jnp.bfloat16)), 0.0
            )
            total = total + jnp.where(
                which == rows + lat, across_rows(counted, high) + across_rows(counted, low), 0.0
            )
        sums[...] = total
        if block == 0:
            pl.semaphore_wait(barrier, bands - 1 + 3 + 4)
        team_exchange(sums, all_sums.at[block], sent_sum.at[block], came_sum.at[block], "whole")
        if block == 0:
            for copy in near_copies(*mask_args) + near_copies(*cell_args) + sibling_loads:
                copy.start()
            team_exchange(share_ref, shared_ref, sent_share, came_share, "whole")
            shared_ref[mine] = share_ref[...]
        all_sums[block, mine] = total
        team_finish(sums, all_sums.at[block], sent_sum.at[block], came_sum.at[block], "whole")
        total = (
            all_sums[block, 0] + all_sums[block, 1] + all_sums[block, 2] + all_sums[block, 3]
        ) * (1.0 / (4 * slot))
        columns = jnp.concatenate([total, jnp.zeros((120, longitudes), jnp.float32)], axis=0).T
        for lat in range(rows):
            average = columns[:, lat : lat + 1]
            power = columns[:, rows + lat : rows + lat + 1]
            scaled = tokens(block, lat) - average
            scaled = scaled * lax.rsqrt(power - average * average + eps_norm)
            scaled = scaled * affine_ref[block, 0:1, :] + affine_ref[block, 1:2, :]
            normed[lat] = scaled
            spectrum = product((forward_ref[0], forward_ref[1]), split_bf16(scaled))
            upper, lower = spectrum[:half], spectrum[half:]
            rest = jnp.where(first_half, upper[:, 128:], lower[:, 128:])
            parts = (upper[:, :128], lower[:, :128], rest)
            for part in range(3):
                for wave in range(each):
                    spread(lat, wave, part, parts[part][wave * bands : (wave + 1) * bands])
        band_exchange(send_a, got_a.at[block], sent_a.at[block], came_a.at[block])
        pieces = []
        for wave in range(each):
            for part in range(3):
                pieces.append(
                    jnp.concatenate([collect(lat, wave, part) for lat in range(rows)], axis=0)
                )
        spectrum = jnp.concatenate(pieces, axis=1).astype(jnp.bfloat16)
        turned_all = product((across_ref[0], across_ref[1]), (spectrum,))

        def combine(both, wave, direction):
            base = wave * 384
            cosine, sine = both[:latitudes, base : base + 384], both[latitudes:, base : base + 384]
            real = cosine[:, :128] + direction * sine[:, 128:256]
            imag = cosine[:, 128:256] - direction * sine[:, :128]
            rest = cosine[:, 256:] + (direction * sign) * swap(sine[:, 256:])
            return real, imag, rest

        rows_mixed = jnp.concatenate(
            [jnp.concatenate(combine(turned_all, wave, 1.0), axis=1) for wave in range(each)], axis=0
        )
        hidden = product(split_bf16(rows_mixed), (mix_ref[block, 0, 0], mix_ref[block, 0, 1]))
        hidden = jnp.maximum(hidden + offset_ref[block, 0:1, :], 0.0)
        mixed = product(split_bf16(hidden), (mix_ref[block, 1, 0], mix_ref[block, 1, 1]))
        mixed = soft_shrink(mixed + offset_ref[block, 1:2, :])
        mixed = jnp.concatenate(
            [mixed[wave * latitudes : (wave + 1) * latitudes] for wave in range(each)], axis=1
        )
        turned_back = product((back_ref[0], back_ref[1]), split_bf16(mixed))
        for wave in range(each):
            parts = combine(turned_back, wave, -1.0)
            for part in range(3):
                for lat in range(rows):
                    spread(lat, wave, part, parts[part][lat * bands : (lat + 1) * bands])
        band_exchange(send_b, got_b.at[block], sent_b.at[block], came_b.at[block])
        for lat in range(rows):
            real, imag, rest = (
                jnp.concatenate([collect(lat, wave, part) for wave in range(each)], axis=0)
                for part in range(3)
            )
            right = jnp.concatenate(
                [
                    jnp.concatenate([real, rest], axis=1),
                    jnp.concatenate([imag, swap(rest)], axis=1),
                ],
                axis=0,
            ).astype(jnp.bfloat16)
            restored = product((inverse_ref[0], inverse_ref[1]), (right,))
            result = tokens(block, lat) + restored + normed[lat]
            for s in range(4):
                piece = result[s * quarter : (s + 1) * quarter]
                tail = piece[:, 128:]
                tail = jnp.where(first_half, tail[:middle], swap(tail[middle:]))
                after[s % 2, s // 2, lat, :quarter] = piece[:, :128].astype(jnp.bfloat16)
                after[s % 2, s // 2, lat, quarter:] = tail.astype(jnp.bfloat16)
        args = (after, token.at[block], sent_out.at[block], came_out.at[block], "half")
        team_exchange(*args)
        token[block, mine] = after[tile]
        team_finish(*args)
        for i in range(2):
            own_loads[2 * block + i].wait()
            sibling_loads[2 * block + i].wait()

    def pair(left, right):
        return jnp.concatenate(
            [jnp.where(first_half, left, swap(right)), jnp.where(first_half, swap(left), right)], 0
        )

    def unpair(both):
        top, low = both[:middle], both[middle:]
        return jnp.where(first_half, top, swap(low)), jnp.where(first_half, swap(top), low)

    def pack(block_rows, target):
        tails = unpair(block_rows[:, 512:640]) + unpair(block_rows[:, 640:])
        for s in range(4):
            place = target(s)
            place[:quarter] = block_rows[:, s * 128 : (s + 1) * 128].astype(jnp.bfloat16)
            place[quarter:] = tails[s].astype(jnp.bfloat16)

    def lanes_of(slices):
        heads = [p[:quarter] for p in slices]
        tails = [p[quarter:] for p in slices]
        return jnp.concatenate(heads + [pair(*tails[:2]), pair(*tails[2:])], axis=1)

    def reorder(values):
        t = [values[:, i * 128 : (i + 1) * 128] for i in range(6)]

        def inner(a, b):
            return jnp.where(first_half, swap(a), swap(b)), jnp.where(first_half, a, b)

        one, tails_a = inner(t[1], t[2])
        three, tails_b = inner(t[4], t[5])
        return jnp.concatenate([t[0], one, t[3], three, tails_a, tails_b], axis=1)

    row_spans = [(s * slot, 128) for s in range(4)] + [(s * slot + 128, slot - 128) for s in range(4)]

    def mlp(block, which_quarter):
        for lat in range(rows):
            slices = [token[block, s, which_quarter, lat].astype(jnp.float32) for s in range(4)]
            stream[lat * quarter : (lat + 1) * quarter] = lanes_of(slices)
        values = stream[...]
        normal = layer_norm(values, second_ref[block, 0:1, :], second_ref[block, 1:2, :])
        normal = normal.astype(jnp.bfloat16)
        wide = w_in.shape[3]
        for part in range(2):

            def piece(i, carry):
                at = pl.multiple_of(i * 256, 256)
                weight = jnp.concatenate(
                    [w_in[block, part, pl.ds(a, n), pl.ds(at, 256)] for a, n in row_spans], axis=0
                )
                z = jnp.dot(normal, weight, preferred_element_type=jnp.float32)
                hidden_ref[:, pl.ds(part * wide + at, 256)] = gelu(z).astype(jnp.bfloat16)
                return carry

            lax.fori_loop(0, wide // 256, piece, 0)
        total = jnp.dot(hidden_ref[:, :wide], w_out[block, 0], preferred_element_type=jnp.float32)
        total = total + jnp.dot(
            hidden_ref[:, wide:], w_out[block, 1], preferred_element_type=jnp.float32
        )
        return reorder(total)

    spectral_filter(0)
    team_finish(share_ref, shared_ref, sent_share, came_share, "whole")
    half_out[...] = mlp(0, 1 - comp).astype(jnp.bfloat16)
    copy = pltpu.make_async_remote_copy(
        src_ref=half_out,
        dst_ref=half_in,
        send_sem=sent_half.at[0],
        recv_sem=came_half.at[0],
        device_id={"comp": 1 - comp},
        device_id_type=MESH,
    )
    copy.start()
    total = mlp(0, comp)
    copy.wait()
    first = stream[...] + total + half_in[...].astype(jnp.float32)
    first = first.astype(jnp.bfloat16)
    stream[...] = first.astype(jnp.float32)

    small = [shared_ref[s] for s in range(4)]
    tails = [s[:, 128:] for s in small]
    whole = jnp.concatenate(
        [s[:, :128] for s in small]
        + [jnp.where(first_half, tails[i], swap(tails[i + 1])) for i in (0, 2)],
        axis=1,
    )
    head, embed = whole[:8].astype(jnp.bfloat16), whole[8:]
    for lat in range(rows):
        flux = across_rows(head, first[lat * quarter : (lat + 1) * quarter])
        flux_ref[lat] = jnp.concatenate([flux, jnp.zeros((8, 128 - quarter), jnp.float32)], axis=1)
    for copy in near_copies(*flux_args):
        copy.start()
    for copy in near_landings(*mask_args) + near_landings(*cell_args) + near_landings(*flux_args):
        copy.wait()

    def flux_at(lat, c):
        b = -1 if lat < 0 else 1 if lat >= rows else 0
        if (b, c) == (0, 0):
            return flux_ref[lat]
        return flux_in[directions.index((b, c)), lat % rows]

    ext_lats = range(-2, rows + 2)
    laid = jnp.concatenate(
        [jnp.concatenate([flux_at(lat, c) for c in (-1, 0, 1)], axis=1) for lat in ext_lats]
        + [jnp.zeros((128 - 8 * len(ext_lats), 384), jnp.float32)],
        axis=0,
    )
    raised = across_rows(pick_ref[...], jnp.concatenate(thirds(laid), axis=0))
    raised = raised[:, :128] + raised[:, 128:256] + raised[:, 256:]
    forcing = product(split_bf16(raised), (spread_ref[0], spread_ref[1]))

    def mask_rows(b, c):
        whole = mask_ref[...] if (b, c) == (0, 0) else masks_in[directions.index((b, c))]
        whole = whole[:, 128:] if c < 0 else whole[:, :128] if c > 0 else whole
        return whole[2 * rows - 3 : 2 * rows] if b < 0 else whole[:3] if b > 0 else whole[: 2 * rows]

    ext_rows = 2 * rows + 6
    masks = jnp.concatenate(
        [jnp.concatenate([mask_rows(b, c) for c in (-1, 0, 1)], axis=1) for b in (-1, 0, 1)]
        + [jnp.zeros((16 - ext_rows, 512), jnp.float32)],
        axis=0,
    )
    masks = across_rows(seen_ref[...], masks.astype(jnp.bfloat16))
    for row in range(ext_rows):
        b = -1 if row < 3 else 1 if row >= 2 * rows + 3 else 0
        at = row if b < 0 else row - 3 if b == 0 else row - 2 * rows - 3
        sources = (
            cols_in[0, at] if b == 0 else corner_in[0 if b < 0 else 1, 0, at],
            ocean_ref[at] if b == 0 else rows_in[0 if b < 0 else 1, at],
            cols_in[1, at] if b == 0 else corner_in[0 if b < 0 else 1, 1, at],
        )
        sources = [s.astype(jnp.float32) for s in sources]
        state = jnp.concatenate([sources[0][8:], sources[1], sources[2][:8]], axis=0)
        level = (row - 3) // 2 + 2
        start = state + masks[:, row : row + 1] * forcing[:, level * 256 : (level + 1) * 256]
        start = start.astype(jnp.bfloat16).astype(jnp.float32)
        if b:
            inside = jnp.where(me > 0, 1.0, 0.0) if b < 0 else jnp.where(me < bands - 1, 1.0, 0.0)
            start = start * inside
        for part in range(2):
            tile_ref[part, row] = start[:, part * 128 : (part + 1) * 128]

    for part in range(2):
        span = slice(part * 128, (part + 1) * 128)

        def strip(i, carry):
            at = pl.multiple_of(i * 16, 16)
            totals = [jnp.zeros((16, 128), jnp.float32) for _ in range(2 * rows)]
            for e in range(7):
                for row in range(ext_rows):
                    values = tile_ref[part, row, pl.ds(at + 5 + e, 16), :]
                    for a in range(7):
                        if 0 <= row - a < 2 * rows:
                            tap = depth_ref[a * 7 + e : a * 7 + e + 1, span]
                            totals[row - a] = totals[row - a] + values * tap
            for row in range(2 * rows):
                conv_ref[row, pl.ds(at, 16), span] = totals[row]
            return carry

        lax.fori_loop(0, cells // 16, strip, 0)

    own_columns = jnp.concatenate([mask_ref[...], jnp.zeros((120, 256), jnp.float32)], axis=0).T
    for start_row in range(0, 2 * rows, 2):
        values = conv_ref[start_row : start_row + 2].reshape(2 * cells, 256)
        normal = layer_norm(values, ocean_affine_ref[0:1, :], ocean_affine_ref[1:2, :])
        normal = normal.astype(jnp.bfloat16)

        def piece(i, carry):
            at = pl.multiple_of(i * 256, 256)
            z = jnp.dot(normal, ocean_in_ref[:, pl.ds(at, 256)], preferred_element_type=jnp.float32)
            wave_ref[:, pl.ds(at, 256)] = gelu(z).astype(jnp.bfloat16)
            return carry

        lax.fori_loop(0, ocean_in_ref.shape[1] // 256, piece, 0)
        update = jnp.dot(wave_ref[...], ocean_out_ref[...], preferred_element_type=jnp.float32)
        update = update * ocean_affine_ref[2:3, :]
        for row in range(start_row, start_row + 2):
            begin = jnp.concatenate([tile_ref[part, row + 3, 8 : 8 + cells] for part in range(2)], axis=1)
            change = update[(row - start_row) * cells : (row - start_row + 1) * cells]
            fresh = (begin + own_columns[:cells, row : row + 1] * change).astype(jnp.bfloat16)
            next_ref[row] = fresh
            field = across_rows(field_ref[...], fresh)
            field = (field[:8] + field[8:16] + field[16:24]) * mask_ref[row : row + 1, :cells]
            surface_ref[row] = field

    for lat in range(rows):
        both = jnp.concatenate([surface_ref[2 * lat], surface_ref[2 * lat + 1]], axis=0)
        patch = across_rows(split_ref[...], jnp.concatenate(thirds(both), axis=0))
        patch = patch[:, :16] + patch[:, 16:32] + patch[:, 32:48]
        total = stream[lat * quarter : (lat + 1) * quarter]
        for e in range(2):
            total = total + product(
                split_bf16(patch[e * quarter : (e + 1) * quarter]),
                split_bf16(embed[e * 16 : (e + 1) * 16]),
            )
        pack(total, lambda s, lat=lat: middle_out.at[s, lat])
    args = (middle_out, middle_in, sent_middle, came_middle, "each")
    team_exchange(*args)
    middle_in[mine] = middle_out[mine]
    team_finish(*args)

    spectral_filter(1)
    for which_quarter in range(2):
        total = mlp(1, which_quarter)
        for lat in range(rows):
            pack(
                total[lat * quarter : (lat + 1) * quarter],
                lambda s, lat=lat: part_out.at[which_quarter, s, lat],
            )
        team_exchange(
            part_out.at[which_quarter], part_in.at[which_quarter],
            sent_part.at[which_quarter], came_part.at[which_quarter], "each",
        )
        part_in[which_quarter, mine] = part_out[which_quarter, mine]
    for which_quarter in range(2):
        team_finish(
            part_out.at[which_quarter], part_in.at[which_quarter],
            sent_part.at[which_quarter], came_part.at[which_quarter], "each",
        )
        for half_of in range(2):
            for lat in range(rows):
                piece = after[half_of, which_quarter, lat].astype(jnp.float32)
                piece = piece + part_in[which_quarter, half_of, lat].astype(jnp.float32)
                piece = piece + part_in[which_quarter, 2 + half_of, lat].astype(jnp.float32)
                tail = piece[quarter:]
                at = (2 * which_quarter + half_of) * quarter
                tail = jnp.concatenate([tail, swap(tail)], axis=0)
                atmosphere_ref[lat, at : at + quarter, :128] = piece[:quarter].astype(jnp.bfloat16)
                atmosphere_ref[lat, at : at + quarter, 128:] = tail[:, : slot - 128].astype(
                    jnp.bfloat16
                )


def on_device(
    atmosphere, spec_weight, spec_bias, norm_gain, norm_shift, fc_in, fc_out, flux_head, flux_embed,
    ocean_state, sea_mask, depth_kernel, ocean_gain, ocean_shift, ocean_in, ocean_out, layer_scale,
    field_head, patch_embed,
):
    column_index = lax.axis_index(("comp", "tile"))
    bands = lax.axis_size("band")
    rows, longitudes, slot = atmosphere.shape
    quarter = longitudes // 4
    count = rows * quarter
    latitudes = rows * bands
    channels, wide = fc_in.shape[1:]
    packed = quarter * slot // 128
    cells, ocean_channels = ocean_state.shape[1:]
    waves = ocean_in.shape[1]

    def heads_first(array):
        split = array.reshape(array.shape[:-1] + (4, slot))
        lead = array.shape[:-1]
        return jnp.concatenate(
            [split[..., :128].reshape(lead + (-1,)), split[..., 128:].reshape(lead + (-1,))], axis=-1
        )

    def taller(array, height):
        return jnp.pad(array, ((0, 0),) * (array.ndim - 2) + ((0, height - array.shape[-2]), (0, 0)))

    affine = jnp.stack([norm_gain[:, 0], norm_shift[:, 0]], axis=1)
    affine = lax.dynamic_slice_in_dim(affine, column_index * slot, slot, axis=2)
    affine = taller(jnp.concatenate([affine, affine[:, :, 128:]], axis=2), 8)
    second = taller(heads_first(jnp.stack([norm_gain[:, 1], norm_shift[:, 1]], axis=1)), 8)
    mixes = [mix_matrices(spec_weight[b], spec_bias[b]) for b in range(2)]
    mix = jnp.stack([m[0] for m in mixes])
    offsets = jnp.stack([m[1] for m in mixes])
    patch = patch_embed.reshape(4, 2, 2, slot).transpose(2, 1, 0, 3)
    patch = jnp.pad(patch, ((0, 0), (0, 0), (0, 4), (0, 0))).reshape(32, slot)
    share = jnp.concatenate([flux_head.astype(jnp.float32).T, patch], axis=0)
    share = jnp.pad(share, ((0, 0), (0, 256 - slot)))
    mask = jnp.pad(sea_mask.astype(jnp.float32), ((0, 8 - sea_mask.shape[0]), (0, 256 - cells)))
    levels = rows + 4
    embed = jnp.eye(levels)[:, None, :, None] * flux_embed[None, :, None, :]
    embed = taller(embed.reshape(levels * 8, levels * ocean_channels), 128)
    embed = jnp.stack(split_bf16(embed))
    depth = taller(depth_kernel.reshape(49, ocean_channels), 56)
    ocean_affine = taller(jnp.stack([ocean_gain, ocean_shift, layer_scale]), 8)
    field = jnp.concatenate([jnp.pad(f, ((0, 4), (0, 0))) for f in thirds(field_head.T)], axis=0)
    inside, outside = pl.BlockSpec(memory_space=pltpu.VMEM), pl.BlockSpec(memory_space=pl.ANY)
    arguments = [
        atmosphere, affine, *transforms(latitudes, longitudes, bands), mix, offsets, second,
        fc_in, fc_out, share, ocean_state, mask, embed, depth, ocean_affine, ocean_in, ocean_out,
        field, *ocean_selectors(quarter),
    ]
    specs = [inside] * 9 + [outside] * 2 + [inside] * (len(arguments) - 11)
    narrow, single = jnp.bfloat16, jnp.float32

    def dma(*shape):
        return pltpu.SemaphoreType.DMA(shape)

    chunks = (bands, 32, 128)
    scratch = [
        pltpu.VMEM((rows, longitudes, 256), single),
        pltpu.VMEM((2, 2, rows, packed, 128), narrow),
        pltpu.VMEM((2, 4, 2, rows, packed, 128), narrow),
        pltpu.VMEM((bands * 32, 128), single),
        pltpu.VMEM((bands * 32, 128), single),
        pltpu.VMEM((8, longitudes), single),
        pltpu.VMEM((2, 4, 8, longitudes), single),
        pltpu.VMEM(chunks, narrow),
        pltpu.VMEM((2,) + chunks, narrow),
        pltpu.VMEM(chunks, narrow),
        pltpu.VMEM((2,) + chunks, narrow),
        pltpu.VMEM((2, 2, channels, wide), narrow),
        pltpu.VMEM((2, 2, wide, channels), narrow),
        pltpu.VMEM((count, channels), single),
        pltpu.VMEM((count, 2 * wide), narrow),
        pltpu.VMEM((count, channels), narrow),
        pltpu.VMEM((count, channels), narrow),
        pltpu.VMEM((2, 4, rows, packed, 128), narrow),
        pltpu.VMEM((2, 4, rows, packed, 128), narrow),
        pltpu.VMEM((4,) + share.shape, single),
        pltpu.VMEM((2, 3, cells, ocean_channels), narrow),
        pltpu.VMEM((2, 2 * rows, 16, ocean_channels), narrow),
        pltpu.VMEM((2, 2, 3, 16, ocean_channels), narrow),
        pltpu.VMEM((8,) + mask.shape, single),
        pltpu.VMEM((rows, 8, 128), single),
        pltpu.VMEM((8, rows, 8, 128), single),
        pltpu.VMEM((2, 2 * rows + 6, cells + 16, 128), single),
        pltpu.VMEM((2 * rows, cells, ocean_channels), single),
        pltpu.VMEM((2 * cells, waves), narrow),
        pltpu.VMEM((4, rows, packed, 128), narrow),
        pltpu.VMEM((4, rows, packed, 128), narrow),
        dma(2, 4), dma(2, 4), dma(2, bands), dma(2, bands), dma(2, bands), dma(2, bands),
        dma(2, 4), dma(2, 4), dma(1), dma(1), dma(2, 4), dma(2, 4), dma(2, 2), dma(2, 2), dma(2, 2),
        dma(4), dma(4), dma(8), dma(8), dma(8), dma(8), dma(8), dma(8), dma(4), dma(4),
    ]
    atmosphere_next, ocean_next, surface = pl.pallas_call(
        functools.partial(step_kernel, bands),
        out_shape=(
            jax.ShapeDtypeStruct(atmosphere.shape, narrow),
            jax.ShapeDtypeStruct(ocean_state.shape, narrow),
            jax.ShapeDtypeStruct((2 * rows, 8, cells), single),
        ),
        in_specs=specs,
        out_specs=(inside,) * 3,
        scratch_shapes=scratch,
        compiler_params=pltpu.CompilerParams(
            collective_id=0, has_side_effects=True, vmem_limit_bytes=63 << 20
        ),
    )(*arguments)
    return (atmosphere_next, ocean_next, surface[:, :4].transpose(0, 2, 1))


def solution(mesh):
    placed = (
        P("band", None, ("comp", "tile")),
        P(None, None, None, ("comp", "tile"), None),
        P(None, None, None, ("comp", "tile")),
        P(),
        P(),
        P(None, None, ("comp", "tile")),
        P(None, ("comp", "tile"), None),
        P(("comp", "tile"), None),
        P(),
        P("band", ("comp", "tile"), None),
        P("band", ("comp", "tile")),
        P(),
        P(),
        P(),
        P(),
        P(),
        P(),
        P(),
        P(None, ("comp", "tile")),
    )
    return jax.shard_map(
        on_device,
        mesh=mesh,
        in_specs=placed,
        out_specs=(
            P("band", None, ("comp", "tile")),
            P("band", ("comp", "tile"), None),
            P("band", ("comp", "tile"), None),
        ),
        check_vma=False,
    )
```

```python
import functools
import math

import jax
import jax.numpy as jnp
import numpy as np
from jax import lax
from jax.experimental import pallas as pl
from jax.experimental.pallas import tpu as pltpu
from jax.sharding import PartitionSpec as P

MESH = pl.DeviceIdType.MESH
full_precision = lax.Precision.HIGHEST
eps_norm = 1e-06
shrink_level = 0.01


def layer_norm(values, scaling, offset):
    average = jnp.mean(values, axis=-1, keepdims=True)
    squares = jnp.mean(values * values, axis=-1, keepdims=True)
    variance = squares - average * average
    return (values - average) * lax.rsqrt(variance + eps_norm) * scaling + offset


def soft_shrink(values):
    zeros = jnp.zeros_like(values)
    return jnp.where(
        values > shrink_level,
        values - shrink_level,
        jnp.where(values < -shrink_level, values + shrink_level, zeros),
    )


def split_bf16(array):
    high = array.astype(jnp.bfloat16)
    return high, (array - high.astype(jnp.float32)).astype(jnp.bfloat16)


def transforms(latitudes, longitudes, bands):
    kept = longitudes // 2
    each, rows = kept // bands, latitudes // bands
    waves = np.arange(kept).reshape(bands, each).T.reshape(-1)
    lats = np.arange(latitudes).reshape(bands, rows).T.reshape(-1)
    lon = np.outer(waves, np.arange(longitudes)) % longitudes * (2.0 * math.pi / longitudes)
    lat = np.outer(np.arange(latitudes), lats) % latitudes * (2.0 * math.pi / latitudes)
    forward = np.concatenate([np.cos(lon), -np.sin(lon)], 0) / math.sqrt(longitudes)
    across = np.stack([np.cos(lat), np.sin(lat)], 0) / math.sqrt(latitudes)
    weight = np.where(waves == 0, 1.0, 2.0)[:, None]
    inverse = np.concatenate([np.cos(lon) * weight, -np.sin(lon) * weight], 0).T
    mats = (
        forward,
        across.reshape(2 * latitudes, latitudes),
        across.transpose(0, 2, 1).reshape(2 * latitudes, latitudes),
        inverse / math.sqrt(longitudes),
    )
    return [jnp.asarray(m, jnp.bfloat16) for m in mats]


def times(left, right):
    return jnp.dot(
        left.astype(jnp.bfloat16), right.astype(jnp.bfloat16), preferred_element_type=jnp.float32
    )


def product(left, right):
    total = None
    for a, b in ((0, 0), (1, 0), (0, 1)):
        if a < len(left) and b < len(right):
            term = jnp.dot(left[a], right[b], preferred_element_type=jnp.float32)
            total = term if total is None else total + term
    return total


directions = [(b, c) for b in (-1, 0, 1) for c in (-1, 0, 1) if (b, c) != (0, 0)]


def ocean_selectors(quarter):
    columns = np.arange(-8, 2 * quarter + 8)
    pick = np.zeros((len(columns), 384), np.float32)
    seen = np.zeros((len(columns), 512), np.float32)
    for i, column in enumerate(columns):
        if not -3 <= column < 2 * quarter + 3:
            continue
        token = column // 2
        side = 0 if token < 0 else 2 if token >= quarter else 1
        pick[i, side * 128 + token % quarter] = 1
        inner = column % (2 * quarter)
        seen[i, inner - 128 if column < 0 else 384 + inner if column >= 2 * quarter else 128 + inner] = 1
    split = np.zeros((2 * quarter, 2 * quarter), np.float32)
    for e in range(2):
        split[e * quarter + np.arange(quarter), 2 * np.arange(quarter) + e] = 1
    return (jnp.asarray(m, jnp.bfloat16) for m in (pick, seen, split))


def thirds(array):
    high = array.astype(jnp.bfloat16)
    rest = array - high.astype(jnp.float32)
    middle = rest.astype(jnp.bfloat16)
    return high, middle, (rest - middle.astype(jnp.float32)).astype(jnp.bfloat16)


def gelu(z):
    return 0.5 * z * (1.0 + lax.erf(z * math.sqrt(0.5)))


def step_kernel(bands, *refs):
    (
        x_ref, weight_ref, bias_ref, gain_ref, shift_ref, fc_in_ref, fc_out_ref, flux_head_ref,
        flux_embed_ref, ocean_ref, sea_ref, depth_ref, ocean_gain_ref, ocean_shift_ref,
        ocean_in_ref, ocean_out_ref, layer_ref, field_head_ref, patch_ref,
        forward_ref, across_ref, back_ref, inverse_ref, pick_ref, seen_ref, split_ref,
        atmosphere_ref, next_ref, surface_ref,
        normed, after, token, stage, landed, sums, all_sums, send_a, got_a, send_b, got_b,
        w_in, w_out, stream, hidden_ref, half_out, half_in, part_out, part_in, shared_ref,
        rows_in, cols_in, corner_in, masks_in, flux_ref, flux_in, tile_ref, conv_ref, wave_ref,
        middle_out, middle_in, order_ref, affine_ref, mix_ref, offset_ref, share_ref, mask_ref,
        level_ref, spread_ref, field_ref, total_ref,
        sent_sum, came_sum, sent_a, came_a, sent_b, came_b, sent_out, came_out,
        sent_half, came_half, sent_part, came_part, load, sent_load, came_load,
        sent_share, came_share, sent_cells, came_cells, sent_mask, came_mask, sent_flux, came_flux,
        sent_middle, came_middle,
    ) = refs
    rows, longitudes, slot = x_ref.shape
    quarter = longitudes // 4
    middle = quarter // 2
    latitudes = rows * bands
    each = longitudes // 2 // bands
    cells = ocean_ref.shape[1]
    me = lax.axis_index("band")
    comp, tile = lax.axis_index("comp"), lax.axis_index("tile")
    mine = comp * 2 + tile

    def member(step):
        return lax.rem(mine + step, 4)

    def team_id(index):
        return {"comp": lax.div(index, 2), "tile": lax.rem(index, 2)}

    def near_id(b, c):
        index = lax.rem(mine + c + 4, 4)
        return {"band": lax.rem(me + b + bands, bands), **team_id(index)}

    own_loads = [
        pltpu.make_async_copy(source.at[block], target.at[block, 0], load.at[block, i])
        for block in range(2)
        for i, (source, target) in enumerate(((fc_in_ref, w_in), (fc_out_ref, w_out)))
    ]
    sibling_loads = [
        pltpu.make_async_remote_copy(
            src_ref=source.at[block],
            dst_ref=target.at[block, 1],
            send_sem=sent_load.at[block, i],
            recv_sem=came_load.at[block, i],
            device_id={"tile": 1 - tile},
            device_id_type=MESH,
        )
        for block in range(2)
        for i, (source, target) in enumerate(((fc_in_ref, w_in), (fc_out_ref, w_out)))
    ]
    barrier = pltpu.get_barrier_semaphore()

    def greet(step, carry):
        pl.semaphore_signal(
            barrier, inc=1, device_id={"band": lax.rem(me + step, bands)}, device_id_type=MESH
        )
        return carry

    for step in range(1, 4):
        pl.semaphore_signal(barrier, inc=1, device_id=team_id(member(step)), device_id_type=MESH)
    for b, c in directions:
        if b and c:
            pl.semaphore_signal(barrier, inc=1, device_id=near_id(b, c), device_id_type=MESH)
    lax.fori_loop(1, bands, greet, 0)
    for copy in own_loads:
        copy.start()

    def near_copies(source_of, target_of, sent, came):
        copies = []
        for d, (b, c) in enumerate(directions):
            copies.append(
                pltpu.make_async_remote_copy(
                    src_ref=source_of(b, c),
                    dst_ref=target_of(-b, -c),
                    send_sem=sent.at[d],
                    recv_sem=came.at[directions.index((-b, -c))],
                    device_id=near_id(b, c),
                    device_id_type=MESH,
                )
            )
        return copies

    def near_landings(source_of, target_of, sent, came):
        copies = []
        for d, (b, c) in enumerate(directions):
            copies.append(
                pltpu.make_async_remote_copy(
                    src_ref=source_of(b, c),
                    dst_ref=target_of(b, c),
                    send_sem=sent.at[d],
                    recv_sem=came.at[d],
                    device_id=near_id(b, c),
                    device_id_type=MESH,
                )
            )
        return copies

    def cells_from(b, c):
        row = pl.ds(0, 2 * rows) if b == 0 else pl.ds(2 * rows - 3 if b > 0 else 0, 3)
        column = pl.ds(0, cells) if c == 0 else pl.ds(cells - 16 if c > 0 else 0, 16)
        return ocean_ref.at[row, column]

    def cells_to(b, c):
        if c == 0:
            return rows_in.at[0 if b < 0 else 1]
        if b == 0:
            return cols_in.at[0 if c < 0 else 1]
        return corner_in.at[0 if b < 0 else 1, 0 if c < 0 else 1]

    cell_args = (cells_from, cells_to, sent_cells, came_cells)
    mask_args = (
        lambda b, c: mask_ref, lambda b, c: masks_in.at[directions.index((b, c))], sent_mask, came_mask
    )
    flux_args = (
        lambda b, c: flux_ref, lambda b, c: flux_in.at[directions.index((b, c))], sent_flux, came_flux
    )

    def team_copy(source, target, sent, came, step, pick, landing):
        index = member(step)
        chosen = {"whole": lambda: source, "half": lambda: source.at[lax.rem(index, 2)],
                  "each": lambda: source.at[index]}[pick]()
        place = index if landing else mine
        return pltpu.make_async_remote_copy(
            src_ref=chosen,
            dst_ref=target.at[place],
            send_sem=sent.at[index],
            recv_sem=came.at[place],
            device_id=team_id(index),
            device_id_type=MESH,
        )

    def team_exchange(source, target, sent, came, pick):
        for step in range(1, 4):
            team_copy(source, target, sent, came, step, pick, False).start()

    def team_finish(source, target, sent, came, pick):
        for step in range(1, 4):
            team_copy(source, target, sent, came, step, pick, True).wait()

    def band_copy(source, target, sent, came, step, landing):
        index = lax.rem(me + step, bands)
        return pltpu.make_async_remote_copy(
            src_ref=source.at[index],
            dst_ref=target.at[index if landing else me],
            send_sem=sent.at[index],
            recv_sem=came.at[index if landing else me],
            device_id={"band": index},
            device_id_type=MESH,
        )

    def band_exchange(source, target, sent, came):
        source[...] = stage[...].astype(jnp.bfloat16).reshape(source.shape)

        def go(step, carry):
            band_copy(source, target, sent, came, step, False).start()
            return carry

        lax.fori_loop(1, bands, go, 0)
        target[me] = source[me]

        def come(step, carry):
            band_copy(source, target, sent, came, step, True).wait()
            return carry

        lax.fori_loop(1, bands, come, 0)
        landed[...] = target[...].astype(jnp.float32).reshape(landed.shape)

    lane = lax.broadcasted_iota(jnp.int32, (1, 128), 1)
    first_half = lane < slot - 128
    sign = jnp.where(first_half, 1.0, -1.0)
    half = longitudes // 2
    counted = jnp.where(lax.broadcasted_iota(jnp.int32, (8, 256), 1) < slot, 1.0, 0.0)
    counted = counted.astype(jnp.bfloat16)
    which = lax.broadcasted_iota(jnp.int32, (8, longitudes), 0)
    turned = (((1,), (1,)), ((), ()))

    def across_rows(left, right):
        return lax.dot_general(left, right, turned, preferred_element_type=jnp.float32)

    def swap(values):
        return pltpu.roll(values, 64, 1)

    def doubled(tails):
        top = jnp.where(first_half, tails, swap(tails))
        low = jnp.where(first_half, swap(tails), tails)
        return jnp.concatenate([top, low], axis=0)

    def tokens(block, lat):
        if block == 0:
            values = x_ref[lat].astype(jnp.float32)
            return jnp.concatenate([values, values[:, 128:]], axis=1)
        pieces = [middle_in[s, lat].astype(jnp.float32) for s in range(4)]
        return jnp.concatenate(
            [jnp.concatenate([p[:quarter], doubled(p[quarter:])], axis=1) for p in pieces], axis=0
        )

    def spread(lat, wave, part, values):
        stage[pl.ds(part * 9 + lat * 3 + wave, bands, stride=32), :] = values

    def collect(lat, wave, part):
        return landed[pl.ds(part * 9 + lat * 3 + wave, bands, stride=32), :]

    def spectral_filter(block):
        total = jnp.zeros((8, longitudes), jnp.float32)
        for lat in range(rows):
            values = tokens(block, lat)
            high, low = split_bf16(values * values)
            total = total + jnp.where(
                which == lat, across_rows(counted, values.astype(jnp.bfloat16)), 0.0
            )
            total = total + jnp.where(
                which == rows + lat, across_rows(counted, high) + across_rows(counted, low), 0.0
            )
        sums[...] = total
        if block == 0:
            pl.semaphore_wait(barrier, bands - 1 + 3 + 4)
        team_exchange(sums, all_sums.at[block], sent_sum.at[block], came_sum.at[block], "whole")
        if block == 0:
            for copy in near_copies(*mask_args) + near_copies(*cell_args) + sibling_loads:
                copy.start()
            team_exchange(share_ref, shared_ref, sent_share, came_share, "whole")
            shared_ref[mine] = share_ref[...]
        all_sums[block, mine] = total
        team_finish(sums, all_sums.at[block], sent_sum.at[block], came_sum.at[block], "whole")
        total = (
            all_sums[block, 0] + all_sums[block, 1] + all_sums[block, 2] + all_sums[block, 3]
        ) * (1.0 / (4 * slot))
        columns = jnp.concatenate([total, jnp.zeros((120, longitudes), jnp.float32)], axis=0).T
        for lat in range(rows):
            average = columns[:, lat : lat + 1]
            power = columns[:, rows + lat : rows + lat + 1]
            scaled = tokens(block, lat) - average
            scaled = scaled * lax.rsqrt(power - average * average + eps_norm)
            scaled = scaled * affine_ref[block, 0:1, :] + affine_ref[block, 2:3, :]
            normed[lat] = scaled
            spectrum = times(forward_ref[...], scaled)
            upper, lower = spectrum[:half], spectrum[half:]
            rest = jnp.where(first_half, upper[:, 128:], lower[:, 128:])
            parts = (upper[:, :128], lower[:, :128], rest)
            for part in range(3):
                for wave in range(each):
                    spread(lat, wave, part, parts[part][wave * bands : (wave + 1) * bands])
        band_exchange(send_a, got_a.at[block], sent_a.at[block], came_a.at[block])
        pieces = []
        for wave in range(each):
            for part in range(3):
                pieces.append(
                    jnp.concatenate([collect(lat, wave, part) for lat in range(rows)], axis=0)
                )
        spectrum = jnp.concatenate(pieces, axis=1).astype(jnp.bfloat16)
        turned_all = times(across_ref[...], spectrum)

        def combine(both, wave, direction):
            base = wave * 384
            cosine, sine = both[:latitudes, base : base + 384], both[latitudes:, base : base + 384]
            real = cosine[:, :128] + direction * sine[:, 128:256]
            imag = cosine[:, 128:256] - direction * sine[:, :128]
            rest = cosine[:, 256:] + (direction * sign) * swap(sine[:, 256:])
            return real, imag, rest

        rows_mixed = jnp.concatenate(
            [jnp.concatenate(combine(turned_all, wave, 1.0), axis=1) for wave in range(each)], axis=0
        )
        hidden = times(rows_mixed, mix_ref[block, 0])
        hidden = jnp.maximum(hidden + offset_ref[block, 0:1, :], 0.0)
        mixed = times(hidden, mix_ref[block, 1])
        mixed = soft_shrink(mixed + offset_ref[block, 1:2, :])
        mixed = jnp.concatenate(
            [mixed[wave * latitudes : (wave + 1) * latitudes] for wave in range(each)], axis=1
        )
        turned_back = times(back_ref[...], mixed)
        for wave in range(each):
            parts = combine(turned_back, wave, -1.0)
            for part in range(3):
                for lat in range(rows):
                    spread(lat, wave, part, parts[part][lat * bands : (lat + 1) * bands])
        band_exchange(send_b, got_b.at[block], sent_b.at[block], came_b.at[block])
        for lat in range(rows):
            real, imag, rest = (
                jnp.concatenate([collect(lat, wave, part) for wave in range(each)], axis=0)
                for part in range(3)
            )
            right = jnp.concatenate(
                [
                    jnp.concatenate([real, rest], axis=1),
                    jnp.concatenate([imag, swap(rest)], axis=1),
                ],
                axis=0,
            ).astype(jnp.bfloat16)
            restored = times(inverse_ref[...], right)
            result = tokens(block, lat) + restored + normed[lat]
            for s in range(4):
                piece = result[s * quarter : (s + 1) * quarter]
                tail = piece[:, 128:]
                tail = jnp.where(first_half, tail[:middle], swap(tail[middle:]))
                after[s % 2, s // 2, lat, :quarter] = piece[:, :128].astype(jnp.bfloat16)
                after[s % 2, s // 2, lat, quarter:] = tail.astype(jnp.bfloat16)
        args = (after, token.at[block], sent_out.at[block], came_out.at[block], "half")
        team_exchange(*args)
        token[block, mine] = after[tile]
        team_finish(*args)
        for i in range(2):
            own_loads[2 * block + i].wait()
            sibling_loads[2 * block + i].wait()

    def pair(left, right):
        return jnp.concatenate(
            [jnp.where(first_half, left, swap(right)), jnp.where(first_half, swap(left), right)], 0
        )

    def unpair(both):
        top, low = both[:middle], both[middle:]
        return jnp.where(first_half, top, swap(low)), jnp.where(first_half, swap(top), low)

    def pack(block_rows, target):
        tails = unpair(block_rows[:, 512:640]) + unpair(block_rows[:, 640:])
        for s in range(4):
            place = target(s)
            place[:quarter] = block_rows[:, s * 128 : (s + 1) * 128].astype(jnp.bfloat16)
            place[quarter:] = tails[s].astype(jnp.bfloat16)

    def lanes_of(slices):
        heads = [p[:quarter] for p in slices]
        tails = [p[quarter:] for p in slices]
        return jnp.concatenate(heads + [pair(*tails[:2]), pair(*tails[2:])], axis=1)

    def reorder(values):
        t = [values[:, i * 128 : (i + 1) * 128] for i in range(6)]

        def inner(a, b):
            return jnp.where(first_half, swap(a), swap(b)), jnp.where(first_half, a, b)

        one, tails_a = inner(t[1], t[2])
        three, tails_b = inner(t[4], t[5])
        return jnp.concatenate([t[0], one, t[3], three, tails_a, tails_b], axis=1)

    row_spans = [(s * slot, 128) for s in range(4)] + [(s * slot + 128, slot - 128) for s in range(4)]

    def mlp(block, which_quarter):
        for lat in range(rows):
            slices = [token[block, s, which_quarter, lat].astype(jnp.float32) for s in range(4)]
            stream[lat * quarter : (lat + 1) * quarter] = lanes_of(slices)
        values = stream[...]
        normal = layer_norm(values, order_ref[block, 1:2, :], order_ref[block, 3:4, :])
        normal = normal.astype(jnp.bfloat16)
        wide = w_in.shape[3]
        for part in range(2):

            def piece(i, carry):
                at = pl.multiple_of(i * 256, 256)
                weight = jnp.concatenate(
                    [w_in[block, part, pl.ds(a, n), pl.ds(at, 256)] for a, n in row_spans], axis=0
                )
                z = jnp.dot(normal, weight, preferred_element_type=jnp.float32)
                hidden_ref[:, pl.ds(part * wide + at, 256)] = gelu(z).astype(jnp.bfloat16)
                return carry

            lax.fori_loop(0, wide // 256, piece, 0)
        total = jnp.dot(hidden_ref[:, :wide], w_out[block, 0], preferred_element_type=jnp.float32)
        total = total + jnp.dot(
            hidden_ref[:, wide:], w_out[block, 1], preferred_element_type=jnp.float32
        )
        total_ref[...] = reorder(total)

    zeros = functools.partial(jnp.zeros, dtype=jnp.float32)
    for block in range(2):
        both = jnp.concatenate([gain_ref[block], shift_ref[block], zeros((4, 4 * slot))], axis=0)
        order_ref[block] = reorder(both)
        head = order_ref[block, :, pl.ds(pl.multiple_of(mine * 128, 128), 128)]
        tail = order_ref[block, :, pl.ds(pl.multiple_of(512 + comp * 128, 128), 128)]
        tail = jnp.where(tile == 0, tail, swap(tail))
        tail = jnp.where(first_half, tail, swap(tail))
        affine_ref[block] = jnp.concatenate([head, tail], axis=1)
        for sublayer in range(2):

            def placed(weight):
                width = weight.shape[1]
                wide = jnp.concatenate([weight, zeros((slot, 128 - width))], axis=1)
                moved = pltpu.roll(wide[width:], width, 1)
                low = jnp.where(lane >= width, moved, 0.0)
                high = jnp.where(first_half, moved, 0.0)
                return (
                    jnp.concatenate([wide[:width], low], axis=0),
                    jnp.concatenate([zeros((width, 128)), high], axis=0),
                )

            real, real_tail = placed(weight_ref[block, sublayer, 0])
            imag, imag_tail = placed(weight_ref[block, sublayer, 1])
            upper = jnp.concatenate([real, imag, real_tail + swap(imag_tail)], axis=1)
            lower = jnp.concatenate([-imag, real, swap(real_tail) - imag_tail], axis=1)
            mix_ref[block, sublayer] = jnp.concatenate(
                [upper[:128], lower[:128], upper[128:], lower[128:]], axis=0
            ).astype(jnp.bfloat16)
            bias = bias_ref[block, sublayer]
            tail = jnp.concatenate([bias[:, 128:], bias[:, 128:]], axis=1)
            offset_ref[block, sublayer : sublayer + 1, :] = jnp.concatenate(
                [bias[0:1, :128], bias[1:2, :128], jnp.where(first_half, tail[0:1], tail[1:2])], axis=1
            )
    share_ref[...] = zeros(share_ref.shape)
    heads = jnp.concatenate([flux_head_ref[...].astype(jnp.float32), zeros((slot, 120))], axis=1)
    heads = jnp.concatenate([heads, zeros((256 - slot, 128))], axis=0).T
    share_ref[0:8, :] = heads[:8]
    for f in range(4):
        for a in range(2):
            for e in range(2):
                at, row = 8 + e * 16 + a * 8 + f, f * 4 + a * 2 + e
                share_ref[at : at + 1, :slot] = patch_ref[row : row + 1, :]
    mask_ref[...] = zeros(mask_ref.shape)
    mask_ref[: 2 * rows, :cells] = sea_ref[...].astype(jnp.float32)
    level_ref[...] = zeros(level_ref.shape)
    for level in range(rows + 4):
        level_ref[level * 8 : level * 8 + 8, level * 256 : (level + 1) * 256] = flux_embed_ref[...]
    spread_ref[0], spread_ref[1] = split_bf16(level_ref[...])
    fields = jnp.concatenate([field_head_ref[...], zeros((256, 124))], axis=1).T
    field_ref[...] = jnp.concatenate(thirds(fields[:8]), axis=0)

    spectral_filter(0)
    team_finish(share_ref, shared_ref, sent_share, came_share, "whole")
    copy = pltpu.make_async_remote_copy(
        src_ref=half_out,
        dst_ref=half_in,
        send_sem=sent_half.at[0],
        recv_sem=came_half.at[0],
        device_id={"comp": 1 - comp},
        device_id_type=MESH,
    )

    def halves(i, carry):
        mlp(0, lax.rem(1 - comp + i, 2))

        @pl.when(i == 0)
        def _():
            half_out[...] = total_ref[...].astype(jnp.bfloat16)
            copy.start()

        return carry

    lax.fori_loop(0, 2, halves, 0)
    copy.wait()
    first = stream[...] + total_ref[...] + half_in[...].astype(jnp.float32)
    first = first.astype(jnp.bfloat16)
    stream[...] = first.astype(jnp.float32)

    small = [shared_ref[s] for s in range(4)]
    tails = [s[:, 128:] for s in small]
    whole = jnp.concatenate(
        [s[:, :128] for s in small]
        + [jnp.where(first_half, tails[i], swap(tails[i + 1])) for i in (0, 2)],
        axis=1,
    )
    head, embed = whole[:8].astype(jnp.bfloat16), whole[8:]
    for lat in range(rows):
        flux = across_rows(head, first[lat * quarter : (lat + 1) * quarter])
        flux_ref[lat] = jnp.concatenate([flux, jnp.zeros((8, 128 - quarter), jnp.float32)], axis=1)
    for copy in near_copies(*flux_args):
        copy.start()
    for copy in near_landings(*mask_args) + near_landings(*cell_args) + near_landings(*flux_args):
        copy.wait()

    def flux_at(lat, c):
        b = -1 if lat < 0 else 1 if lat >= rows else 0
        if (b, c) == (0, 0):
            return flux_ref[lat]
        return flux_in[directions.index((b, c)), lat % rows]

    ext_lats = range(-2, rows + 2)
    laid = jnp.concatenate(
        [jnp.concatenate([flux_at(lat, c) for c in (-1, 0, 1)], axis=1) for lat in ext_lats]
        + [jnp.zeros((128 - 8 * len(ext_lats), 384), jnp.float32)],
        axis=0,
    )
    raised = across_rows(pick_ref[...], jnp.concatenate(thirds(laid), axis=0))
    raised = raised[:, :128] + raised[:, 128:256] + raised[:, 256:]
    forcing = product(split_bf16(raised), (spread_ref[0], spread_ref[1]))

    def mask_rows(b, c):
        whole = mask_ref[...] if (b, c) == (0, 0) else masks_in[directions.index((b, c))]
        whole = whole[:, 128:] if c < 0 else whole[:, :128] if c > 0 else whole
        return whole[2 * rows - 3 : 2 * rows] if b < 0 else whole[:3] if b > 0 else whole[: 2 * rows]

    ext_rows = 2 * rows + 6
    masks = jnp.concatenate(
        [jnp.concatenate([mask_rows(b, c) for c in (-1, 0, 1)], axis=1) for b in (-1, 0, 1)]
        + [jnp.zeros((16 - ext_rows, 512), jnp.float32)],
        axis=0,
    )
    masks = across_rows(seen_ref[...], masks.astype(jnp.bfloat16))
    for row in range(ext_rows):
        b = -1 if row < 3 else 1 if row >= 2 * rows + 3 else 0
        at = row if b < 0 else row - 3 if b == 0 else row - 2 * rows - 3
        sources = (
            cols_in[0, at] if b == 0 else corner_in[0 if b < 0 else 1, 0, at],
            ocean_ref[at] if b == 0 else rows_in[0 if b < 0 else 1, at],
            cols_in[1, at] if b == 0 else corner_in[0 if b < 0 else 1, 1, at],
        )
        sources = [s.astype(jnp.float32) for s in sources]
        state = jnp.concatenate([sources[0][8:], sources[1], sources[2][:8]], axis=0)
        level = (row - 3) // 2 + 2
        start = state + masks[:, row : row + 1] * forcing[:, level * 256 : (level + 1) * 256]
        start = start.astype(jnp.bfloat16).astype(jnp.float32)
        if b:
            inside = jnp.where(me > 0, 1.0, 0.0) if b < 0 else jnp.where(me < bands - 1, 1.0, 0.0)
            start = start * inside
        for part in range(2):
            tile_ref[part, row] = start[:, part * 128 : (part + 1) * 128]

    for part in range(2):
        span = slice(part * 128, (part + 1) * 128)

        def strip(i, carry):
            at = pl.multiple_of(i * 16, 16)
            totals = [jnp.zeros((16, 128), jnp.float32) for _ in range(2 * rows)]
            for e in range(7):
                for row in range(ext_rows):
                    values = tile_ref[part, row, pl.ds(at + 5 + e, 16), :]
                    for a in range(7):
                        if 0 <= row - a < 2 * rows:
                            tap = depth_ref[a, e : e + 1, span]
                            totals[row - a] = totals[row - a] + values * tap
            for row in range(2 * rows):
                conv_ref[row, pl.ds(at, 16), span] = totals[row]
            return carry

        lax.fori_loop(0, cells // 16, strip, 0)

    own_columns = jnp.concatenate([mask_ref[...], jnp.zeros((120, 256), jnp.float32)], axis=0).T
    for start_row in range(0, 2 * rows, 2):
        values = conv_ref[start_row : start_row + 2].reshape(2 * cells, 256)
        normal = layer_norm(values, ocean_gain_ref[...], ocean_shift_ref[...])
        normal = normal.astype(jnp.bfloat16)

        def piece(i, carry):
            at = pl.multiple_of(i * 256, 256)
            z = jnp.dot(normal, ocean_in_ref[:, pl.ds(at, 256)], preferred_element_type=jnp.float32)
            wave_ref[:, pl.ds(at, 256)] = gelu(z).astype(jnp.bfloat16)
            return carry

        lax.fori_loop(0, ocean_in_ref.shape[1] // 256, piece, 0)
        update = jnp.dot(wave_ref[...], ocean_out_ref[...], preferred_element_type=jnp.float32)
        update = update * layer_ref[...]
        for row in range(start_row, start_row + 2):
            begin = jnp.concatenate([tile_ref[part, row + 3, 8 : 8 + cells] for part in range(2)], axis=1)
            change = update[(row - start_row) * cells : (row - start_row + 1) * cells]
            fresh = (begin + own_columns[:cells, row : row + 1] * change).astype(jnp.bfloat16)
            next_ref[row] = fresh
            field = across_rows(field_ref[...], fresh)
            field = (field[:8] + field[8:16] + field[16:24]) * mask_ref[row : row + 1, :cells]
            surface_ref[row] = field

    for lat in range(rows):
        both = jnp.concatenate([surface_ref[2 * lat], surface_ref[2 * lat + 1]], axis=0)
        patch = across_rows(split_ref[...], jnp.concatenate(thirds(both), axis=0))
        patch = patch[:, :16] + patch[:, 16:32] + patch[:, 32:48]
        total = stream[lat * quarter : (lat + 1) * quarter]
        for e in range(2):
            total = total + product(
                split_bf16(patch[e * quarter : (e + 1) * quarter]),
                split_bf16(embed[e * 16 : (e + 1) * 16]),
            )
        pack(total, lambda s, lat=lat: middle_out.at[s, lat])
    args = (middle_out, middle_in, sent_middle, came_middle, "each")
    team_exchange(*args)
    middle_in[mine] = middle_out[mine]
    team_finish(*args)

    spectral_filter(1)

    def quarters(which_quarter, carry):
        mlp(1, which_quarter)
        for lat in range(rows):
            pack(
                total_ref[lat * quarter : (lat + 1) * quarter],
                lambda s, lat=lat: part_out.at[which_quarter, s, lat],
            )
        team_exchange(
            part_out.at[which_quarter], part_in.at[which_quarter],
            sent_part.at[which_quarter], came_part.at[which_quarter], "each",
        )
        part_in[which_quarter, mine] = part_out[which_quarter, mine]
        return carry

    lax.fori_loop(0, 2, quarters, 0)
    for which_quarter in range(2):
        team_finish(
            part_out.at[which_quarter], part_in.at[which_quarter],
            sent_part.at[which_quarter], came_part.at[which_quarter], "each",
        )
        for half_of in range(2):
            for lat in range(rows):
                piece = after[half_of, which_quarter, lat].astype(jnp.float32)
                piece = piece + part_in[which_quarter, half_of, lat].astype(jnp.float32)
                piece = piece + part_in[which_quarter, 2 + half_of, lat].astype(jnp.float32)
                tail = piece[quarter:]
                at = (2 * which_quarter + half_of) * quarter
                tail = jnp.concatenate([tail, swap(tail)], axis=0)
                atmosphere_ref[lat, at : at + quarter, :128] = piece[:quarter].astype(jnp.bfloat16)
                atmosphere_ref[lat, at : at + quarter, 128:] = tail[:, : slot - 128].astype(
                    jnp.bfloat16
                )


def on_device(
    atmosphere, spec_weight, spec_bias, norm_gain, norm_shift, fc_in, fc_out, flux_head, flux_embed,
    ocean_state, sea_mask, depth_kernel, ocean_gain, ocean_shift, ocean_in, ocean_out, layer_scale,
    field_head, patch_embed,
):
    bands = lax.axis_size("band")
    rows, longitudes, slot = atmosphere.shape
    quarter = longitudes // 4
    count = rows * quarter
    latitudes = rows * bands
    channels, wide = fc_in.shape[1:]
    packed = quarter * slot // 128
    cells, ocean_channels = ocean_state.shape[1:]
    waves = ocean_in.shape[1]

    inside, outside = pl.BlockSpec(memory_space=pltpu.VMEM), pl.BlockSpec(memory_space=pl.ANY)
    arguments = [
        atmosphere, spec_weight, spec_bias, norm_gain, norm_shift, fc_in, fc_out, flux_head,
        flux_embed, ocean_state, sea_mask, depth_kernel, ocean_gain[None], ocean_shift[None],
        ocean_in, ocean_out, layer_scale[None], field_head, patch_embed,
        *transforms(latitudes, longitudes, bands), *ocean_selectors(quarter),
    ]
    specs = [inside] * 5 + [outside] * 2 + [inside] * (len(arguments) - 7)
    levels = (rows + 4) * ocean_channels
    narrow, single = jnp.bfloat16, jnp.float32

    def dma(*shape):
        return pltpu.SemaphoreType.DMA(shape)

    chunks = (bands, 32, 128)
    scratch = [
        pltpu.VMEM((rows, longitudes, 256), single),
        pltpu.VMEM((2, 2, rows, packed, 128), narrow),
        pltpu.VMEM((2, 4, 2, rows, packed, 128), narrow),
        pltpu.VMEM((bands * 32, 128), single),
        pltpu.VMEM((bands * 32, 128), single),
        pltpu.VMEM((8, longitudes), single),
        pltpu.VMEM((2, 4, 8, longitudes), single),
        pltpu.VMEM(chunks, narrow),
        pltpu.VMEM((2,) + chunks, narrow),
        pltpu.VMEM(chunks, narrow),
        pltpu.VMEM((2,) + chunks, narrow),
        pltpu.VMEM((2, 2, channels, wide), narrow),
        pltpu.VMEM((2, 2, wide, channels), narrow),
        pltpu.VMEM((count, channels), single),
        pltpu.VMEM((count, 2 * wide), narrow),
        pltpu.VMEM((count, channels), narrow),
        pltpu.VMEM((count, channels), narrow),
        pltpu.VMEM((2, 4, rows, packed, 128), narrow),
        pltpu.VMEM((2, 4, rows, packed, 128), narrow),
        pltpu.VMEM((4, 40, 256), single),
        pltpu.VMEM((2, 3, cells, ocean_channels), narrow),
        pltpu.VMEM((2, 2 * rows, 16, ocean_channels), narrow),
        pltpu.VMEM((2, 2, 3, 16, ocean_channels), narrow),
        pltpu.VMEM((8, 8, 256), single),
        pltpu.VMEM((rows, 8, 128), single),
        pltpu.VMEM((8, rows, 8, 128), single),
        pltpu.VMEM((2, 2 * rows + 6, cells + 16, 128), single),
        pltpu.VMEM((2 * rows, cells, ocean_channels), single),
        pltpu.VMEM((2 * cells, waves), narrow),
        pltpu.VMEM((4, rows, packed, 128), narrow),
        pltpu.VMEM((4, rows, packed, 128), narrow),
        pltpu.VMEM((2, 8, channels), single),
        pltpu.VMEM((2, 8, 256), single),
        pltpu.VMEM((2, 2, 2 * slot, 2 * slot), narrow),
        pltpu.VMEM((2, 8, 2 * slot), single),
        pltpu.VMEM((40, 256), single),
        pltpu.VMEM((8, 256), single),
        pltpu.VMEM((128, levels), single),
        pltpu.VMEM((2, 128, levels), narrow),
        pltpu.VMEM((24, ocean_channels), narrow),
        pltpu.VMEM((count, channels), single),
        dma(2, 4), dma(2, 4), dma(2, bands), dma(2, bands), dma(2, bands), dma(2, bands),
        dma(2, 4), dma(2, 4), dma(1), dma(1), dma(2, 4), dma(2, 4), dma(2, 2), dma(2, 2), dma(2, 2),
        dma(4), dma(4), dma(8), dma(8), dma(8), dma(8), dma(8), dma(8), dma(4), dma(4),
    ]
    atmosphere_next, ocean_next, surface = pl.pallas_call(
        functools.partial(step_kernel, bands),
        out_shape=(
            jax.ShapeDtypeStruct(atmosphere.shape, narrow),
            jax.ShapeDtypeStruct(ocean_state.shape, narrow),
            jax.ShapeDtypeStruct((2 * rows, 8, cells), single),
        ),
        in_specs=specs,
        out_specs=(inside,) * 3,
        scratch_shapes=scratch,
        compiler_params=pltpu.CompilerParams(
            collective_id=0, has_side_effects=True, vmem_limit_bytes=63 << 20
        ),
    )(*arguments)
    return (atmosphere_next, ocean_next, surface[:, :4].transpose(0, 2, 1))


def solution(mesh):
    placed = (
        P("band", None, ("comp", "tile")),
        P(None, None, None, ("comp", "tile"), None),
        P(None, None, None, ("comp", "tile")),
        P(),
        P(),
        P(None, None, ("comp", "tile")),
        P(None, ("comp", "tile"), None),
        P(("comp", "tile"), None),
        P(),
        P("band", ("comp", "tile"), None),
        P("band", ("comp", "tile")),
        P(),
        P(),
        P(),
        P(),
        P(),
        P(),
        P(),
        P(None, ("comp", "tile")),
    )
    return jax.shard_map(
        on_device,
        mesh=mesh,
        in_specs=placed,
        out_specs=(
            P("band", None, ("comp", "tile")),
            P("band", ("comp", "tile"), None),
            P("band", ("comp", "tile"), None),
        ),
        check_vma=False,
    )
```

```python
import functools
import math

import jax
import jax.numpy as jnp
import numpy as np
from jax import lax
from jax.experimental import pallas as pl
from jax.experimental.pallas import tpu as pltpu
from jax.sharding import PartitionSpec as P

MESH = pl.DeviceIdType.MESH
full_precision = lax.Precision.HIGHEST
eps_norm = 1e-06
shrink_level = 0.01


def layer_norm(values, scaling, offset):
    average = jnp.mean(values, axis=-1, keepdims=True)
    squares = jnp.mean(values * values, axis=-1, keepdims=True)
    variance = squares - average * average
    return (values - average) * lax.rsqrt(variance + eps_norm) * scaling + offset


def soft_shrink(values):
    zeros = jnp.zeros_like(values)
    return jnp.where(
        values > shrink_level,
        values - shrink_level,
        jnp.where(values < -shrink_level, values + shrink_level, zeros),
    )


def split_bf16(array):
    high = array.astype(jnp.bfloat16)
    return high, (array - high.astype(jnp.float32)).astype(jnp.bfloat16)


def transforms(latitudes, longitudes, bands):
    kept = longitudes // 2
    each, rows = kept // bands, latitudes // bands
    waves = np.arange(kept).reshape(bands, each).T.reshape(-1)
    lats = np.arange(latitudes).reshape(bands, rows).T.reshape(-1)
    lon = np.outer(waves, np.arange(longitudes)) % longitudes * (2.0 * math.pi / longitudes)
    lat = np.outer(np.arange(latitudes), lats) % latitudes * (2.0 * math.pi / latitudes)
    forward = np.concatenate([np.cos(lon), -np.sin(lon)], 0) / math.sqrt(longitudes)
    across = np.stack([np.cos(lat), np.sin(lat)], 0) / math.sqrt(latitudes)
    weight = np.where(waves == 0, 1.0, 2.0)[:, None]
    inverse = np.concatenate([np.cos(lon) * weight, -np.sin(lon) * weight], 0).T
    mats = (
        forward,
        across.reshape(2 * latitudes, latitudes),
        across.transpose(0, 2, 1).reshape(2 * latitudes, latitudes),
        inverse / math.sqrt(longitudes),
    )
    return [jnp.asarray(m, jnp.bfloat16) for m in mats]


def times(left, right):
    return jnp.dot(
        left.astype(jnp.bfloat16), right.astype(jnp.bfloat16), preferred_element_type=jnp.float32
    )


def product(left, right):
    total = None
    for a, b in ((0, 0), (1, 0), (0, 1)):
        if a < len(left) and b < len(right):
            term = jnp.dot(left[a], right[b], preferred_element_type=jnp.float32)
            total = term if total is None else total + term
    return total


directions = [(b, c) for b in (-1, 0, 1) for c in (-1, 0, 1) if (b, c) != (0, 0)]


def ocean_selectors(quarter):
    columns = np.arange(-8, 2 * quarter + 8)
    pick = np.zeros((len(columns), 384), np.float32)
    seen = np.zeros((len(columns), 512), np.float32)
    for i, column in enumerate(columns):
        if not -3 <= column < 2 * quarter + 3:
            continue
        token = column // 2
        side = 0 if token < 0 else 2 if token >= quarter else 1
        pick[i, side * 128 + token % quarter] = 1
        inner = column % (2 * quarter)
        seen[i, inner - 128 if column < 0 else 384 + inner if column >= 2 * quarter else 128 + inner] = 1
    split = np.zeros((2 * quarter, 2 * quarter), np.float32)
    for e in range(2):
        split[e * quarter + np.arange(quarter), 2 * np.arange(quarter) + e] = 1
    return (jnp.asarray(m, jnp.bfloat16) for m in (pick, seen, split))


def thirds(array):
    high = array.astype(jnp.bfloat16)
    rest = array - high.astype(jnp.float32)
    middle = rest.astype(jnp.bfloat16)
    return high, middle, (rest - middle.astype(jnp.float32)).astype(jnp.bfloat16)


def gelu(z):
    return 0.5 * z * (1.0 + lax.erf(z * math.sqrt(0.5)))


def step_kernel(bands, *refs):
    (
        x_ref, weight_ref, bias_ref, gain_ref, shift_ref, fc_in_ref, fc_out_ref, flux_head_ref,
        flux_embed_ref, ocean_ref, sea_ref, depth_ref, ocean_gain_ref, ocean_shift_ref,
        ocean_in_ref, ocean_out_ref, layer_ref, field_head_ref, patch_ref,
        forward_ref, across_ref, back_ref, inverse_ref, pick_ref, seen_ref, split_ref,
        atmosphere_ref, next_ref, surface_ref,
        normed, after, token, stage, landed, sums, all_sums, send_a, got_a, send_b, got_b,
        w_in, w_out, stream, hidden_ref, half_out, half_in, part_out, part_in, shared_ref,
        rows_in, cols_in, corner_in, masks_in, flux_ref, flux_in, tile_ref, conv_ref, wave_ref,
        middle_out, middle_in, order_ref, affine_ref, mix_ref, offset_ref, share_ref, mask_ref,
        level_ref, spread_ref, field_ref, total_ref, turned_ref, flat_ref, near_sums, all_near,
        sent_sum, came_sum, sent_a, came_a, sent_b, came_b, sent_out, came_out,
        sent_half, came_half, sent_part, came_part, load, sent_load, came_load,
        sent_share, came_share, sent_cells, came_cells, sent_mask, came_mask, sent_flux, came_flux,
        sent_middle, came_middle, sent_near, came_near,
    ) = refs
    rows, slot, longitudes = x_ref.shape
    quarter = longitudes // 4
    middle = quarter // 2
    latitudes = rows * bands
    each = longitudes // 2 // bands
    cells = ocean_ref.shape[1]
    me = lax.axis_index("band")
    comp, tile = lax.axis_index("comp"), lax.axis_index("tile")
    mine = comp * 2 + tile

    def member(step):
        return lax.rem(mine + step, 4)

    def team_id(index):
        return {"comp": lax.div(index, 2), "tile": lax.rem(index, 2)}

    def near_id(b, c):
        index = lax.rem(mine + c + 4, 4)
        return {"band": lax.rem(me + b + bands, bands), **team_id(index)}

    own_loads = [
        pltpu.make_async_copy(source.at[block], target.at[block, 0], load.at[block, i])
        for block in range(2)
        for i, (source, target) in enumerate(((fc_in_ref, w_in), (fc_out_ref, w_out)))
    ]
    sibling_loads = [
        pltpu.make_async_remote_copy(
            src_ref=source.at[block],
            dst_ref=target.at[block, 1],
            send_sem=sent_load.at[block, i],
            recv_sem=came_load.at[block, i],
            device_id={"tile": 1 - tile},
            device_id_type=MESH,
        )
        for block in range(2)
        for i, (source, target) in enumerate(((fc_in_ref, w_in), (fc_out_ref, w_out)))
    ]
    barrier = pltpu.get_barrier_semaphore()

    def greet(step, carry):
        pl.semaphore_signal(
            barrier, inc=1, device_id={"band": lax.rem(me + step, bands)}, device_id_type=MESH
        )
        return carry

    for step in range(1, 4):
        pl.semaphore_signal(barrier, inc=1, device_id=team_id(member(step)), device_id_type=MESH)
    for b, c in directions:
        if b and c:
            pl.semaphore_signal(barrier, inc=1, device_id=near_id(b, c), device_id_type=MESH)
    lax.fori_loop(1, bands, greet, 0)
    for copy in own_loads:
        copy.start()

    def near_copies(source_of, target_of, sent, came):
        copies = []
        for d, (b, c) in enumerate(directions):
            copies.append(
                pltpu.make_async_remote_copy(
                    src_ref=source_of(b, c),
                    dst_ref=target_of(-b, -c),
                    send_sem=sent.at[d],
                    recv_sem=came.at[directions.index((-b, -c))],
                    device_id=near_id(b, c),
                    device_id_type=MESH,
                )
            )
        return copies

    def near_landings(source_of, target_of, sent, came):
        copies = []
        for d, (b, c) in enumerate(directions):
            copies.append(
                pltpu.make_async_remote_copy(
                    src_ref=source_of(b, c),
                    dst_ref=target_of(b, c),
                    send_sem=sent.at[d],
                    recv_sem=came.at[d],
                    device_id=near_id(b, c),
                    device_id_type=MESH,
                )
            )
        return copies

    def cells_from(b, c):
        row = pl.ds(0, 2 * rows) if b == 0 else pl.ds(2 * rows - 3 if b > 0 else 0, 3)
        column = pl.ds(0, cells) if c == 0 else pl.ds(cells - 16 if c > 0 else 0, 16)
        return ocean_ref.at[row, column]

    def cells_to(b, c):
        if c == 0:
            return rows_in.at[0 if b < 0 else 1]
        if b == 0:
            return cols_in.at[0 if c < 0 else 1]
        return corner_in.at[0 if b < 0 else 1, 0 if c < 0 else 1]

    cell_args = (cells_from, cells_to, sent_cells, came_cells)
    mask_args = (
        lambda b, c: mask_ref, lambda b, c: masks_in.at[directions.index((b, c))], sent_mask, came_mask
    )
    flux_args = (
        lambda b, c: flux_ref, lambda b, c: flux_in.at[directions.index((b, c))], sent_flux, came_flux
    )

    def team_copy(source, target, sent, came, step, pick, landing):
        index = member(step)
        chosen = {"whole": lambda: source, "each": lambda: source.at[index]}[pick]()
        place = index if landing else mine
        return pltpu.make_async_remote_copy(
            src_ref=chosen,
            dst_ref=target.at[place],
            send_sem=sent.at[index],
            recv_sem=came.at[place],
            device_id=team_id(index),
            device_id_type=MESH,
        )

    def team_exchange(source, target, sent, came, pick):
        for step in range(1, 4):
            team_copy(source, target, sent, came, step, pick, False).start()

    def team_finish(source, target, sent, came, pick):
        for step in range(1, 4):
            team_copy(source, target, sent, came, step, pick, True).wait()

    def out_copy(block, turn, step, landing):
        index = member(step)
        place = index if landing else mine
        wanted = lax.rem(1 - (comp if landing else lax.div(index, 2)) + turn, 2)
        return pltpu.make_async_remote_copy(
            src_ref=after.at[lax.rem(index, 2), wanted],
            dst_ref=token.at[block, place, wanted],
            send_sem=sent_out.at[block, turn, index],
            recv_sem=came_out.at[block, turn, place],
            device_id=team_id(index),
            device_id_type=MESH,
        )

    def band_copy(source, target, sent, came, step, landing):
        index = lax.rem(me + step, bands)
        return pltpu.make_async_remote_copy(
            src_ref=source.at[index],
            dst_ref=target.at[index if landing else me],
            send_sem=sent.at[index],
            recv_sem=came.at[index if landing else me],
            device_id={"band": index},
            device_id_type=MESH,
        )

    def band_exchange(source, target, sent, came):
        source[...] = stage[...].astype(jnp.bfloat16).reshape(source.shape)

        def go(step, carry):
            band_copy(source, target, sent, came, step, False).start()
            return carry

        lax.fori_loop(1, bands, go, 0)
        target[me] = source[me]

        def come(step, carry):
            band_copy(source, target, sent, came, step, True).wait()
            return carry

        lax.fori_loop(1, bands, come, 0)
        landed[...] = target[...].astype(jnp.float32).reshape(landed.shape)

    lane = lax.broadcasted_iota(jnp.int32, (1, 128), 1)
    first_half = lane < slot - 128
    sign = jnp.where(first_half, 1.0, -1.0)
    half = longitudes // 2
    counted = jnp.ones((8, slot), jnp.bfloat16)
    which = lax.broadcasted_iota(jnp.int32, (8, longitudes), 0)
    turned = (((1,), (1,)), ((), ()))

    def across_rows(left, right):
        return lax.dot_general(left, right, turned, preferred_element_type=jnp.float32)

    def swap(values):
        return pltpu.roll(values, 64, 1)

    def doubled(tails):
        top = jnp.where(first_half, tails, swap(tails))
        low = jnp.where(first_half, swap(tails), tails)
        return jnp.concatenate([top, low], axis=0)

    def tokens(block, lat):
        if block == 0:
            return turned_ref[lat]
        pieces = [middle_in[s, lat].astype(jnp.float32) for s in range(4)]
        return jnp.concatenate(
            [jnp.concatenate([p[:quarter], doubled(p[quarter:])], axis=1) for p in pieces], axis=0
        )

    def spread(lat, wave, part, values):
        stage[pl.ds(part * 9 + lat * 3 + wave, bands, stride=32), :] = values

    def collect(lat, wave, part):
        return landed[pl.ds(part * 9 + lat * 3 + wave, bands, stride=32), :]

    def spectral_filter(block):
        if block == 0:
            total = jnp.zeros((8, longitudes), jnp.float32)
            for lat in range(rows):
                values = x_ref[lat].astype(jnp.float32)
                high, low = split_bf16(values * values)
                total = total + jnp.where(which == lat, times(counted, x_ref[lat]), 0.0)
                total = total + jnp.where(
                    which == rows + lat, times(counted, high) + times(counted, low), 0.0
                )
            sums[...] = total
            pl.semaphore_wait(barrier, bands - 1 + 3 + 4)
            team_exchange(sums, all_sums, sent_sum, came_sum, "whole")
            for copy in near_copies(*mask_args) + near_copies(*cell_args) + sibling_loads:
                copy.start()
            team_exchange(share_ref, shared_ref, sent_share, came_share, "whole")
            shared_ref[mine] = share_ref[...]
            all_sums[mine] = total
            team_finish(sums, all_sums, sent_sum, came_sum, "whole")
            total = all_sums[0] + all_sums[1] + all_sums[2] + all_sums[3]
            columns = jnp.concatenate([total, jnp.zeros((120, longitudes), jnp.float32)], axis=0).T
        else:
            blank = jnp.zeros((120, 128), jnp.float32)
            columns = jnp.concatenate(
                [jnp.concatenate([all_near[s], blank], axis=0).T[:quarter] for s in range(4)], axis=0
            )
        columns = columns * (1.0 / (4 * slot))
        for lat in range(rows):
            average = columns[:, lat : lat + 1]
            power = columns[:, rows + lat : rows + lat + 1]
            scaled = tokens(block, lat) - average
            scaled = scaled * lax.rsqrt(power - average * average + eps_norm)
            scaled = scaled * affine_ref[block, 0:1, :] + affine_ref[block, 2:3, :]
            normed[lat] = scaled
            spectrum = times(forward_ref[...], scaled)
            upper, lower = spectrum[:half], spectrum[half:]
            rest = jnp.where(first_half, upper[:, 128:], lower[:, 128:])
            parts = (upper[:, :128], lower[:, :128], rest)
            for part in range(3):
                for wave in range(each):
                    spread(lat, wave, part, parts[part][wave * bands : (wave + 1) * bands])
        band_exchange(send_a, got_a.at[block], sent_a.at[block], came_a.at[block])
        pieces = []
        for wave in range(each):
            for part in range(3):
                pieces.append(
                    jnp.concatenate([collect(lat, wave, part) for lat in range(rows)], axis=0)
                )
        spectrum = jnp.concatenate(pieces, axis=1).astype(jnp.bfloat16)
        turned_all = times(across_ref[...], spectrum)

        def combine(both, wave, direction):
            base = wave * 384
            cosine, sine = both[:latitudes, base : base + 384], both[latitudes:, base : base + 384]
            real = cosine[:, :128] + direction * sine[:, 128:256]
            imag = cosine[:, 128:256] - direction * sine[:, :128]
            rest = cosine[:, 256:] + (direction * sign) * swap(sine[:, 256:])
            return real, imag, rest

        rows_mixed = jnp.concatenate(
            [jnp.concatenate(combine(turned_all, wave, 1.0), axis=1) for wave in range(each)], axis=0
        )
        hidden = times(rows_mixed, mix_ref[block, 0])
        hidden = jnp.maximum(hidden + offset_ref[block, 0:1, :], 0.0)
        mixed = times(hidden, mix_ref[block, 1])
        mixed = soft_shrink(mixed + offset_ref[block, 1:2, :])
        mixed = jnp.concatenate(
            [mixed[wave * latitudes : (wave + 1) * latitudes] for wave in range(each)], axis=1
        )
        turned_back = times(back_ref[...], mixed)
        for wave in range(each):
            parts = combine(turned_back, wave, -1.0)
            for part in range(3):
                for lat in range(rows):
                    spread(lat, wave, part, parts[part][lat * bands : (lat + 1) * bands])
        band_exchange(send_b, got_b.at[block], sent_b.at[block], came_b.at[block])
        for lat in range(rows):
            real, imag, rest = (
                jnp.concatenate([collect(lat, wave, part) for wave in range(each)], axis=0)
                for part in range(3)
            )
            right = jnp.concatenate(
                [
                    jnp.concatenate([real, rest], axis=1),
                    jnp.concatenate([imag, swap(rest)], axis=1),
                ],
                axis=0,
            ).astype(jnp.bfloat16)
            restored = times(inverse_ref[...], right)
            result = tokens(block, lat) + restored + normed[lat]
            for s in range(4):
                piece = result[s * quarter : (s + 1) * quarter]
                tail = piece[:, 128:]
                tail = jnp.where(first_half, tail[:middle], swap(tail[middle:]))
                after[s % 2, s // 2, lat, :quarter] = piece[:, :128].astype(jnp.bfloat16)
                after[s % 2, s // 2, lat, quarter:] = tail.astype(jnp.bfloat16)
        for turn in range(2):
            for step in range(1, 4):
                out_copy(block, turn, step, False).start()
        token[block, mine] = after[tile]
        for i in range(2):
            own_loads[2 * block + i].wait()
            sibling_loads[2 * block + i].wait()

    def pair(left, right):
        return jnp.concatenate(
            [jnp.where(first_half, left, swap(right)), jnp.where(first_half, swap(left), right)], 0
        )

    def unpair(both):
        top, low = both[:middle], both[middle:]
        return jnp.where(first_half, top, swap(low)), jnp.where(first_half, swap(top), low)

    def pack(block_rows, target):
        tails = unpair(block_rows[:, 512:640]) + unpair(block_rows[:, 640:])
        for s in range(4):
            place = target(s)
            place[:quarter] = block_rows[:, s * 128 : (s + 1) * 128].astype(jnp.bfloat16)
            place[quarter:] = tails[s].astype(jnp.bfloat16)

    def lanes_of(slices):
        heads = [p[:quarter] for p in slices]
        tails = [p[quarter:] for p in slices]
        return jnp.concatenate(heads + [pair(*tails[:2]), pair(*tails[2:])], axis=1)

    def reorder(values):
        t = [values[:, i * 128 : (i + 1) * 128] for i in range(6)]

        def inner(a, b):
            return jnp.where(first_half, swap(a), swap(b)), jnp.where(first_half, a, b)

        one, tails_a = inner(t[1], t[2])
        three, tails_b = inner(t[4], t[5])
        return jnp.concatenate([t[0], one, t[3], three, tails_a, tails_b], axis=1)

    row_spans = [(s * slot, 128) for s in range(4)] + [(s * slot + 128, slot - 128) for s in range(4)]

    def mlp(block, which_quarter):
        for lat in range(rows):
            slices = [token[block, s, which_quarter, lat].astype(jnp.float32) for s in range(4)]
            stream[lat * quarter : (lat + 1) * quarter] = lanes_of(slices)
        values = stream[...]
        normal = layer_norm(values, order_ref[block, 1:2, :], order_ref[block, 3:4, :])
        normal = normal.astype(jnp.bfloat16)
        wide = w_in.shape[3]
        for part in range(2):

            def piece(i, carry):
                at = pl.multiple_of(i * 256, 256)
                weight = jnp.concatenate(
                    [w_in[block, part, pl.ds(a, n), pl.ds(at, 256)] for a, n in row_spans], axis=0
                )
                z = jnp.dot(normal, weight, preferred_element_type=jnp.float32)
                hidden_ref[:, pl.ds(part * wide + at, 256)] = gelu(z).astype(jnp.bfloat16)
                return carry

            lax.fori_loop(0, wide // 256, piece, 0)
        total = jnp.dot(hidden_ref[:, :wide], w_out[block, 0], preferred_element_type=jnp.float32)
        total = total + jnp.dot(
            hidden_ref[:, wide:], w_out[block, 1], preferred_element_type=jnp.float32
        )
        total_ref[...] = reorder(total)

    zeros = functools.partial(jnp.zeros, dtype=jnp.float32)
    for block in range(2):
        both = jnp.concatenate([gain_ref[block], shift_ref[block], zeros((4, 4 * slot))], axis=0)
        order_ref[block] = reorder(both)
        head = order_ref[block, :, pl.ds(pl.multiple_of(mine * 128, 128), 128)]
        tail = order_ref[block, :, pl.ds(pl.multiple_of(512 + comp * 128, 128), 128)]
        tail = jnp.where(tile == 0, tail, swap(tail))
        tail = jnp.where(first_half, tail, swap(tail))
        affine_ref[block] = jnp.concatenate([head, tail], axis=1)
        for sublayer in range(2):

            def placed(weight):
                width = weight.shape[1]
                wide = jnp.concatenate([weight, zeros((slot, 128 - width))], axis=1)
                moved = pltpu.roll(wide[width:], width, 1)
                low = jnp.where(lane >= width, moved, 0.0)
                high = jnp.where(first_half, moved, 0.0)
                return (
                    jnp.concatenate([wide[:width], low], axis=0),
                    jnp.concatenate([zeros((width, 128)), high], axis=0),
                )

            real, real_tail = placed(weight_ref[block, sublayer, 0])
            imag, imag_tail = placed(weight_ref[block, sublayer, 1])
            upper = jnp.concatenate([real, imag, real_tail + swap(imag_tail)], axis=1)
            lower = jnp.concatenate([-imag, real, swap(real_tail) - imag_tail], axis=1)
            mix_ref[block, sublayer] = jnp.concatenate(
                [upper[:128], lower[:128], upper[128:], lower[128:]], axis=0
            ).astype(jnp.bfloat16)
            bias = bias_ref[block, sublayer]
            tail = jnp.concatenate([bias[:, 128:], bias[:, 128:]], axis=1)
            offset_ref[block, sublayer : sublayer + 1, :] = jnp.concatenate(
                [bias[0:1, :128], bias[1:2, :128], jnp.where(first_half, tail[0:1], tail[1:2])], axis=1
            )
    share_ref[...] = zeros(share_ref.shape)
    share_ref[0:8, :slot] = flux_head_ref[...].astype(jnp.float32)
    for lat in range(rows):
        values = x_ref[lat].astype(jnp.float32)
        turned_ref[lat] = jnp.concatenate([values, values[128:]], axis=0).T
    for f in range(4):
        for a in range(2):
            for e in range(2):
                at, row = 8 + e * 16 + a * 8 + f, f * 4 + a * 2 + e
                share_ref[at : at + 1, :slot] = patch_ref[row : row + 1, :]
    mask_ref[...] = zeros(mask_ref.shape)
    mask_ref[: 2 * rows, :cells] = sea_ref[...].astype(jnp.float32)
    level_ref[...] = zeros(level_ref.shape)
    for level in range(rows + 4):
        level_ref[level * 8 : level * 8 + 8, level * 256 : (level + 1) * 256] = flux_embed_ref[...]
    spread_ref[0], spread_ref[1] = split_bf16(level_ref[...])
    fields = jnp.concatenate([field_head_ref[...], zeros((4, 256))], axis=0)
    field_ref[...] = jnp.concatenate(thirds(fields), axis=0)

    spectral_filter(0)
    team_finish(share_ref, shared_ref, sent_share, came_share, "whole")
    copy = pltpu.make_async_remote_copy(
        src_ref=half_out,
        dst_ref=half_in,
        send_sem=sent_half.at[0],
        recv_sem=came_half.at[0],
        device_id={"comp": 1 - comp},
        device_id_type=MESH,
    )

    def halves(i, carry):
        for step in range(1, 4):
            out_copy(0, i, step, True).wait()
        mlp(0, lax.rem(1 - comp + i, 2))

        @pl.when(i == 0)
        def _():
            half_out[...] = total_ref[...].astype(jnp.bfloat16)
            copy.start()

        return carry

    lax.fori_loop(0, 2, halves, 0)
    copy.wait()
    first = stream[...] + total_ref[...] + half_in[...].astype(jnp.float32)
    first = first.astype(jnp.bfloat16)
    stream[...] = first.astype(jnp.float32)

    small = [shared_ref[s] for s in range(4)]
    tails = [s[:, 128:] for s in small]
    whole = jnp.concatenate(
        [s[:, :128] for s in small]
        + [jnp.where(first_half, tails[i], swap(tails[i + 1])) for i in (0, 2)],
        axis=1,
    )
    head, embed = whole[:8].astype(jnp.bfloat16), whole[8:]
    for lat in range(rows):
        flux = across_rows(head, first[lat * quarter : (lat + 1) * quarter])
        flux_ref[lat] = jnp.concatenate([flux, jnp.zeros((8, 128 - quarter), jnp.float32)], axis=1)
    for copy in near_copies(*flux_args):
        copy.start()
    for copy in near_landings(*mask_args) + near_landings(*cell_args) + near_landings(*flux_args):
        copy.wait()

    def flux_at(lat, c):
        b = -1 if lat < 0 else 1 if lat >= rows else 0
        if (b, c) == (0, 0):
            return flux_ref[lat]
        return flux_in[directions.index((b, c)), lat % rows]

    ext_lats = range(-2, rows + 2)
    laid = jnp.concatenate(
        [jnp.concatenate([flux_at(lat, c) for c in (-1, 0, 1)], axis=1) for lat in ext_lats]
        + [jnp.zeros((128 - 8 * len(ext_lats), 384), jnp.float32)],
        axis=0,
    )
    raised = across_rows(pick_ref[...], jnp.concatenate(thirds(laid), axis=0))
    raised = raised[:, :128] + raised[:, 128:256] + raised[:, 256:]
    forcing = product(split_bf16(raised), (spread_ref[0], spread_ref[1]))

    def mask_rows(b, c):
        whole = mask_ref[...] if (b, c) == (0, 0) else masks_in[directions.index((b, c))]
        whole = whole[:, 128:] if c < 0 else whole[:, :128] if c > 0 else whole
        return whole[2 * rows - 3 : 2 * rows] if b < 0 else whole[:3] if b > 0 else whole[: 2 * rows]

    ext_rows = 2 * rows + 6
    masks = jnp.concatenate(
        [jnp.concatenate([mask_rows(b, c) for c in (-1, 0, 1)], axis=1) for b in (-1, 0, 1)]
        + [jnp.zeros((16 - ext_rows, 512), jnp.float32)],
        axis=0,
    )
    masks = across_rows(seen_ref[...], masks.astype(jnp.bfloat16))
    for row in range(ext_rows):
        b = -1 if row < 3 else 1 if row >= 2 * rows + 3 else 0
        at = row if b < 0 else row - 3 if b == 0 else row - 2 * rows - 3
        sources = (
            cols_in[0, at] if b == 0 else corner_in[0 if b < 0 else 1, 0, at],
            ocean_ref[at] if b == 0 else rows_in[0 if b < 0 else 1, at],
            cols_in[1, at] if b == 0 else corner_in[0 if b < 0 else 1, 1, at],
        )
        sources = [s.astype(jnp.float32) for s in sources]
        state = jnp.concatenate([sources[0][8:], sources[1], sources[2][:8]], axis=0)
        level = (row - 3) // 2 + 2
        start = state + masks[:, row : row + 1] * forcing[:, level * 256 : (level + 1) * 256]
        start = start.astype(jnp.bfloat16).astype(jnp.float32)
        if b:
            inside = jnp.where(me > 0, 1.0, 0.0) if b < 0 else jnp.where(me < bands - 1, 1.0, 0.0)
            start = start * inside
        for part in range(2):
            tile_ref[part, row] = start[:, part * 128 : (part + 1) * 128]

    for part in range(2):
        span = slice(part * 128, (part + 1) * 128)

        def strip(i, carry):
            at = pl.multiple_of(i * 16, 16)
            totals = [jnp.zeros((16, 128), jnp.float32) for _ in range(2 * rows)]
            for e in range(7):
                for row in range(ext_rows):
                    values = tile_ref[part, row, pl.ds(at + 5 + e, 16), :]
                    for a in range(7):
                        if 0 <= row - a < 2 * rows:
                            tap = depth_ref[a, e : e + 1, span]
                            totals[row - a] = totals[row - a] + values * tap
            for row in range(2 * rows):
                conv_ref[row, pl.ds(at, 16), span] = totals[row]
            return carry

        lax.fori_loop(0, cells // 16, strip, 0)

    own_columns = jnp.concatenate([mask_ref[...], jnp.zeros((120, 256), jnp.float32)], axis=0).T
    for start_row in range(0, 2 * rows, 2):
        values = conv_ref[start_row : start_row + 2].reshape(2 * cells, 256)
        normal = layer_norm(values, ocean_gain_ref[...], ocean_shift_ref[...])
        normal = normal.astype(jnp.bfloat16)

        def piece(i, carry):
            at = pl.multiple_of(i * 256, 256)
            z = jnp.dot(normal, ocean_in_ref[:, pl.ds(at, 256)], preferred_element_type=jnp.float32)
            wave_ref[:, pl.ds(at, 256)] = gelu(z).astype(jnp.bfloat16)
            return carry

        lax.fori_loop(0, ocean_in_ref.shape[1] // 256, piece, 0)
        update = jnp.dot(wave_ref[...], ocean_out_ref[...], preferred_element_type=jnp.float32)
        update = update * layer_ref[...]
        for row in range(start_row, start_row + 2):
            begin = jnp.concatenate([tile_ref[part, row + 3, 8 : 8 + cells] for part in range(2)], axis=1)
            change = update[(row - start_row) * cells : (row - start_row + 1) * cells]
            fresh = (begin + own_columns[:cells, row : row + 1] * change).astype(jnp.bfloat16)
            next_ref[row] = fresh
            field = across_rows(field_ref[...], fresh)
            field = (field[:8] + field[8:16] + field[16:24]) * mask_ref[row : row + 1, :cells]
            flat_ref[row] = field
            surface_ref[row] = field[:4]

    near = zeros((8, quarter))
    for lat in range(rows):
        both = jnp.concatenate([flat_ref[2 * lat], flat_ref[2 * lat + 1]], axis=0)
        patch = across_rows(split_ref[...], jnp.concatenate(thirds(both), axis=0))
        patch = patch[:, :16] + patch[:, 16:32] + patch[:, 32:48]
        total = stream[lat * quarter : (lat + 1) * quarter]
        for e in range(2):
            total = total + product(
                split_bf16(patch[e * quarter : (e + 1) * quarter]),
                split_bf16(embed[e * 16 : (e + 1) * 16]),
            )
        pack(total, lambda s, lat=lat: middle_out.at[s, lat])
        rounded = total.astype(jnp.bfloat16)
        wide = rounded.astype(jnp.float32)
        high, low = split_bf16(wide * wide)
        every = jnp.ones((8, 4 * slot), jnp.bfloat16)
        plain, power = across_rows(every, rounded), across_rows(every, high) + across_rows(every, low)
        row_index = lax.broadcasted_iota(jnp.int32, (8, quarter), 0)
        near = near + jnp.where(row_index == lat, plain, 0.0)
        near = near + jnp.where(row_index == rows + lat, power, 0.0)
    near_sums[...] = jnp.concatenate([near, zeros((8, 128 - quarter))], axis=1)
    near_args = (near_sums, all_near, sent_near, came_near, "whole")
    team_exchange(*near_args)
    all_near[mine] = near_sums[...]
    args = (middle_out, middle_in, sent_middle, came_middle, "each")
    team_exchange(*args)
    middle_in[mine] = middle_out[mine]
    team_finish(*args)
    team_finish(*near_args)

    spectral_filter(1)

    def quarters(i, carry):
        for step in range(1, 4):
            out_copy(1, i, step, True).wait()
        which_quarter = lax.rem(1 - comp + i, 2)
        mlp(1, which_quarter)
        for lat in range(rows):
            pack(
                total_ref[lat * quarter : (lat + 1) * quarter],
                lambda s, lat=lat: part_out.at[which_quarter, s, lat],
            )
        team_exchange(
            part_out.at[which_quarter], part_in.at[which_quarter],
            sent_part.at[which_quarter], came_part.at[which_quarter], "each",
        )
        part_in[which_quarter, mine] = part_out[which_quarter, mine]
        return carry

    lax.fori_loop(0, 2, quarters, 0)
    for which_quarter in range(2):
        team_finish(
            part_out.at[which_quarter], part_in.at[which_quarter],
            sent_part.at[which_quarter], came_part.at[which_quarter], "each",
        )
        for half_of in range(2):
            for lat in range(rows):
                piece = after[half_of, which_quarter, lat].astype(jnp.float32)
                piece = piece + part_in[which_quarter, half_of, lat].astype(jnp.float32)
                piece = piece + part_in[which_quarter, 2 + half_of, lat].astype(jnp.float32)
                tail = piece[quarter:]
                at = (2 * which_quarter + half_of) * quarter
                tail = jnp.concatenate([tail, swap(tail)], axis=0)
                atmosphere_ref[lat, at : at + quarter, :128] = piece[:quarter].astype(jnp.bfloat16)
                atmosphere_ref[lat, at : at + quarter, 128:] = tail[:, : slot - 128].astype(
                    jnp.bfloat16
                )


def on_device(
    atmosphere, spec_weight, spec_bias, norm_gain, norm_shift, fc_in, fc_out, flux_head, flux_embed,
    ocean_state, sea_mask, depth_kernel, ocean_gain, ocean_shift, ocean_in, ocean_out, layer_scale,
    field_head, patch_embed,
):
    bands = lax.axis_size("band")
    rows, longitudes, slot = atmosphere.shape
    quarter = longitudes // 4
    count = rows * quarter
    latitudes = rows * bands
    channels, wide = fc_in.shape[1:]
    packed = quarter * slot // 128
    cells, ocean_channels = ocean_state.shape[1:]
    waves = ocean_in.shape[1]

    inside, outside = pl.BlockSpec(memory_space=pltpu.VMEM), pl.BlockSpec(memory_space=pl.ANY)
    arguments = [
        atmosphere.transpose(0, 2, 1), spec_weight, spec_bias, norm_gain, norm_shift, fc_in, fc_out,
        flux_head.T,
        flux_embed, ocean_state, sea_mask, depth_kernel, ocean_gain[None], ocean_shift[None],
        ocean_in, ocean_out, layer_scale[None], field_head.T, patch_embed,
        *transforms(latitudes, longitudes, bands), *ocean_selectors(quarter),
    ]
    specs = [inside] * 5 + [outside] * 2 + [inside] * (len(arguments) - 7)
    levels = (rows + 4) * ocean_channels
    narrow, single = jnp.bfloat16, jnp.float32

    def dma(*shape):
        return pltpu.SemaphoreType.DMA(shape)

    chunks = (bands, 32, 128)
    scratch = [
        pltpu.VMEM((rows, longitudes, 256), single),
        pltpu.VMEM((2, 2, rows, packed, 128), narrow),
        pltpu.VMEM((2, 4, 2, rows, packed, 128), narrow),
        pltpu.VMEM((bands * 32, 128), single),
        pltpu.VMEM((bands * 32, 128), single),
        pltpu.VMEM((8, longitudes), single),
        pltpu.VMEM((4, 8, longitudes), single),
        pltpu.VMEM(chunks, narrow),
        pltpu.VMEM((2,) + chunks, narrow),
        pltpu.VMEM(chunks, narrow),
        pltpu.VMEM((2,) + chunks, narrow),
        pltpu.VMEM((2, 2, channels, wide), narrow),
        pltpu.VMEM((2, 2, wide, channels), narrow),
        pltpu.VMEM((count, channels), single),
        pltpu.VMEM((count, 2 * wide), narrow),
        pltpu.VMEM((count, channels), narrow),
        pltpu.VMEM((count, channels), narrow),
        pltpu.VMEM((2, 4, rows, packed, 128), narrow),
        pltpu.VMEM((2, 4, rows, packed, 128), narrow),
        pltpu.VMEM((4, 40, 256), single),
        pltpu.VMEM((2, 3, cells, ocean_channels), narrow),
        pltpu.VMEM((2, 2 * rows, 16, ocean_channels), narrow),
        pltpu.VMEM((2, 2, 3, 16, ocean_channels), narrow),
        pltpu.VMEM((8, 8, 256), single),
        pltpu.VMEM((rows, 8, 128), single),
        pltpu.VMEM((8, rows, 8, 128), single),
        pltpu.VMEM((2, 2 * rows + 6, cells + 16, 128), single),
        pltpu.VMEM((2 * rows, cells, ocean_channels), single),
        pltpu.VMEM((2 * cells, waves), narrow),
        pltpu.VMEM((4, rows, packed, 128), narrow),
        pltpu.VMEM((4, rows, packed, 128), narrow),
        pltpu.VMEM((2, 8, channels), single),
        pltpu.VMEM((2, 8, 256), single),
        pltpu.VMEM((2, 2, 2 * slot, 2 * slot), narrow),
        pltpu.VMEM((2, 8, 2 * slot), single),
        pltpu.VMEM((40, 256), single),
        pltpu.VMEM((8, 256), single),
        pltpu.VMEM((128, levels), single),
        pltpu.VMEM((2, 128, levels), narrow),
        pltpu.VMEM((24, ocean_channels), narrow),
        pltpu.VMEM((count, channels), single),
        pltpu.VMEM((rows, longitudes, 256), single),
        pltpu.VMEM((2 * rows, 8, cells), single),
        pltpu.VMEM((8, 128), single),
        pltpu.VMEM((4, 8, 128), single),
        dma(4), dma(4), dma(2, bands), dma(2, bands), dma(2, bands), dma(2, bands),
        dma(2, 2, 4), dma(2, 2, 4), dma(1), dma(1), dma(2, 4), dma(2, 4), dma(2, 2), dma(2, 2), dma(2, 2),
        dma(4), dma(4), dma(8), dma(8), dma(8), dma(8), dma(8), dma(8), dma(4), dma(4),
        dma(4), dma(4),
    ]
    atmosphere_next, ocean_next, surface = pl.pallas_call(
        functools.partial(step_kernel, bands),
        out_shape=(
            jax.ShapeDtypeStruct(atmosphere.shape, narrow),
            jax.ShapeDtypeStruct(ocean_state.shape, narrow),
            jax.ShapeDtypeStruct((2 * rows, 4, cells), single),
        ),
        in_specs=specs,
        out_specs=(inside,) * 3,
        scratch_shapes=scratch,
        compiler_params=pltpu.CompilerParams(
            collective_id=0, has_side_effects=True, vmem_limit_bytes=63 << 20
        ),
    )(*arguments)
    return (atmosphere_next, ocean_next, surface.transpose(0, 2, 1))


def solution(mesh):
    placed = (
        P("band", None, ("comp", "tile")),
        P(None, None, None, ("comp", "tile"), None),
        P(None, None, None, ("comp", "tile")),
        P(),
        P(),
        P(None, None, ("comp", "tile")),
        P(None, ("comp", "tile"), None),
        P(("comp", "tile"), None),
        P(),
        P("band", ("comp", "tile"), None),
        P("band", ("comp", "tile")),
        P(),
        P(),
        P(),
        P(),
        P(),
        P(),
        P(),
        P(None, ("comp", "tile")),
    )
    return jax.shard_map(
        on_device,
        mesh=mesh,
        in_specs=placed,
        out_specs=(
            P("band", None, ("comp", "tile")),
            P("band", ("comp", "tile"), None),
            P("band", ("comp", "tile"), None),
        ),
        check_vma=False,
    )
```

```python
import functools
import math

import jax
import jax.numpy as jnp
import numpy as np
from jax import lax
from jax.experimental import pallas as pl
from jax.experimental.pallas import tpu as pltpu
from jax.sharding import PartitionSpec as P

MESH = pl.DeviceIdType.MESH
full_precision = lax.Precision.HIGHEST
eps_norm = 1e-06
shrink_level = 0.01


def layer_norm(values, scaling, offset):
    average = jnp.mean(values, axis=-1, keepdims=True)
    squares = jnp.mean(values * values, axis=-1, keepdims=True)
    variance = squares - average * average
    return (values - average) * lax.rsqrt(variance + eps_norm) * scaling + offset


def soft_shrink(values):
    zeros = jnp.zeros_like(values)
    return jnp.where(
        values > shrink_level,
        values - shrink_level,
        jnp.where(values < -shrink_level, values + shrink_level, zeros),
    )


def split_bf16(array):
    high = array.astype(jnp.bfloat16)
    return high, (array - high.astype(jnp.float32)).astype(jnp.bfloat16)


def transforms(latitudes, longitudes, bands):
    kept = longitudes // 2
    each, rows = kept // bands, latitudes // bands
    waves = np.arange(kept).reshape(bands, each).T.reshape(-1)
    lats = np.arange(latitudes).reshape(bands, rows).T.reshape(-1)
    lon = np.outer(waves, np.arange(longitudes)) % longitudes * (2.0 * math.pi / longitudes)
    lat = np.outer(np.arange(latitudes), lats) % latitudes * (2.0 * math.pi / latitudes)
    forward = np.concatenate([np.cos(lon), -np.sin(lon)], 0) / math.sqrt(longitudes)
    across = np.stack([np.cos(lat), np.sin(lat)], 0) / math.sqrt(latitudes)
    weight = np.where(waves == 0, 1.0, 2.0)[:, None]
    inverse = np.concatenate([np.cos(lon) * weight, -np.sin(lon) * weight], 0).T
    mats = (
        forward,
        across.reshape(2 * latitudes, latitudes),
        across.transpose(0, 2, 1).reshape(2 * latitudes, latitudes),
        inverse / math.sqrt(longitudes),
    )
    return [jnp.asarray(m, jnp.bfloat16) for m in mats]


def times(left, right):
    return jnp.dot(
        left.astype(jnp.bfloat16), right.astype(jnp.bfloat16), preferred_element_type=jnp.float32
    )


def product(left, right):
    total = None
    for a, b in ((0, 0), (1, 0), (0, 1)):
        if a < len(left) and b < len(right):
            term = jnp.dot(left[a], right[b], preferred_element_type=jnp.float32)
            total = term if total is None else total + term
    return total


directions = [(b, c) for b in (-1, 0, 1) for c in (-1, 0, 1) if (b, c) != (0, 0)]


def ocean_selectors(quarter):
    columns = np.arange(-8, 2 * quarter + 8)
    pick = np.zeros((len(columns), 384), np.float32)
    seen = np.zeros((len(columns), 512), np.float32)
    for i, column in enumerate(columns):
        if not -3 <= column < 2 * quarter + 3:
            continue
        token = column // 2
        side = 0 if token < 0 else 2 if token >= quarter else 1
        pick[i, side * 128 + token % quarter] = 1
        inner = column % (2 * quarter)
        seen[i, inner - 128 if column < 0 else 384 + inner if column >= 2 * quarter else 128 + inner] = 1
    split = np.zeros((2 * quarter, 2 * quarter), np.float32)
    for e in range(2):
        split[e * quarter + np.arange(quarter), 2 * np.arange(quarter) + e] = 1
    return (jnp.asarray(m, jnp.bfloat16) for m in (pick, seen, split))


def thirds(array):
    high = array.astype(jnp.bfloat16)
    rest = array - high.astype(jnp.float32)
    middle = rest.astype(jnp.bfloat16)
    return high, middle, (rest - middle.astype(jnp.float32)).astype(jnp.bfloat16)


def gelu(z):
    return 0.5 * z * (1.0 + lax.erf(z * math.sqrt(0.5)))


def step_kernel(bands, *refs):
    (
        x_ref, weight_ref, bias_ref, gain_ref, shift_ref, fc_in_ref, fc_out_ref, flux_head_ref,
        flux_embed_ref, ocean_ref, sea_ref, depth_ref, ocean_gain_ref, ocean_shift_ref,
        ocean_in_ref, ocean_out_ref, layer_ref, field_head_ref, patch_ref,
        forward_ref, across_ref, back_ref, inverse_ref, pick_ref, seen_ref, split_ref,
        atmosphere_ref, next_ref, surface_ref,
        normed, after, token, stage, landed, sums, all_sums, send_a, got_a, send_b, got_b,
        w_in, w_out, stream, hidden_ref, half_out, half_in, part_out, part_in, shared_ref,
        rows_in, cols_in, corner_in, masks_in, flux_ref, flux_in, tile_ref, conv_ref, wave_ref,
        middle_out, middle_in, order_ref, affine_ref, mix_ref, offset_ref, share_ref, mask_ref,
        level_ref, spread_ref, field_ref, total_ref, turned_ref, flat_ref, near_sums, all_near,
        seen_masks, own_masks,
        sent_sum, came_sum, sent_a, came_a, sent_b, came_b, sent_out, came_out,
        sent_half, came_half, sent_part, came_part, load, sent_load, came_load,
        sent_share, came_share, sent_cells, came_cells, sent_mask, came_mask, sent_flux, came_flux,
        sent_middle, came_middle, sent_near, came_near,
    ) = refs
    rows, slot, longitudes = x_ref.shape
    quarter = longitudes // 4
    middle = quarter // 2
    latitudes = rows * bands
    each = longitudes // 2 // bands
    cells = ocean_ref.shape[1]
    me = lax.axis_index("band")
    comp, tile = lax.axis_index("comp"), lax.axis_index("tile")
    mine = comp * 2 + tile

    def member(step):
        return lax.rem(mine + step, 4)

    def team_id(index):
        return {"comp": lax.div(index, 2), "tile": lax.rem(index, 2)}

    def near_id(b, c):
        index = lax.rem(mine + c + 4, 4)
        return {"band": lax.rem(me + b + bands, bands), **team_id(index)}

    own_loads = [
        pltpu.make_async_copy(source.at[block], target.at[block, 0], load.at[block, i])
        for block in range(2)
        for i, (source, target) in enumerate(((fc_in_ref, w_in), (fc_out_ref, w_out)))
    ]
    sibling_loads = [
        pltpu.make_async_remote_copy(
            src_ref=source.at[block],
            dst_ref=target.at[block, 1],
            send_sem=sent_load.at[block, i],
            recv_sem=came_load.at[block, i],
            device_id={"tile": 1 - tile},
            device_id_type=MESH,
        )
        for block in range(2)
        for i, (source, target) in enumerate(((fc_in_ref, w_in), (fc_out_ref, w_out)))
    ]
    barrier = pltpu.get_barrier_semaphore()

    def greet(step, carry):
        pl.semaphore_signal(
            barrier, inc=1, device_id={"band": lax.rem(me + step, bands)}, device_id_type=MESH
        )
        return carry

    for step in range(1, 4):
        pl.semaphore_signal(barrier, inc=1, device_id=team_id(member(step)), device_id_type=MESH)
    for b, c in directions:
        if b and c:
            pl.semaphore_signal(barrier, inc=1, device_id=near_id(b, c), device_id_type=MESH)
    lax.fori_loop(1, bands, greet, 0)
    for copy in own_loads:
        copy.start()

    def near_copies(source_of, target_of, sent, came):
        copies = []
        for d, (b, c) in enumerate(directions):
            copies.append(
                pltpu.make_async_remote_copy(
                    src_ref=source_of(b, c),
                    dst_ref=target_of(-b, -c),
                    send_sem=sent.at[d],
                    recv_sem=came.at[directions.index((-b, -c))],
                    device_id=near_id(b, c),
                    device_id_type=MESH,
                )
            )
        return copies

    def near_landings(source_of, target_of, sent, came):
        copies = []
        for d, (b, c) in enumerate(directions):
            copies.append(
                pltpu.make_async_remote_copy(
                    src_ref=source_of(b, c),
                    dst_ref=target_of(b, c),
                    send_sem=sent.at[d],
                    recv_sem=came.at[d],
                    device_id=near_id(b, c),
                    device_id_type=MESH,
                )
            )
        return copies

    def cells_from(b, c):
        row = pl.ds(0, 2 * rows) if b == 0 else pl.ds(2 * rows - 3 if b > 0 else 0, 3)
        column = pl.ds(0, cells) if c == 0 else pl.ds(cells - 16 if c > 0 else 0, 16)
        return ocean_ref.at[row, column]

    def cells_to(b, c):
        if c == 0:
            return rows_in.at[0 if b < 0 else 1]
        if b == 0:
            return cols_in.at[0 if c < 0 else 1]
        return corner_in.at[0 if b < 0 else 1, 0 if c < 0 else 1]

    cell_args = (cells_from, cells_to, sent_cells, came_cells)
    mask_args = (
        lambda b, c: mask_ref, lambda b, c: masks_in.at[directions.index((b, c))], sent_mask, came_mask
    )
    flux_args = (
        lambda b, c: flux_ref, lambda b, c: flux_in.at[directions.index((b, c))], sent_flux, came_flux
    )

    def team_copy(source, target, sent, came, step, pick, landing):
        index = member(step)
        chosen = {"whole": lambda: source, "each": lambda: source.at[index]}[pick]()
        place = index if landing else mine
        return pltpu.make_async_remote_copy(
            src_ref=chosen,
            dst_ref=target.at[place],
            send_sem=sent.at[index],
            recv_sem=came.at[place],
            device_id=team_id(index),
            device_id_type=MESH,
        )

    def team_exchange(source, target, sent, came, pick):
        for step in range(1, 4):
            team_copy(source, target, sent, came, step, pick, False).start()

    def team_finish(source, target, sent, came, pick):
        for step in range(1, 4):
            team_copy(source, target, sent, came, step, pick, True).wait()

    def out_copy(block, turn, step, landing):
        index = member(step)
        place = index if landing else mine
        wanted = turn
        if block == 0:
            wanted = lax.rem(1 - (comp if landing else lax.div(index, 2)) + turn, 2)
        return pltpu.make_async_remote_copy(
            src_ref=after.at[lax.rem(index, 2), wanted],
            dst_ref=token.at[block, place, wanted],
            send_sem=sent_out.at[block, turn, index],
            recv_sem=came_out.at[block, turn, place],
            device_id=team_id(index),
            device_id_type=MESH,
        )

    def band_copy(source, target, sent, came, step, landing):
        index = lax.rem(me + step, bands)
        return pltpu.make_async_remote_copy(
            src_ref=source.at[index],
            dst_ref=target.at[index if landing else me],
            send_sem=sent.at[index],
            recv_sem=came.at[index if landing else me],
            device_id={"band": index},
            device_id_type=MESH,
        )

    def band_exchange(source, target, sent, came, meanwhile):
        source[...] = stage[: bands * 32].astype(jnp.bfloat16).reshape(source.shape)

        def go(step, carry):
            band_copy(source, target, sent, came, step, False).start()
            return carry

        lax.fori_loop(1, bands, go, 0)
        target[me] = source[me]
        meanwhile()

        def widen(index):
            at = pl.multiple_of(index * 32, 32)
            landed[pl.ds(at, 32), :] = target[index].astype(jnp.float32)

        widen(me)

        def come(step, carry):
            band_copy(source, target, sent, came, step, True).wait()
            widen(lax.rem(me + step, bands))
            return carry

        lax.fori_loop(1, bands, come, 0)

    lane = lax.broadcasted_iota(jnp.int32, (1, 128), 1)
    first_half = lane < slot - 128
    sign = jnp.where(first_half, 1.0, -1.0)
    half = longitudes // 2
    counted = jnp.ones((8, slot), jnp.bfloat16)
    which = lax.broadcasted_iota(jnp.int32, (8, longitudes), 0)
    turned = (((1,), (1,)), ((), ()))

    def across_rows(left, right):
        return lax.dot_general(left, right, turned, preferred_element_type=jnp.float32)

    def swap(values):
        return pltpu.roll(values, 64, 1)

    def doubled(tails):
        top = jnp.where(first_half, tails, swap(tails))
        low = jnp.where(first_half, swap(tails), tails)
        return jnp.concatenate([top, low], axis=0)

    def tokens(block, lat):
        if block == 0:
            return turned_ref[lat]
        pieces = [middle_in[s, lat].astype(jnp.float32) for s in range(4)]
        return jnp.concatenate(
            [jnp.concatenate([p[:quarter], doubled(p[quarter:])], axis=1) for p in pieces], axis=0
        )

    def spread(lat, wave, part, values):
        stage[pl.ds(part * 9 + lat * 3 + wave, bands, stride=32), :] = values

    def collect(lat, wave, part):
        return landed[pl.ds(part * 9 + lat * 3 + wave, bands, stride=32), :]

    def spectral_filter(block, while_first, while_second):
        if block == 0:
            total = jnp.zeros((8, longitudes), jnp.float32)
            for lat in range(rows):
                values = x_ref[lat].astype(jnp.float32)
                high, low = split_bf16(values * values)
                total = total + jnp.where(which == lat, times(counted, x_ref[lat]), 0.0)
                total = total + jnp.where(
                    which == rows + lat, times(counted, high) + times(counted, low), 0.0
                )
            sums[...] = total
            pl.semaphore_wait(barrier, bands - 1 + 3 + 4)
            team_exchange(sums, all_sums, sent_sum, came_sum, "whole")
            for copy in near_copies(*mask_args) + near_copies(*cell_args) + sibling_loads:
                copy.start()
            team_exchange(share_ref, shared_ref, sent_share, came_share, "whole")
            shared_ref[mine] = share_ref[...]
            all_sums[mine] = total
            team_finish(sums, all_sums, sent_sum, came_sum, "whole")
            total = all_sums[0] + all_sums[1] + all_sums[2] + all_sums[3]
            columns = jnp.concatenate([total, jnp.zeros((120, longitudes), jnp.float32)], axis=0).T
        else:
            blank = jnp.zeros((120, 128), jnp.float32)
            columns = jnp.concatenate(
                [jnp.concatenate([all_near[s], blank], axis=0).T[:quarter] for s in range(4)], axis=0
            )
        columns = columns * (1.0 / (4 * slot))
        for lat in range(rows):
            average = columns[:, lat : lat + 1]
            power = columns[:, rows + lat : rows + lat + 1]
            scaled = tokens(block, lat) - average
            scaled = scaled * lax.rsqrt(power - average * average + eps_norm)
            scaled = scaled * affine_ref[block, 0:1, :] + affine_ref[block, 2:3, :]
            normed[lat] = scaled
            spectrum = times(forward_ref[...], scaled)
            upper, lower = spectrum[:half], spectrum[half:]
            rest = jnp.where(first_half, upper[:, 128:], lower[:, 128:])
            parts = (upper[:, :128], lower[:, :128], rest)
            for part in range(3):
                for wave in range(each):
                    spread(lat, wave, part, parts[part][wave * bands : (wave + 1) * bands])
        band_exchange(send_a, got_a.at[block], sent_a.at[block], came_a.at[block], while_first)
        pieces = []
        for wave in range(each):
            for part in range(3):
                pieces.append(
                    jnp.concatenate([collect(lat, wave, part) for lat in range(rows)], axis=0)
                )
        spectrum = jnp.concatenate(pieces, axis=1).astype(jnp.bfloat16)
        turned_all = times(across_ref[...], spectrum)

        def combine(both, wave, direction):
            base = wave * 384
            cosine, sine = both[:latitudes, base : base + 384], both[latitudes:, base : base + 384]
            real = cosine[:, :128] + direction * sine[:, 128:256]
            imag = cosine[:, 128:256] - direction * sine[:, :128]
            rest = cosine[:, 256:] + (direction * sign) * swap(sine[:, 256:])
            return real, imag, rest

        rows_mixed = jnp.concatenate(
            [jnp.concatenate(combine(turned_all, wave, 1.0), axis=1) for wave in range(each)], axis=0
        )
        hidden = times(rows_mixed, mix_ref[block, 0])
        hidden = jnp.maximum(hidden + offset_ref[block, 0:1, :], 0.0)
        mixed = times(hidden, mix_ref[block, 1])
        mixed = soft_shrink(mixed + offset_ref[block, 1:2, :])
        mixed = jnp.concatenate(
            [mixed[wave * latitudes : (wave + 1) * latitudes] for wave in range(each)], axis=1
        )
        turned_back = times(back_ref[...], mixed)
        for wave in range(each):
            parts = combine(turned_back, wave, -1.0)
            for part in range(3):
                for lat in range(rows):
                    spread(lat, wave, part, parts[part][lat * bands : (lat + 1) * bands])
        band_exchange(send_b, got_b.at[block], sent_b.at[block], came_b.at[block], while_second)
        for lat in range(rows):
            real, imag, rest = (
                jnp.concatenate([collect(lat, wave, part) for wave in range(each)], axis=0)
                for part in range(3)
            )
            right = jnp.concatenate(
                [
                    jnp.concatenate([real, rest], axis=1),
                    jnp.concatenate([imag, swap(rest)], axis=1),
                ],
                axis=0,
            ).astype(jnp.bfloat16)
            restored = times(inverse_ref[...], right)
            result = tokens(block, lat) + restored + normed[lat]
            for s in range(4):
                piece = result[s * quarter : (s + 1) * quarter]
                tail = piece[:, 128:]
                tail = jnp.where(first_half, tail[:middle], swap(tail[middle:]))
                after[s % 2, s // 2, lat, :quarter] = piece[:, :128].astype(jnp.bfloat16)
                after[s % 2, s // 2, lat, quarter:] = tail.astype(jnp.bfloat16)
        for turn in range(2):
            for step in range(1, 4):
                out_copy(block, turn, step, False).start()
        token[block, mine] = after[tile]
        for i in range(2):
            own_loads[2 * block + i].wait()
            sibling_loads[2 * block + i].wait()

    def pair(left, right):
        return jnp.concatenate(
            [jnp.where(first_half, left, swap(right)), jnp.where(first_half, swap(left), right)], 0
        )

    def unpair(both):
        top, low = both[:middle], both[middle:]
        return jnp.where(first_half, top, swap(low)), jnp.where(first_half, swap(top), low)

    def pack(block_rows, target):
        tails = unpair(block_rows[:, 512:640]) + unpair(block_rows[:, 640:])
        for s in range(4):
            place = target(s)
            place[:quarter] = block_rows[:, s * 128 : (s + 1) * 128].astype(jnp.bfloat16)
            place[quarter:] = tails[s].astype(jnp.bfloat16)

    def lanes_of(slices):
        heads = [p[:quarter] for p in slices]
        tails = [p[quarter:] for p in slices]
        return jnp.concatenate(heads + [pair(*tails[:2]), pair(*tails[2:])], axis=1)

    def reorder(values):
        t = [values[:, i * 128 : (i + 1) * 128] for i in range(6)]

        def inner(a, b):
            return jnp.where(first_half, swap(a), swap(b)), jnp.where(first_half, a, b)

        one, tails_a = inner(t[1], t[2])
        three, tails_b = inner(t[4], t[5])
        return jnp.concatenate([t[0], one, t[3], three, tails_a, tails_b], axis=1)

    row_spans = [(s * slot, 128) for s in range(4)] + [(s * slot + 128, slot - 128) for s in range(4)]

    def mlp(block, which_quarter):
        for lat in range(rows):
            slices = [token[block, s, which_quarter, lat].astype(jnp.float32) for s in range(4)]
            stream[lat * quarter : (lat + 1) * quarter] = lanes_of(slices)
        values = stream[...]
        normal = layer_norm(values, order_ref[block, 1:2, :], order_ref[block, 3:4, :])
        normal = normal.astype(jnp.bfloat16)
        wide = w_in.shape[3]
        for part in range(2):

            def piece(i, carry):
                at = pl.multiple_of(i * 256, 256)
                weight = jnp.concatenate(
                    [w_in[block, part, pl.ds(a, n), pl.ds(at, 256)] for a, n in row_spans], axis=0
                )
                z = jnp.dot(normal, weight, preferred_element_type=jnp.float32)
                hidden_ref[:, pl.ds(part * wide + at, 256)] = gelu(z).astype(jnp.bfloat16)
                return carry

            lax.fori_loop(0, wide // 256, piece, 0)
        total = jnp.dot(hidden_ref[:, :wide], w_out[block, 0], preferred_element_type=jnp.float32)
        total = total + jnp.dot(
            hidden_ref[:, wide:], w_out[block, 1], preferred_element_type=jnp.float32
        )
        total_ref[...] = reorder(total)

    zeros = functools.partial(jnp.zeros, dtype=jnp.float32)
    for block in range(2):
        both = jnp.concatenate([gain_ref[block], shift_ref[block], zeros((4, 4 * slot))], axis=0)
        order_ref[block] = reorder(both)
        head = order_ref[block, :, pl.ds(pl.multiple_of(mine * 128, 128), 128)]
        tail = order_ref[block, :, pl.ds(pl.multiple_of(512 + comp * 128, 128), 128)]
        tail = jnp.where(tile == 0, tail, swap(tail))
        tail = jnp.where(first_half, tail, swap(tail))
        affine_ref[block] = jnp.concatenate([head, tail], axis=1)
    share_ref[...] = zeros(share_ref.shape)
    share_ref[0:8, :slot] = flux_head_ref[...].astype(jnp.float32)
    for lat in range(rows):
        values = x_ref[lat].astype(jnp.float32)
        turned_ref[lat] = jnp.concatenate([values, values[128:]], axis=0).T
    for f in range(4):
        for a in range(2):
            for e in range(2):
                at, row = 8 + e * 16 + a * 8 + f, f * 4 + a * 2 + e
                share_ref[at : at + 1, :slot] = patch_ref[row : row + 1, :]
    mask_ref[...] = zeros(mask_ref.shape)
    mask_ref[: 2 * rows, :cells] = sea_ref[...].astype(jnp.float32)
    ext_rows = 2 * rows + 6

    def prepare_products():
        for block in range(2):
            for sublayer in range(2):

                def placed(weight):
                    width = weight.shape[1]
                    wide = jnp.concatenate([weight, zeros((slot, 128 - width))], axis=1)
                    moved = pltpu.roll(wide[width:], width, 1)
                    low = jnp.where(lane >= width, moved, 0.0)
                    high = jnp.where(first_half, moved, 0.0)
                    return (
                        jnp.concatenate([wide[:width], low], axis=0),
                        jnp.concatenate([zeros((width, 128)), high], axis=0),
                    )

                real, real_tail = placed(weight_ref[block, sublayer, 0])
                imag, imag_tail = placed(weight_ref[block, sublayer, 1])
                upper = jnp.concatenate([real, imag, real_tail + swap(imag_tail)], axis=1)
                lower = jnp.concatenate([-imag, real, swap(real_tail) - imag_tail], axis=1)
                mix_ref[block, sublayer] = jnp.concatenate(
                    [upper[:128], lower[:128], upper[128:], lower[128:]], axis=0
                ).astype(jnp.bfloat16)
                bias = bias_ref[block, sublayer]
                tail = jnp.concatenate([bias[:, 128:], bias[:, 128:]], axis=1)
                offset_ref[block, sublayer : sublayer + 1, :] = jnp.concatenate(
                    [bias[0:1, :128], bias[1:2, :128], jnp.where(first_half, tail[0:1], tail[1:2])], axis=1
                )
        level_ref[...] = zeros(level_ref.shape)
        for level in range(rows + 4):
            level_ref[level * 8 : level * 8 + 8, level * 256 : (level + 1) * 256] = flux_embed_ref[...]
        spread_ref[0], spread_ref[1] = split_bf16(level_ref[...])
        fields = jnp.concatenate([field_head_ref[...], zeros((4, 256))], axis=0)
        field_ref[...] = jnp.concatenate(thirds(fields), axis=0)

    def mask_rows(b, c):
        whole = mask_ref[...] if (b, c) == (0, 0) else masks_in[directions.index((b, c))]
        whole = whole[:, 128:] if c < 0 else whole[:, :128] if c > 0 else whole
        return whole[2 * rows - 3 : 2 * rows] if b < 0 else whole[:3] if b > 0 else whole[: 2 * rows]

    def prepare_masks():
        for copy in near_landings(*mask_args) + near_landings(*cell_args):
            copy.wait()
        masks = jnp.concatenate(
            [jnp.concatenate([mask_rows(b, c) for c in (-1, 0, 1)], axis=1) for b in (-1, 0, 1)]
            + [jnp.zeros((16 - ext_rows, 512), jnp.float32)],
            axis=0,
        )
        seen_masks[...] = across_rows(seen_ref[...], masks.astype(jnp.bfloat16))
        own_masks[...] = jnp.concatenate([mask_ref[...], zeros((120, 256))], axis=0).T

    spectral_filter(0, prepare_products, prepare_masks)
    team_finish(share_ref, shared_ref, sent_share, came_share, "whole")
    copy = pltpu.make_async_remote_copy(
        src_ref=half_out,
        dst_ref=half_in,
        send_sem=sent_half.at[0],
        recv_sem=came_half.at[0],
        device_id={"comp": 1 - comp},
        device_id_type=MESH,
    )

    def halves(i, carry):
        for step in range(1, 4):
            out_copy(0, i, step, True).wait()
        mlp(0, lax.rem(1 - comp + i, 2))

        @pl.when(i == 0)
        def _():
            half_out[...] = total_ref[...].astype(jnp.bfloat16)
            copy.start()

        return carry

    lax.fori_loop(0, 2, halves, 0)
    copy.wait()
    first = stream[...] + total_ref[...] + half_in[...].astype(jnp.float32)
    first = first.astype(jnp.bfloat16)
    stream[...] = first.astype(jnp.float32)

    small = [shared_ref[s] for s in range(4)]
    tails = [s[:, 128:] for s in small]
    whole = jnp.concatenate(
        [s[:, :128] for s in small]
        + [jnp.where(first_half, tails[i], swap(tails[i + 1])) for i in (0, 2)],
        axis=1,
    )
    head, embed = whole[:8].astype(jnp.bfloat16), whole[8:]
    for lat in range(rows):
        flux = across_rows(head, first[lat * quarter : (lat + 1) * quarter])
        flux_ref[lat] = jnp.concatenate([flux, jnp.zeros((8, 128 - quarter), jnp.float32)], axis=1)
    for copy in near_copies(*flux_args):
        copy.start()
    for copy in near_landings(*flux_args):
        copy.wait()

    def flux_at(lat, c):
        b = -1 if lat < 0 else 1 if lat >= rows else 0
        if (b, c) == (0, 0):
            return flux_ref[lat]
        return flux_in[directions.index((b, c)), lat % rows]

    ext_lats = range(-2, rows + 2)
    laid = jnp.concatenate(
        [jnp.concatenate([flux_at(lat, c) for c in (-1, 0, 1)], axis=1) for lat in ext_lats]
        + [jnp.zeros((128 - 8 * len(ext_lats), 384), jnp.float32)],
        axis=0,
    )
    raised = across_rows(pick_ref[...], jnp.concatenate(thirds(laid), axis=0))
    raised = raised[:, :128] + raised[:, 128:256] + raised[:, 256:]
    forcing = product(split_bf16(raised), (spread_ref[0], spread_ref[1]))

    for row in range(ext_rows):
        b = -1 if row < 3 else 1 if row >= 2 * rows + 3 else 0
        at = row if b < 0 else row - 3 if b == 0 else row - 2 * rows - 3
        sources = (
            cols_in[0, at] if b == 0 else corner_in[0 if b < 0 else 1, 0, at],
            ocean_ref[at] if b == 0 else rows_in[0 if b < 0 else 1, at],
            cols_in[1, at] if b == 0 else corner_in[0 if b < 0 else 1, 1, at],
        )
        sources = [s.astype(jnp.float32) for s in sources]
        state = jnp.concatenate([sources[0][8:], sources[1], sources[2][:8]], axis=0)
        level = (row - 3) // 2 + 2
        start = state + seen_masks[:, row : row + 1] * forcing[:, level * 256 : (level + 1) * 256]
        start = start.astype(jnp.bfloat16).astype(jnp.float32)
        if b:
            inside = jnp.where(me > 0, 1.0, 0.0) if b < 0 else jnp.where(me < bands - 1, 1.0, 0.0)
            start = start * inside
        for part in range(2):
            tile_ref[part, row] = start[:, part * 128 : (part + 1) * 128]

    for part in range(2):
        span = slice(part * 128, (part + 1) * 128)

        def strip(i, carry):
            at = pl.multiple_of(i * 16, 16)
            totals = [jnp.zeros((16, 128), jnp.float32) for _ in range(2 * rows)]
            for e in range(7):
                for row in range(ext_rows):
                    values = tile_ref[part, row, pl.ds(at + 5 + e, 16), :]
                    for a in range(7):
                        if 0 <= row - a < 2 * rows:
                            tap = depth_ref[a, e : e + 1, span]
                            totals[row - a] = totals[row - a] + values * tap
            for row in range(2 * rows):
                conv_ref[row, pl.ds(at, 16), span] = totals[row]
            return carry

        lax.fori_loop(0, cells // 16, strip, 0)

    for start_row in range(0, 2 * rows, 2):
        values = conv_ref[start_row : start_row + 2].reshape(2 * cells, 256)
        normal = layer_norm(values, ocean_gain_ref[...], ocean_shift_ref[...])
        normal = normal.astype(jnp.bfloat16)

        def piece(i, carry):
            at = pl.multiple_of(i * 256, 256)
            z = jnp.dot(normal, ocean_in_ref[:, pl.ds(at, 256)], preferred_element_type=jnp.float32)
            wave_ref[:, pl.ds(at, 256)] = gelu(z).astype(jnp.bfloat16)
            return carry

        lax.fori_loop(0, ocean_in_ref.shape[1] // 256, piece, 0)
        update = jnp.dot(wave_ref[...], ocean_out_ref[...], preferred_element_type=jnp.float32)
        update = update * layer_ref[...]
        for row in range(start_row, start_row + 2):
            begin = jnp.concatenate([tile_ref[part, row + 3, 8 : 8 + cells] for part in range(2)], axis=1)
            change = update[(row - start_row) * cells : (row - start_row + 1) * cells]
            fresh = (begin + own_masks[:cells, row : row + 1] * change).astype(jnp.bfloat16)
            next_ref[row] = fresh
            field = across_rows(field_ref[...], fresh)
            field = (field[:8] + field[8:16] + field[16:24]) * mask_ref[row : row + 1, :cells]
            flat_ref[row] = field
            surface_ref[row] = field[:4]

    near = zeros((8, quarter))
    for lat in range(rows):
        both = jnp.concatenate([flat_ref[2 * lat], flat_ref[2 * lat + 1]], axis=0)
        patch = across_rows(split_ref[...], jnp.concatenate(thirds(both), axis=0))
        patch = patch[:, :16] + patch[:, 16:32] + patch[:, 32:48]
        total = stream[lat * quarter : (lat + 1) * quarter]
        for e in range(2):
            total = total + product(
                split_bf16(patch[e * quarter : (e + 1) * quarter]),
                split_bf16(embed[e * 16 : (e + 1) * 16]),
            )
        pack(total, lambda s, lat=lat: middle_out.at[s, lat])
        rounded = total.astype(jnp.bfloat16)
        wide = rounded.astype(jnp.float32)
        high, low = split_bf16(wide * wide)
        every = jnp.ones((8, 4 * slot), jnp.bfloat16)
        plain, power = across_rows(every, rounded), across_rows(every, high) + across_rows(every, low)
        row_index = lax.broadcasted_iota(jnp.int32, (8, quarter), 0)
        near = near + jnp.where(row_index == lat, plain, 0.0)
        near = near + jnp.where(row_index == rows + lat, power, 0.0)
    near_sums[...] = jnp.concatenate([near, zeros((8, 128 - quarter))], axis=1)
    near_args = (near_sums, all_near, sent_near, came_near, "whole")
    team_exchange(*near_args)
    all_near[mine] = near_sums[...]
    args = (middle_out, middle_in, sent_middle, came_middle, "each")
    team_exchange(*args)
    middle_in[mine] = middle_out[mine]
    team_finish(*args)
    team_finish(*near_args)

    spectral_filter(1, lambda: None, lambda: None)

    def quarters(which_quarter, carry):
        for step in range(1, 4):
            out_copy(1, which_quarter, step, True).wait()
        mlp(1, which_quarter)
        for lat in range(rows):
            pack(
                total_ref[lat * quarter : (lat + 1) * quarter],
                lambda s, lat=lat: part_out.at[which_quarter, s, lat],
            )
        team_exchange(
            part_out.at[which_quarter], part_in.at[which_quarter],
            sent_part.at[which_quarter], came_part.at[which_quarter], "each",
        )
        part_in[which_quarter, mine] = part_out[which_quarter, mine]
        return carry

    lax.fori_loop(0, 2, quarters, 0)
    for which_quarter in range(2):
        team_finish(
            part_out.at[which_quarter], part_in.at[which_quarter],
            sent_part.at[which_quarter], came_part.at[which_quarter], "each",
        )
        for half_of in range(2):
            for lat in range(rows):
                piece = after[half_of, which_quarter, lat].astype(jnp.float32)
                piece = piece + part_in[which_quarter, half_of, lat].astype(jnp.float32)
                piece = piece + part_in[which_quarter, 2 + half_of, lat].astype(jnp.float32)
                tail = piece[quarter:]
                at = (2 * which_quarter + half_of) * quarter
                tail = jnp.concatenate([tail, swap(tail)], axis=0)
                atmosphere_ref[lat, at : at + quarter, :128] = piece[:quarter].astype(jnp.bfloat16)
                atmosphere_ref[lat, at : at + quarter, 128:] = tail[:, : slot - 128].astype(
                    jnp.bfloat16
                )


def on_device(
    atmosphere, spec_weight, spec_bias, norm_gain, norm_shift, fc_in, fc_out, flux_head, flux_embed,
    ocean_state, sea_mask, depth_kernel, ocean_gain, ocean_shift, ocean_in, ocean_out, layer_scale,
    field_head, patch_embed,
):
    bands = lax.axis_size("band")
    rows, longitudes, slot = atmosphere.shape
    quarter = longitudes // 4
    count = rows * quarter
    latitudes = rows * bands
    channels, wide = fc_in.shape[1:]
    packed = quarter * slot // 128
    cells, ocean_channels = ocean_state.shape[1:]
    waves = ocean_in.shape[1]

    inside, outside = pl.BlockSpec(memory_space=pltpu.VMEM), pl.BlockSpec(memory_space=pl.ANY)
    arguments = [
        atmosphere.transpose(0, 2, 1), spec_weight, spec_bias, norm_gain, norm_shift, fc_in, fc_out,
        flux_head.T,
        flux_embed, ocean_state, sea_mask, depth_kernel, ocean_gain[None], ocean_shift[None],
        ocean_in, ocean_out, layer_scale[None], field_head.T, patch_embed,
        *transforms(latitudes, longitudes, bands), *ocean_selectors(quarter),
    ]
    specs = [inside] * 5 + [outside] * 2 + [inside] * (len(arguments) - 7)
    levels = (rows + 4) * ocean_channels
    narrow, single = jnp.bfloat16, jnp.float32

    def dma(*shape):
        return pltpu.SemaphoreType.DMA(shape)

    chunks = (bands, 32, 128)
    scratch = [
        pltpu.VMEM((rows, longitudes, 256), single),
        pltpu.VMEM((2, 2, rows, packed, 128), narrow),
        pltpu.VMEM((2, 4, 2, rows, packed, 128), narrow),
        pltpu.VMEM((bands * 32 + 32, 128), single),
        pltpu.VMEM((bands * 32 + 32, 128), single),
        pltpu.VMEM((8, longitudes), single),
        pltpu.VMEM((4, 8, longitudes), single),
        pltpu.VMEM(chunks, narrow),
        pltpu.VMEM((2,) + chunks, narrow),
        pltpu.VMEM(chunks, narrow),
        pltpu.VMEM((2,) + chunks, narrow),
        pltpu.VMEM((2, 2, channels, wide), narrow),
        pltpu.VMEM((2, 2, wide, channels), narrow),
        pltpu.VMEM((count, channels), single),
        pltpu.VMEM((count, 2 * wide), narrow),
        pltpu.VMEM((count, channels), narrow),
        pltpu.VMEM((count, channels), narrow),
        pltpu.VMEM((2, 4, rows, packed, 128), narrow),
        pltpu.VMEM((2, 4, rows, packed, 128), narrow),
        pltpu.VMEM((4, 40, 256), single),
        pltpu.VMEM((2, 3, cells, ocean_channels), narrow),
        pltpu.VMEM((2, 2 * rows, 16, ocean_channels), narrow),
        pltpu.VMEM((2, 2, 3, 16, ocean_channels), narrow),
        pltpu.VMEM((8, 8, 256), single),
        pltpu.VMEM((rows, 8, 128), single),
        pltpu.VMEM((8, rows, 8, 128), single),
        pltpu.VMEM((2, 2 * rows + 6, cells + 16, 128), single),
        pltpu.VMEM((2 * rows, cells, ocean_channels), single),
        pltpu.VMEM((2 * cells, waves), narrow),
        pltpu.VMEM((4, rows, packed, 128), narrow),
        pltpu.VMEM((4, rows, packed, 128), narrow),
        pltpu.VMEM((2, 8, channels), single),
        pltpu.VMEM((2, 8, 256), single),
        pltpu.VMEM((2, 2, 2 * slot, 2 * slot), narrow),
        pltpu.VMEM((2, 8, 2 * slot), single),
        pltpu.VMEM((40, 256), single),
        pltpu.VMEM((8, 256), single),
        pltpu.VMEM((128, levels), single),
        pltpu.VMEM((2, 128, levels), narrow),
        pltpu.VMEM((24, ocean_channels), narrow),
        pltpu.VMEM((count, channels), single),
        pltpu.VMEM((rows, longitudes, 256), single),
        pltpu.VMEM((2 * rows, 8, cells), single),
        pltpu.VMEM((8, 128), single),
        pltpu.VMEM((4, 8, 128), single),
        pltpu.VMEM((cells + 16, 16), single),
        pltpu.VMEM((256, 128), single),
        dma(4), dma(4), dma(2, bands), dma(2, bands), dma(2, bands), dma(2, bands),
        dma(2, 2, 4), dma(2, 2, 4), dma(1), dma(1), dma(2, 4), dma(2, 4), dma(2, 2), dma(2, 2), dma(2, 2),
        dma(4), dma(4), dma(8), dma(8), dma(8), dma(8), dma(8), dma(8), dma(4), dma(4),
        dma(4), dma(4),
    ]
    atmosphere_next, ocean_next, surface = pl.pallas_call(
        functools.partial(step_kernel, bands),
        out_shape=(
            jax.ShapeDtypeStruct(atmosphere.shape, narrow),
            jax.ShapeDtypeStruct(ocean_state.shape, narrow),
            jax.ShapeDtypeStruct((2 * rows, 4, cells), single),
        ),
        in_specs=specs,
        out_specs=(inside,) * 3,
        scratch_shapes=scratch,
        compiler_params=pltpu.CompilerParams(
            collective_id=0, has_side_effects=True, vmem_limit_bytes=63 << 20
        ),
    )(*arguments)
    return (atmosphere_next, ocean_next, surface.transpose(0, 2, 1))


def solution(mesh):
    placed = (
        P("band", None, ("comp", "tile")),
        P(None, None, None, ("comp", "tile"), None),
        P(None, None, None, ("comp", "tile")),
        P(),
        P(),
        P(None, None, ("comp", "tile")),
        P(None, ("comp", "tile"), None),
        P(("comp", "tile"), None),
        P(),
        P("band", ("comp", "tile"), None),
        P("band", ("comp", "tile")),
        P(),
        P(),
        P(),
        P(),
        P(),
        P(),
        P(),
        P(None, ("comp", "tile")),
    )
    return jax.shard_map(
        on_device,
        mesh=mesh,
        in_specs=placed,
        out_specs=(
            P("band", None, ("comp", "tile")),
            P("band", ("comp", "tile"), None),
            P("band", ("comp", "tile"), None),
        ),
        check_vma=False,
    )
```

```python
import functools
import math

import jax
import jax.numpy as jnp
import numpy as np
from jax import lax
from jax.experimental import pallas as pl
from jax.experimental.pallas import tpu as pltpu
from jax.sharding import PartitionSpec as P

MESH = pl.DeviceIdType.MESH
full_precision = lax.Precision.HIGHEST
eps_norm = 1e-06
shrink_level = 0.01


def layer_norm(values, scaling, offset):
    average = jnp.mean(values, axis=-1, keepdims=True)
    squares = jnp.mean(values * values, axis=-1, keepdims=True)
    variance = squares - average * average
    return (values - average) * lax.rsqrt(variance + eps_norm) * scaling + offset


def soft_shrink(values):
    zeros = jnp.zeros_like(values)
    return jnp.where(
        values > shrink_level,
        values - shrink_level,
        jnp.where(values < -shrink_level, values + shrink_level, zeros),
    )


def split_bf16(array):
    high = array.astype(jnp.bfloat16)
    return high, (array - high.astype(jnp.float32)).astype(jnp.bfloat16)


def transforms(latitudes, longitudes, bands):
    kept = longitudes // 2
    each, rows = kept // bands, latitudes // bands
    waves = np.arange(kept).reshape(bands, each).T.reshape(-1)
    lats = np.arange(latitudes).reshape(bands, rows).T.reshape(-1)
    lon = np.outer(waves, np.arange(longitudes)) % longitudes * (2.0 * math.pi / longitudes)
    lat = np.outer(np.arange(latitudes), lats) % latitudes * (2.0 * math.pi / latitudes)
    forward = np.concatenate([np.cos(lon), -np.sin(lon)], 0) / math.sqrt(longitudes)
    across = np.stack([np.cos(lat), np.sin(lat)], 0) / math.sqrt(latitudes)
    weight = np.where(waves == 0, 1.0, 2.0)[:, None]
    inverse = np.concatenate([np.cos(lon) * weight, -np.sin(lon) * weight], 0).T
    mats = (
        forward,
        across.reshape(2 * latitudes, latitudes),
        across.transpose(0, 2, 1).reshape(2 * latitudes, latitudes),
        inverse / math.sqrt(longitudes),
    )
    return [jnp.asarray(m, jnp.bfloat16) for m in mats]


def times(left, right):
    return jnp.dot(
        left.astype(jnp.bfloat16), right.astype(jnp.bfloat16), preferred_element_type=jnp.float32
    )


def product(left, right):
    total = None
    for a, b in ((0, 0), (1, 0), (0, 1)):
        if a < len(left) and b < len(right):
            term = jnp.dot(left[a], right[b], preferred_element_type=jnp.float32)
            total = term if total is None else total + term
    return total


directions = [(b, c) for b in (-1, 0, 1) for c in (-1, 0, 1) if (b, c) != (0, 0)]


def ocean_selectors(quarter):
    columns = np.arange(-8, 2 * quarter + 8)
    pick = np.zeros((len(columns), 384), np.float32)
    seen = np.zeros((len(columns), 512), np.float32)
    for i, column in enumerate(columns):
        if not -3 <= column < 2 * quarter + 3:
            continue
        token = column // 2
        side = 0 if token < 0 else 2 if token >= quarter else 1
        pick[i, side * 128 + token % quarter] = 1
        inner = column % (2 * quarter)
        seen[i, inner - 128 if column < 0 else 384 + inner if column >= 2 * quarter else 128 + inner] = 1
    split = np.zeros((2 * quarter, 2 * quarter), np.float32)
    for e in range(2):
        split[e * quarter + np.arange(quarter), 2 * np.arange(quarter) + e] = 1
    return (jnp.asarray(m, jnp.bfloat16) for m in (pick, seen, split))


def thirds(array):
    high = array.astype(jnp.bfloat16)
    rest = array - high.astype(jnp.float32)
    middle = rest.astype(jnp.bfloat16)
    return high, middle, (rest - middle.astype(jnp.float32)).astype(jnp.bfloat16)


def gelu(z):
    return 0.5 * z * (1.0 + lax.erf(z * math.sqrt(0.5)))


def step_kernel(bands, *refs):
    (
        x_ref, weight_ref, bias_ref, gain_ref, shift_ref, fc_in_ref, fc_out_ref, flux_head_ref,
        flux_embed_ref, ocean_ref, sea_ref, depth_ref, ocean_gain_ref, ocean_shift_ref,
        ocean_in_ref, ocean_out_ref, layer_ref, field_head_ref, patch_ref,
        forward_ref, across_ref, back_ref, inverse_ref, pick_ref, seen_ref, split_ref,
        atmosphere_ref, next_ref, surface_ref,
        normed, after, token, stage, landed, sums, all_sums, send_a, got_a, send_b, got_b,
        w_in, w_out, stream, hidden_ref, half_out, half_in, part_out, part_in, shared_ref,
        rows_in, cols_in, corner_in, masks_in, flux_ref, flux_in, tile_ref, conv_ref, wave_ref,
        middle_out, middle_in, order_ref, affine_ref, mix_ref, offset_ref, share_ref, mask_ref,
        level_ref, spread_ref, field_ref, total_ref, turned_ref, flat_ref, near_sums, all_near,
        seen_masks, own_masks,
        sent_sum, came_sum, sent_a, came_a, sent_b, came_b, sent_out, came_out,
        sent_half, came_half, sent_part, came_part, load, sent_load, came_load,
        sent_share, came_share, sent_cells, came_cells, sent_mask, came_mask, sent_flux, came_flux,
        sent_middle, came_middle, sent_near, came_near,
    ) = refs
    rows, slot, longitudes = x_ref.shape
    quarter = longitudes // 4
    middle = quarter // 2
    latitudes = rows * bands
    each = longitudes // 2 // bands
    cells = ocean_ref.shape[1]
    me = lax.axis_index("band")
    comp, tile = lax.axis_index("comp"), lax.axis_index("tile")
    mine = comp * 2 + tile

    def member(step):
        return lax.rem(mine + step, 4)

    def team_id(index):
        return {"comp": lax.div(index, 2), "tile": lax.rem(index, 2)}

    def near_id(b, c):
        index = lax.rem(mine + c + 4, 4)
        return {"band": lax.rem(me + b + bands, bands), **team_id(index)}

    own_loads = [
        pltpu.make_async_copy(source.at[block], target.at[block, 0], load.at[block, i])
        for block in range(2)
        for i, (source, target) in enumerate(((fc_in_ref, w_in), (fc_out_ref, w_out)))
    ]
    sibling_loads = [
        pltpu.make_async_remote_copy(
            src_ref=source.at[block],
            dst_ref=target.at[block, 1],
            send_sem=sent_load.at[block, i],
            recv_sem=came_load.at[block, i],
            device_id={"tile": 1 - tile},
            device_id_type=MESH,
        )
        for block in range(2)
        for i, (source, target) in enumerate(((fc_in_ref, w_in), (fc_out_ref, w_out)))
    ]
    barrier = pltpu.get_barrier_semaphore()

    def greet(step, carry):
        pl.semaphore_signal(
            barrier, inc=1, device_id={"band": lax.rem(me + step, bands)}, device_id_type=MESH
        )
        return carry

    for step in range(1, 4):
        pl.semaphore_signal(barrier, inc=1, device_id=team_id(member(step)), device_id_type=MESH)
    for b, c in directions:
        if b and c:
            pl.semaphore_signal(barrier, inc=1, device_id=near_id(b, c), device_id_type=MESH)
    lax.fori_loop(1, bands, greet, 0)
    for copy in own_loads:
        copy.start()

    def near_copies(source_of, target_of, sent, came):
        copies = []
        for d, (b, c) in enumerate(directions):
            copies.append(
                pltpu.make_async_remote_copy(
                    src_ref=source_of(b, c),
                    dst_ref=target_of(-b, -c),
                    send_sem=sent.at[d],
                    recv_sem=came.at[directions.index((-b, -c))],
                    device_id=near_id(b, c),
                    device_id_type=MESH,
                )
            )
        return copies

    def near_landings(source_of, target_of, sent, came):
        copies = []
        for d, (b, c) in enumerate(directions):
            copies.append(
                pltpu.make_async_remote_copy(
                    src_ref=source_of(b, c),
                    dst_ref=target_of(b, c),
                    send_sem=sent.at[d],
                    recv_sem=came.at[d],
                    device_id=near_id(b, c),
                    device_id_type=MESH,
                )
            )
        return copies

    def cells_from(b, c):
        row = pl.ds(0, 2 * rows) if b == 0 else pl.ds(2 * rows - 3 if b > 0 else 0, 3)
        column = pl.ds(0, cells) if c == 0 else pl.ds(cells - 16 if c > 0 else 0, 16)
        return ocean_ref.at[row, column]

    def cells_to(b, c):
        if c == 0:
            return rows_in.at[0 if b < 0 else 1]
        if b == 0:
            return cols_in.at[0 if c < 0 else 1]
        return corner_in.at[0 if b < 0 else 1, 0 if c < 0 else 1]

    cell_args = (cells_from, cells_to, sent_cells, came_cells)
    mask_args = (
        lambda b, c: mask_ref, lambda b, c: masks_in.at[directions.index((b, c))], sent_mask, came_mask
    )
    flux_args = (
        lambda b, c: flux_ref, lambda b, c: flux_in.at[directions.index((b, c))], sent_flux, came_flux
    )

    def team_copy(source, target, sent, came, step, pick, landing):
        index = member(step)
        chosen = {"whole": lambda: source, "each": lambda: source.at[index]}[pick]()
        place = index if landing else mine
        return pltpu.make_async_remote_copy(
            src_ref=chosen,
            dst_ref=target.at[place],
            send_sem=sent.at[index],
            recv_sem=came.at[place],
            device_id=team_id(index),
            device_id_type=MESH,
        )

    def team_exchange(source, target, sent, came, pick):
        for step in range(1, 4):
            team_copy(source, target, sent, came, step, pick, False).start()

    def team_finish(source, target, sent, came, pick):
        for step in range(1, 4):
            team_copy(source, target, sent, came, step, pick, True).wait()

    def out_copy(block, turn, lat, step, landing):
        index = member(step)
        place = index if landing else mine
        wanted = turn
        if block == 0:
            wanted = lax.rem(1 - (comp if landing else lax.div(index, 2)) + turn, 2)
        return pltpu.make_async_remote_copy(
            src_ref=after.at[lax.rem(index, 2), wanted, lat],
            dst_ref=token.at[block, place, wanted, lat],
            send_sem=sent_out.at[block, turn, lat, index],
            recv_sem=came_out.at[block, turn, lat, place],
            device_id=team_id(index),
            device_id_type=MESH,
        )

    def band_peer(step):
        x = lax.rem(me // 16 + step // 16, bands // 16)
        y = lax.rem(lax.rem(me // 8, 2) + lax.rem(step // 8, 2), 2)
        return x * 16 + y * 8 + lax.rem(lax.rem(me, 8) + lax.rem(step, 8), 8)

    def band_copy(source, target, sent, came, step, landing):
        index = band_peer(step)
        return pltpu.make_async_remote_copy(
            src_ref=source.at[index],
            dst_ref=target.at[index if landing else me],
            send_sem=sent.at[index],
            recv_sem=came.at[index if landing else me],
            device_id={"band": index},
            device_id_type=MESH,
        )

    def band_exchange(source, target, sent, came, meanwhile):
        source[...] = stage[: bands * 32].astype(jnp.bfloat16).reshape(source.shape)

        def go(step, carry):
            band_copy(source, target, sent, came, step, False).start()
            return carry

        lax.fori_loop(1, bands, go, 0)
        target[me] = source[me]
        meanwhile()

        def widen(index):
            at = pl.multiple_of(index * 32, 32)
            landed[pl.ds(at, 32), :] = target[index].astype(jnp.float32)

        widen(me)

        def come(step, carry):
            band_copy(source, target, sent, came, step, True).wait()
            widen(band_peer(step))
            return carry

        lax.fori_loop(1, bands, come, 0)

    lane = lax.broadcasted_iota(jnp.int32, (1, 128), 1)
    first_half = lane < slot - 128
    sign = jnp.where(first_half, 1.0, -1.0)
    half = longitudes // 2
    counted = jnp.ones((8, slot), jnp.bfloat16)
    which = lax.broadcasted_iota(jnp.int32, (8, longitudes), 0)
    turned = (((1,), (1,)), ((), ()))

    def across_rows(left, right):
        return lax.dot_general(left, right, turned, preferred_element_type=jnp.float32)

    def swap(values):
        return pltpu.roll(values, 64, 1)

    def doubled(tails):
        top = jnp.where(first_half, tails, swap(tails))
        low = jnp.where(first_half, swap(tails), tails)
        return jnp.concatenate([top, low], axis=0)

    def tokens(block, lat):
        if block == 0:
            return turned_ref[lat]
        pieces = [middle_in[lat, s].astype(jnp.float32) for s in range(4)]
        return jnp.concatenate(
            [jnp.concatenate([p[:quarter], doubled(p[quarter:])], axis=1) for p in pieces], axis=0
        )

    def spread(lat, wave, part, values):
        stage[pl.ds(part * 9 + lat * 3 + wave, bands, stride=32), :] = values

    def collect(lat, wave, part):
        return landed[pl.ds(part * 9 + lat * 3 + wave, bands, stride=32), :]

    def spectral_filter(block, while_first, while_second):
        if block == 0:
            total = jnp.zeros((8, longitudes), jnp.float32)
            for lat in range(rows):
                values = x_ref[lat].astype(jnp.float32)
                high, low = split_bf16(values * values)
                total = total + jnp.where(which == lat, times(counted, x_ref[lat]), 0.0)
                total = total + jnp.where(
                    which == rows + lat, times(counted, high) + times(counted, low), 0.0
                )
            sums[...] = total
            pl.semaphore_wait(barrier, bands - 1 + 3 + 4)
            team_exchange(sums, all_sums, sent_sum, came_sum, "whole")
            for copy in near_copies(*mask_args) + near_copies(*cell_args) + sibling_loads:
                copy.start()
            team_exchange(share_ref, shared_ref, sent_share, came_share, "whole")
            shared_ref[mine] = share_ref[...]
            all_sums[mine] = total
            team_finish(sums, all_sums, sent_sum, came_sum, "whole")
            total = all_sums[0] + all_sums[1] + all_sums[2] + all_sums[3]
            columns = jnp.concatenate([total, jnp.zeros((120, longitudes), jnp.float32)], axis=0).T
        else:
            blank = jnp.zeros((120, 128), jnp.float32)
            columns = jnp.concatenate(
                [jnp.concatenate([all_near[s], blank], axis=0).T[:quarter] for s in range(4)], axis=0
            )
        columns = columns * (1.0 / (4 * slot))
        for lat in range(rows):
            average = columns[:, lat : lat + 1]
            power = columns[:, rows + lat : rows + lat + 1]
            scaled = tokens(block, lat) - average
            scaled = scaled * lax.rsqrt(power - average * average + eps_norm)
            scaled = scaled * affine_ref[block, 0:1, :] + affine_ref[block, 2:3, :]
            normed[lat] = scaled
            spectrum = times(forward_ref[...], scaled)
            upper, lower = spectrum[:half], spectrum[half:]
            rest = jnp.where(first_half, upper[:, 128:], lower[:, 128:])
            parts = (upper[:, :128], lower[:, :128], rest)
            for part in range(3):
                for wave in range(each):
                    spread(lat, wave, part, parts[part][wave * bands : (wave + 1) * bands])
        band_exchange(send_a, got_a.at[block], sent_a.at[block], came_a.at[block], while_first)
        pieces = []
        for wave in range(each):
            for part in range(3):
                pieces.append(
                    jnp.concatenate([collect(lat, wave, part) for lat in range(rows)], axis=0)
                )
        spectrum = jnp.concatenate(pieces, axis=1).astype(jnp.bfloat16)
        turned_all = times(across_ref[...], spectrum)

        def combine(both, wave, direction):
            base = wave * 384
            cosine, sine = both[:latitudes, base : base + 384], both[latitudes:, base : base + 384]
            real = cosine[:, :128] + direction * sine[:, 128:256]
            imag = cosine[:, 128:256] - direction * sine[:, :128]
            rest = cosine[:, 256:] + (direction * sign) * swap(sine[:, 256:])
            return real, imag, rest

        rows_mixed = jnp.concatenate(
            [jnp.concatenate(combine(turned_all, wave, 1.0), axis=1) for wave in range(each)], axis=0
        )
        hidden = times(rows_mixed, mix_ref[block, 0])
        hidden = jnp.maximum(hidden + offset_ref[block, 0:1, :], 0.0)
        mixed = times(hidden, mix_ref[block, 1])
        mixed = soft_shrink(mixed + offset_ref[block, 1:2, :])
        mixed = jnp.concatenate(
            [mixed[wave * latitudes : (wave + 1) * latitudes] for wave in range(each)], axis=1
        )
        turned_back = times(back_ref[...], mixed)
        for wave in range(each):
            parts = combine(turned_back, wave, -1.0)
            for part in range(3):
                for lat in range(rows):
                    spread(lat, wave, part, parts[part][lat * bands : (lat + 1) * bands])
        band_exchange(send_b, got_b.at[block], sent_b.at[block], came_b.at[block], while_second)
        for lat in range(rows):
            real, imag, rest = (
                jnp.concatenate([collect(lat, wave, part) for wave in range(each)], axis=0)
                for part in range(3)
            )
            right = jnp.concatenate(
                [
                    jnp.concatenate([real, rest], axis=1),
                    jnp.concatenate([imag, swap(rest)], axis=1),
                ],
                axis=0,
            ).astype(jnp.bfloat16)
            restored = times(inverse_ref[...], right)
            result = tokens(block, lat) + restored + normed[lat]
            for s in range(4):
                piece = result[s * quarter : (s + 1) * quarter]
                tail = piece[:, 128:]
                tail = jnp.where(first_half, tail[:middle], swap(tail[middle:]))
                after[s % 2, s // 2, lat, :quarter] = piece[:, :128].astype(jnp.bfloat16)
                after[s % 2, s // 2, lat, quarter:] = tail.astype(jnp.bfloat16)
            for step in range(1, 4):
                out_copy(block, 0, lat, step, False).start()
        for lat in range(rows):
            for step in range(1, 4):
                out_copy(block, 1, lat, step, False).start()
        token[block, mine] = after[tile]
        for i in range(2):
            own_loads[2 * block + i].wait()
            sibling_loads[2 * block + i].wait()

    def pair(left, right):
        return jnp.concatenate(
            [jnp.where(first_half, left, swap(right)), jnp.where(first_half, swap(left), right)], 0
        )

    def unpair(both):
        top, low = both[:middle], both[middle:]
        return jnp.where(first_half, top, swap(low)), jnp.where(first_half, swap(top), low)

    def pack(block_rows, target):
        tails = unpair(block_rows[:, 512:640]) + unpair(block_rows[:, 640:])
        for s in range(4):
            place = target(s)
            place[:quarter] = block_rows[:, s * 128 : (s + 1) * 128].astype(jnp.bfloat16)
            place[quarter:] = tails[s].astype(jnp.bfloat16)

    def lanes_of(slices):
        heads = [p[:quarter] for p in slices]
        tails = [p[quarter:] for p in slices]
        return jnp.concatenate(heads + [pair(*tails[:2]), pair(*tails[2:])], axis=1)

    def reorder(values):
        t = [values[:, i * 128 : (i + 1) * 128] for i in range(6)]

        def inner(a, b):
            return jnp.where(first_half, swap(a), swap(b)), jnp.where(first_half, a, b)

        one, tails_a = inner(t[1], t[2])
        three, tails_b = inner(t[4], t[5])
        return jnp.concatenate([t[0], one, t[3], three, tails_a, tails_b], axis=1)

    row_spans = [(s * slot, 128) for s in range(4)] + [(s * slot + 128, slot - 128) for s in range(4)]

    def mlp(block, which_quarter):
        for lat in range(rows):
            slices = [token[block, s, which_quarter, lat].astype(jnp.float32) for s in range(4)]
            stream[lat * quarter : (lat + 1) * quarter] = lanes_of(slices)
        values = stream[...]
        normal = layer_norm(values, order_ref[block, 1:2, :], order_ref[block, 3:4, :])
        normal = normal.astype(jnp.bfloat16)
        wide = w_in.shape[3]
        for part in range(2):

            def piece(i, carry):
                at = pl.multiple_of(i * 256, 256)
                weight = jnp.concatenate(
                    [w_in[block, part, pl.ds(a, n), pl.ds(at, 256)] for a, n in row_spans], axis=0
                )
                z = jnp.dot(normal, weight, preferred_element_type=jnp.float32)
                hidden_ref[:, pl.ds(part * wide + at, 256)] = gelu(z).astype(jnp.bfloat16)
                return carry

            lax.fori_loop(0, wide // 256, piece, 0)
        total = jnp.dot(hidden_ref[:, :wide], w_out[block, 0], preferred_element_type=jnp.float32)
        total = total + jnp.dot(
            hidden_ref[:, wide:], w_out[block, 1], preferred_element_type=jnp.float32
        )
        total_ref[...] = reorder(total)

    zeros = functools.partial(jnp.zeros, dtype=jnp.float32)
    for block in range(2):
        both = jnp.concatenate([gain_ref[block], shift_ref[block], zeros((4, 4 * slot))], axis=0)
        order_ref[block] = reorder(both)
        head = order_ref[block, :, pl.ds(pl.multiple_of(mine * 128, 128), 128)]
        tail = order_ref[block, :, pl.ds(pl.multiple_of(512 + comp * 128, 128), 128)]
        tail = jnp.where(tile == 0, tail, swap(tail))
        tail = jnp.where(first_half, tail, swap(tail))
        affine_ref[block] = jnp.concatenate([head, tail], axis=1)
    share_ref[...] = zeros(share_ref.shape)
    share_ref[0:8, :slot] = flux_head_ref[...].astype(jnp.float32)
    for lat in range(rows):
        values = x_ref[lat].astype(jnp.float32)
        turned_ref[lat] = jnp.concatenate([values, values[128:]], axis=0).T
    for f in range(4):
        for a in range(2):
            for e in range(2):
                at, row = 8 + e * 16 + a * 8 + f, f * 4 + a * 2 + e
                share_ref[at : at + 1, :slot] = patch_ref[row : row + 1, :]
    mask_ref[...] = zeros(mask_ref.shape)
    mask_ref[: 2 * rows, :cells] = sea_ref[...].astype(jnp.float32)
    ext_rows = 2 * rows + 6

    def prepare_products():
        for block in range(2):
            for sublayer in range(2):

                def placed(weight):
                    width = weight.shape[1]
                    wide = jnp.concatenate([weight, zeros((slot, 128 - width))], axis=1)
                    moved = pltpu.roll(wide[width:], width, 1)
                    low = jnp.where(lane >= width, moved, 0.0)
                    high = jnp.where(first_half, moved, 0.0)
                    return (
                        jnp.concatenate([wide[:width], low], axis=0),
                        jnp.concatenate([zeros((width, 128)), high], axis=0),
                    )

                real, real_tail = placed(weight_ref[block, sublayer, 0])
                imag, imag_tail = placed(weight_ref[block, sublayer, 1])
                upper = jnp.concatenate([real, imag, real_tail + swap(imag_tail)], axis=1)
                lower = jnp.concatenate([-imag, real, swap(real_tail) - imag_tail], axis=1)
                mix_ref[block, sublayer] = jnp.concatenate(
                    [upper[:128], lower[:128], upper[128:], lower[128:]], axis=0
                ).astype(jnp.bfloat16)
                bias = bias_ref[block, sublayer]
                tail = jnp.concatenate([bias[:, 128:], bias[:, 128:]], axis=1)
                offset_ref[block, sublayer : sublayer + 1, :] = jnp.concatenate(
                    [bias[0:1, :128], bias[1:2, :128], jnp.where(first_half, tail[0:1], tail[1:2])], axis=1
                )
        level_ref[...] = zeros(level_ref.shape)
        for level in range(rows + 4):
            level_ref[level * 8 : level * 8 + 8, level * 256 : (level + 1) * 256] = flux_embed_ref[...]
        spread_ref[0], spread_ref[1] = split_bf16(level_ref[...])
        fields = jnp.concatenate([field_head_ref[...], zeros((4, 256))], axis=0)
        field_ref[...] = jnp.concatenate(thirds(fields), axis=0)

    def mask_rows(b, c):
        whole = mask_ref[...] if (b, c) == (0, 0) else masks_in[directions.index((b, c))]
        whole = whole[:, 128:] if c < 0 else whole[:, :128] if c > 0 else whole
        return whole[2 * rows - 3 : 2 * rows] if b < 0 else whole[:3] if b > 0 else whole[: 2 * rows]

    def prepare_masks():
        for copy in near_landings(*mask_args) + near_landings(*cell_args):
            copy.wait()
        masks = jnp.concatenate(
            [jnp.concatenate([mask_rows(b, c) for c in (-1, 0, 1)], axis=1) for b in (-1, 0, 1)]
            + [jnp.zeros((16 - ext_rows, 512), jnp.float32)],
            axis=0,
        )
        seen_masks[...] = across_rows(seen_ref[...], masks.astype(jnp.bfloat16))
        own_masks[...] = jnp.concatenate([mask_ref[...], zeros((120, 256))], axis=0).T

    spectral_filter(0, prepare_products, prepare_masks)
    team_finish(share_ref, shared_ref, sent_share, came_share, "whole")
    copy = pltpu.make_async_remote_copy(
        src_ref=half_out,
        dst_ref=half_in,
        send_sem=sent_half.at[0],
        recv_sem=came_half.at[0],
        device_id={"comp": 1 - comp},
        device_id_type=MESH,
    )

    def halves(i, carry):
        for lat in range(rows):
            for step in range(1, 4):
                out_copy(0, i, lat, step, True).wait()
        mlp(0, lax.rem(1 - comp + i, 2))

        @pl.when(i == 0)
        def _():
            half_out[...] = total_ref[...].astype(jnp.bfloat16)
            copy.start()

        return carry

    lax.fori_loop(0, 2, halves, 0)
    copy.wait()
    first = stream[...] + total_ref[...] + half_in[...].astype(jnp.float32)
    first = first.astype(jnp.bfloat16)
    stream[...] = first.astype(jnp.float32)

    small = [shared_ref[s] for s in range(4)]
    tails = [s[:, 128:] for s in small]
    whole = jnp.concatenate(
        [s[:, :128] for s in small]
        + [jnp.where(first_half, tails[i], swap(tails[i + 1])) for i in (0, 2)],
        axis=1,
    )
    head, embed = whole[:8].astype(jnp.bfloat16), whole[8:]
    for lat in range(rows):
        flux = across_rows(head, first[lat * quarter : (lat + 1) * quarter])
        flux_ref[lat] = jnp.concatenate([flux, jnp.zeros((8, 128 - quarter), jnp.float32)], axis=1)
    for copy in near_copies(*flux_args):
        copy.start()
    for copy in near_landings(*flux_args):
        copy.wait()

    def flux_at(lat, c):
        b = -1 if lat < 0 else 1 if lat >= rows else 0
        if (b, c) == (0, 0):
            return flux_ref[lat]
        return flux_in[directions.index((b, c)), lat % rows]

    ext_lats = range(-2, rows + 2)
    laid = jnp.concatenate(
        [jnp.concatenate([flux_at(lat, c) for c in (-1, 0, 1)], axis=1) for lat in ext_lats]
        + [jnp.zeros((128 - 8 * len(ext_lats), 384), jnp.float32)],
        axis=0,
    )
    raised = across_rows(pick_ref[...], jnp.concatenate(thirds(laid), axis=0))
    raised = raised[:, :128] + raised[:, 128:256] + raised[:, 256:]
    forcing = product(split_bf16(raised), (spread_ref[0], spread_ref[1]))

    for row in range(ext_rows):
        b = -1 if row < 3 else 1 if row >= 2 * rows + 3 else 0
        at = row if b < 0 else row - 3 if b == 0 else row - 2 * rows - 3
        sources = (
            cols_in[0, at] if b == 0 else corner_in[0 if b < 0 else 1, 0, at],
            ocean_ref[at] if b == 0 else rows_in[0 if b < 0 else 1, at],
            cols_in[1, at] if b == 0 else corner_in[0 if b < 0 else 1, 1, at],
        )
        sources = [s.astype(jnp.float32) for s in sources]
        state = jnp.concatenate([sources[0][8:], sources[1], sources[2][:8]], axis=0)
        level = (row - 3) // 2 + 2
        start = state + seen_masks[:, row : row + 1] * forcing[:, level * 256 : (level + 1) * 256]
        start = start.astype(jnp.bfloat16).astype(jnp.float32)
        if b:
            inside = jnp.where(me > 0, 1.0, 0.0) if b < 0 else jnp.where(me < bands - 1, 1.0, 0.0)
            start = start * inside
        for part in range(2):
            tile_ref[part, row] = start[:, part * 128 : (part + 1) * 128]

    for part in range(2):
        span = slice(part * 128, (part + 1) * 128)

        def strip(i, carry):
            at = pl.multiple_of(i * 16, 16)
            totals = [jnp.zeros((16, 128), jnp.float32) for _ in range(2 * rows)]
            for e in range(7):
                for row in range(ext_rows):
                    values = tile_ref[part, row, pl.ds(at + 5 + e, 16), :]
                    for a in range(7):
                        if 0 <= row - a < 2 * rows:
                            tap = depth_ref[a, e : e + 1, span]
                            totals[row - a] = totals[row - a] + values * tap
            for row in range(2 * rows):
                conv_ref[row, pl.ds(at, 16), span] = totals[row]
            return carry

        lax.fori_loop(0, cells // 16, strip, 0)

    for start_row in range(0, 2 * rows, 2):
        values = conv_ref[start_row : start_row + 2].reshape(2 * cells, 256)
        normal = layer_norm(values, ocean_gain_ref[...], ocean_shift_ref[...])
        normal = normal.astype(jnp.bfloat16)

        def piece(i, carry):
            at = pl.multiple_of(i * 256, 256)
            z = jnp.dot(normal, ocean_in_ref[:, pl.ds(at, 256)], preferred_element_type=jnp.float32)
            wave_ref[:, pl.ds(at, 256)] = gelu(z).astype(jnp.bfloat16)
            return carry

        lax.fori_loop(0, ocean_in_ref.shape[1] // 256, piece, 0)
        update = jnp.dot(wave_ref[...], ocean_out_ref[...], preferred_element_type=jnp.float32)
        update = update * layer_ref[...]
        for row in range(start_row, start_row + 2):
            begin = jnp.concatenate([tile_ref[part, row + 3, 8 : 8 + cells] for part in range(2)], axis=1)
            change = update[(row - start_row) * cells : (row - start_row + 1) * cells]
            fresh = (begin + own_masks[:cells, row : row + 1] * change).astype(jnp.bfloat16)
            next_ref[row] = fresh
            field = across_rows(field_ref[...], fresh)
            field = (field[:8] + field[8:16] + field[16:24]) * mask_ref[row : row + 1, :cells]
            flat_ref[row] = field
            surface_ref[row] = field[:4]

    def middle_args(lat):
        return middle_out.at[lat], middle_in.at[lat], sent_middle.at[lat], came_middle.at[lat], "each"

    near = zeros((8, quarter))
    for lat in range(rows):
        both = jnp.concatenate([flat_ref[2 * lat], flat_ref[2 * lat + 1]], axis=0)
        patch = across_rows(split_ref[...], jnp.concatenate(thirds(both), axis=0))
        patch = patch[:, :16] + patch[:, 16:32] + patch[:, 32:48]
        total = stream[lat * quarter : (lat + 1) * quarter]
        for e in range(2):
            total = total + product(
                split_bf16(patch[e * quarter : (e + 1) * quarter]),
                split_bf16(embed[e * 16 : (e + 1) * 16]),
            )
        pack(total, lambda s, lat=lat: middle_out.at[lat, s])
        team_exchange(*middle_args(lat))
        middle_in[lat, mine] = middle_out[lat, mine]
        rounded = total.astype(jnp.bfloat16)
        wide = rounded.astype(jnp.float32)
        high, low = split_bf16(wide * wide)
        every = jnp.ones((8, 4 * slot), jnp.bfloat16)
        plain, power = across_rows(every, rounded), across_rows(every, high) + across_rows(every, low)
        row_index = lax.broadcasted_iota(jnp.int32, (8, quarter), 0)
        near = near + jnp.where(row_index == lat, plain, 0.0)
        near = near + jnp.where(row_index == rows + lat, power, 0.0)
    near_sums[...] = jnp.concatenate([near, zeros((8, 128 - quarter))], axis=1)
    near_args = (near_sums, all_near, sent_near, came_near, "whole")
    team_exchange(*near_args)
    all_near[mine] = near_sums[...]
    for lat in range(rows):
        team_finish(*middle_args(lat))
    team_finish(*near_args)

    spectral_filter(1, lambda: None, lambda: None)

    def quarters(which_quarter, carry):
        for lat in range(rows):
            for step in range(1, 4):
                out_copy(1, which_quarter, lat, step, True).wait()
        mlp(1, which_quarter)
        for lat in range(rows):
            pack(
                total_ref[lat * quarter : (lat + 1) * quarter],
                lambda s, lat=lat: part_out.at[which_quarter, s, lat],
            )
        team_exchange(
            part_out.at[which_quarter], part_in.at[which_quarter],
            sent_part.at[which_quarter], came_part.at[which_quarter], "each",
        )
        part_in[which_quarter, mine] = part_out[which_quarter, mine]
        return carry

    lax.fori_loop(0, 2, quarters, 0)
    for which_quarter in range(2):
        team_finish(
            part_out.at[which_quarter], part_in.at[which_quarter],
            sent_part.at[which_quarter], came_part.at[which_quarter], "each",
        )
        for half_of in range(2):
            for lat in range(rows):
                piece = after[half_of, which_quarter, lat].astype(jnp.float32)
                piece = piece + part_in[which_quarter, half_of, lat].astype(jnp.float32)
                piece = piece + part_in[which_quarter, 2 + half_of, lat].astype(jnp.float32)
                tail = piece[quarter:]
                at = (2 * which_quarter + half_of) * quarter
                tail = jnp.concatenate([tail, swap(tail)], axis=0)
                atmosphere_ref[lat, at : at + quarter, :128] = piece[:quarter].astype(jnp.bfloat16)
                atmosphere_ref[lat, at : at + quarter, 128:] = tail[:, : slot - 128].astype(
                    jnp.bfloat16
                )


def on_device(
    atmosphere, spec_weight, spec_bias, norm_gain, norm_shift, fc_in, fc_out, flux_head, flux_embed,
    ocean_state, sea_mask, depth_kernel, ocean_gain, ocean_shift, ocean_in, ocean_out, layer_scale,
    field_head, patch_embed,
):
    bands = lax.axis_size("band")
    rows, longitudes, slot = atmosphere.shape
    quarter = longitudes // 4
    count = rows * quarter
    latitudes = rows * bands
    channels, wide = fc_in.shape[1:]
    packed = quarter * slot // 128
    cells, ocean_channels = ocean_state.shape[1:]
    waves = ocean_in.shape[1]

    inside, outside = pl.BlockSpec(memory_space=pltpu.VMEM), pl.BlockSpec(memory_space=pl.ANY)
    arguments = [
        atmosphere.transpose(0, 2, 1), spec_weight, spec_bias, norm_gain, norm_shift, fc_in, fc_out,
        flux_head.T,
        flux_embed, ocean_state, sea_mask, depth_kernel, ocean_gain[None], ocean_shift[None],
        ocean_in, ocean_out, layer_scale[None], field_head.T, patch_embed,
        *transforms(latitudes, longitudes, bands), *ocean_selectors(quarter),
    ]
    specs = [inside] * 5 + [outside] * 2 + [inside] * (len(arguments) - 7)
    levels = (rows + 4) * ocean_channels
    narrow, single = jnp.bfloat16, jnp.float32

    def dma(*shape):
        return pltpu.SemaphoreType.DMA(shape)

    chunks = (bands, 32, 128)
    scratch = [
        pltpu.VMEM((rows, longitudes, 256), single),
        pltpu.VMEM((2, 2, rows, packed, 128), narrow),
        pltpu.VMEM((2, 4, 2, rows, packed, 128), narrow),
        pltpu.VMEM((bands * 32 + 32, 128), single),
        pltpu.VMEM((bands * 32 + 32, 128), single),
        pltpu.VMEM((8, longitudes), single),
        pltpu.VMEM((4, 8, longitudes), single),
        pltpu.VMEM(chunks, narrow),
        pltpu.VMEM((2,) + chunks, narrow),
        pltpu.VMEM(chunks, narrow),
        pltpu.VMEM((2,) + chunks, narrow),
        pltpu.VMEM((2, 2, channels, wide), narrow),
        pltpu.VMEM((2, 2, wide, channels), narrow),
        pltpu.VMEM((count, channels), single),
        pltpu.VMEM((count, 2 * wide), narrow),
        pltpu.VMEM((count, channels), narrow),
        pltpu.VMEM((count, channels), narrow),
        pltpu.VMEM((2, 4, rows, packed, 128), narrow),
        pltpu.VMEM((2, 4, rows, packed, 128), narrow),
        pltpu.VMEM((4, 40, 256), single),
        pltpu.VMEM((2, 3, cells, ocean_channels), narrow),
        pltpu.VMEM((2, 2 * rows, 16, ocean_channels), narrow),
        pltpu.VMEM((2, 2, 3, 16, ocean_channels), narrow),
        pltpu.VMEM((8, 8, 256), single),
        pltpu.VMEM((rows, 8, 128), single),
        pltpu.VMEM((8, rows, 8, 128), single),
        pltpu.VMEM((2, 2 * rows + 6, cells + 16, 128), single),
        pltpu.VMEM((2 * rows, cells, ocean_channels), single),
        pltpu.VMEM((2 * cells, waves), narrow),
        pltpu.VMEM((rows, 4, packed, 128), narrow),
        pltpu.VMEM((rows, 4, packed, 128), narrow),
        pltpu.VMEM((2, 8, channels), single),
        pltpu.VMEM((2, 8, 256), single),
        pltpu.VMEM((2, 2, 2 * slot, 2 * slot), narrow),
        pltpu.VMEM((2, 8, 2 * slot), single),
        pltpu.VMEM((40, 256), single),
        pltpu.VMEM((8, 256), single),
        pltpu.VMEM((128, levels), single),
        pltpu.VMEM((2, 128, levels), narrow),
        pltpu.VMEM((24, ocean_channels), narrow),
        pltpu.VMEM((count, channels), single),
        pltpu.VMEM((rows, longitudes, 256), single),
        pltpu.VMEM((2 * rows, 8, cells), single),
        pltpu.VMEM((8, 128), single),
        pltpu.VMEM((4, 8, 128), single),
        pltpu.VMEM((cells + 16, 16), single),
        pltpu.VMEM((256, 128), single),
        dma(4), dma(4), dma(2, bands), dma(2, bands), dma(2, bands), dma(2, bands),
        dma(2, 2, rows, 4), dma(2, 2, rows, 4), dma(1), dma(1), dma(2, 4), dma(2, 4), dma(2, 2), dma(2, 2), dma(2, 2),
        dma(4), dma(4), dma(8), dma(8), dma(8), dma(8), dma(8), dma(8), dma(rows, 4), dma(rows, 4),
        dma(4), dma(4),
    ]
    atmosphere_next, ocean_next, surface = pl.pallas_call(
        functools.partial(step_kernel, bands),
        out_shape=(
            jax.ShapeDtypeStruct(atmosphere.shape, narrow),
            jax.ShapeDtypeStruct(ocean_state.shape, narrow),
            jax.ShapeDtypeStruct((2 * rows, 4, cells), single),
        ),
        in_specs=specs,
        out_specs=(inside,) * 3,
        scratch_shapes=scratch,
        compiler_params=pltpu.CompilerParams(
            collective_id=0, has_side_effects=True, vmem_limit_bytes=63 << 20
        ),
    )(*arguments)
    return (atmosphere_next, ocean_next, surface.transpose(0, 2, 1))


def solution(mesh):
    placed = (
        P("band", None, ("comp", "tile")),
        P(None, None, None, ("comp", "tile"), None),
        P(None, None, None, ("comp", "tile")),
        P(),
        P(),
        P(None, None, ("comp", "tile")),
        P(None, ("comp", "tile"), None),
        P(("comp", "tile"), None),
        P(),
        P("band", ("comp", "tile"), None),
        P("band", ("comp", "tile")),
        P(),
        P(),
        P(),
        P(),
        P(),
        P(),
        P(),
        P(None, ("comp", "tile")),
    )
    return jax.shard_map(
        on_device,
        mesh=mesh,
        in_specs=placed,
        out_specs=(
            P("band", None, ("comp", "tile")),
            P("band", ("comp", "tile"), None),
            P("band", ("comp", "tile"), None),
        ),
        check_vma=False,
    )
```

```python
import functools
import math

import jax
import jax.numpy as jnp
import numpy as np
from jax import lax
from jax.experimental import pallas as pl
from jax.experimental.pallas import tpu as pltpu
from jax.sharding import PartitionSpec as P

MESH = pl.DeviceIdType.MESH
full_precision = lax.Precision.HIGHEST
eps_norm = 1e-06
shrink_level = 0.01


def layer_norm(values, scaling, offset):
    average = jnp.mean(values, axis=-1, keepdims=True)
    squares = jnp.mean(values * values, axis=-1, keepdims=True)
    variance = squares - average * average
    return (values - average) * lax.rsqrt(variance + eps_norm) * scaling + offset


def soft_shrink(values):
    zeros = jnp.zeros_like(values)
    return jnp.where(
        values > shrink_level,
        values - shrink_level,
        jnp.where(values < -shrink_level, values + shrink_level, zeros),
    )


def split_bf16(array):
    high = array.astype(jnp.bfloat16)
    return high, (array - high.astype(jnp.float32)).astype(jnp.bfloat16)


def transforms(latitudes, longitudes, bands):
    kept = longitudes // 2
    each, rows = kept // bands, latitudes // bands
    waves = np.arange(kept).reshape(bands, each).T.reshape(-1)
    lats = np.arange(latitudes).reshape(bands, rows).T.reshape(-1)
    lon = np.outer(waves, np.arange(longitudes)) % longitudes * (2.0 * math.pi / longitudes)
    lat = np.outer(np.arange(latitudes), lats) % latitudes * (2.0 * math.pi / latitudes)
    forward = np.concatenate([np.cos(lon), -np.sin(lon)], 0) / math.sqrt(longitudes)
    across = np.stack([np.cos(lat), np.sin(lat)], 0) / math.sqrt(latitudes)
    weight = np.where(waves == 0, 1.0, 2.0)[:, None]
    inverse = np.concatenate([np.cos(lon) * weight, -np.sin(lon) * weight], 0).T
    mats = (
        forward,
        across.reshape(2 * latitudes, latitudes),
        across.transpose(0, 2, 1).reshape(2 * latitudes, latitudes),
        inverse / math.sqrt(longitudes),
    )
    return [jnp.asarray(m, jnp.bfloat16) for m in mats]


def times(left, right):
    return jnp.dot(
        left.astype(jnp.bfloat16), right.astype(jnp.bfloat16), preferred_element_type=jnp.float32
    )


def product(left, right):
    total = None
    for a, b in ((0, 0), (1, 0), (0, 1)):
        if a < len(left) and b < len(right):
            term = jnp.dot(left[a], right[b], preferred_element_type=jnp.float32)
            total = term if total is None else total + term
    return total


directions = [(b, c) for b in (-1, 0, 1) for c in (-1, 0, 1) if (b, c) != (0, 0)]


def ocean_selectors(quarter):
    columns = np.arange(-8, 2 * quarter + 8)
    pick = np.zeros((len(columns), 384), np.float32)
    seen = np.zeros((len(columns), 512), np.float32)
    for i, column in enumerate(columns):
        if not -3 <= column < 2 * quarter + 3:
            continue
        token = column // 2
        side = 0 if token < 0 else 2 if token >= quarter else 1
        pick[i, side * 128 + token % quarter] = 1
        inner = column % (2 * quarter)
        seen[i, inner - 128 if column < 0 else 384 + inner if column >= 2 * quarter else 128 + inner] = 1
    split = np.zeros((2 * quarter, 2 * quarter), np.float32)
    for e in range(2):
        split[e * quarter + np.arange(quarter), 2 * np.arange(quarter) + e] = 1
    return (jnp.asarray(m, jnp.bfloat16) for m in (pick, seen, split))


def thirds(array):
    high = array.astype(jnp.bfloat16)
    rest = array - high.astype(jnp.float32)
    middle = rest.astype(jnp.bfloat16)
    return high, middle, (rest - middle.astype(jnp.float32)).astype(jnp.bfloat16)


def gelu(z):
    return 0.5 * z * (1.0 + lax.erf(z * math.sqrt(0.5)))


def step_kernel(bands, *refs):
    (
        x_ref, weight_ref, bias_ref, gain_ref, shift_ref, fc_in_ref, fc_out_ref, flux_head_ref,
        flux_embed_ref, ocean_ref, sea_ref, depth_ref, ocean_gain_ref, ocean_shift_ref,
        ocean_in_ref, ocean_out_ref, layer_ref, field_head_ref, patch_ref,
        forward_ref, across_ref, back_ref, inverse_ref, pick_ref, seen_ref, split_ref,
        atmosphere_ref, next_ref, surface_ref,
        normed, after, token, stage, landed, sums, all_sums, send_a, got_a, send_b, got_b,
        w_in, w_out, stream, hidden_ref, half_out, half_in, part_out, part_in, shared_ref,
        rows_in, cols_in, corner_in, masks_in, flux_ref, flux_in, tile_ref, conv_ref, wave_ref,
        middle_out, middle_in, order_ref, affine_ref, mix_ref, offset_ref, share_ref, mask_ref,
        level_ref, spread_ref, field_ref, total_ref, turned_ref, flat_ref, near_sums, all_near,
        seen_masks, own_masks,
        sent_sum, came_sum, sent_a, came_a, sent_b, came_b, sent_out, came_out,
        sent_half, came_half, sent_part, came_part, load, sent_load, came_load,
        sent_share, came_share, sent_cells, came_cells, sent_mask, came_mask, sent_flux, came_flux,
        sent_middle, came_middle, sent_near, came_near,
    ) = refs
    rows, slot, longitudes = x_ref.shape
    quarter = longitudes // 4
    middle = quarter // 2
    latitudes = rows * bands
    each = longitudes // 2 // bands
    cells = ocean_ref.shape[1]
    me = lax.axis_index("band")
    comp, tile = lax.axis_index("comp"), lax.axis_index("tile")
    mine = comp * 2 + tile

    def member(step):
        return lax.rem(mine + step, 4)

    def team_id(index):
        return {"comp": lax.div(index, 2), "tile": lax.rem(index, 2)}

    def near_id(b, c):
        index = lax.rem(mine + c + 4, 4)
        return {"band": lax.rem(me + b + bands, bands), **team_id(index)}

    own_loads = [
        pltpu.make_async_copy(source.at[block], target.at[block, 0], load.at[block, i])
        for block in range(2)
        for i, (source, target) in enumerate(((fc_in_ref, w_in), (fc_out_ref, w_out)))
    ]
    sibling_loads = [
        pltpu.make_async_remote_copy(
            src_ref=source.at[block],
            dst_ref=target.at[block, 1],
            send_sem=sent_load.at[block, i],
            recv_sem=came_load.at[block, i],
            device_id={"tile": 1 - tile},
            device_id_type=MESH,
        )
        for block in range(2)
        for i, (source, target) in enumerate(((fc_in_ref, w_in), (fc_out_ref, w_out)))
    ]
    barrier = pltpu.get_barrier_semaphore()

    def greet(step, carry):
        pl.semaphore_signal(
            barrier, inc=1, device_id={"band": lax.rem(me + step, bands)}, device_id_type=MESH
        )
        return carry

    for step in range(1, 4):
        pl.semaphore_signal(barrier, inc=1, device_id=team_id(member(step)), device_id_type=MESH)
    for b, c in directions:
        if b and c:
            pl.semaphore_signal(barrier, inc=1, device_id=near_id(b, c), device_id_type=MESH)
    lax.fori_loop(1, bands, greet, 0)
    for copy in own_loads:
        copy.start()

    def near_copies(source_of, target_of, sent, came):
        copies = []
        for d, (b, c) in enumerate(directions):
            copies.append(
                pltpu.make_async_remote_copy(
                    src_ref=source_of(b, c),
                    dst_ref=target_of(-b, -c),
                    send_sem=sent.at[d],
                    recv_sem=came.at[directions.index((-b, -c))],
                    device_id=near_id(b, c),
                    device_id_type=MESH,
                )
            )
        return copies

    def near_landings(source_of, target_of, sent, came):
        copies = []
        for d, (b, c) in enumerate(directions):
            copies.append(
                pltpu.make_async_remote_copy(
                    src_ref=source_of(b, c),
                    dst_ref=target_of(b, c),
                    send_sem=sent.at[d],
                    recv_sem=came.at[d],
                    device_id=near_id(b, c),
                    device_id_type=MESH,
                )
            )
        return copies

    def cells_from(b, c):
        row = pl.ds(0, 2 * rows) if b == 0 else pl.ds(2 * rows - 3 if b > 0 else 0, 3)
        column = pl.ds(0, cells) if c == 0 else pl.ds(cells - 16 if c > 0 else 0, 16)
        return ocean_ref.at[row, column]

    def cells_to(b, c):
        if c == 0:
            return rows_in.at[0 if b < 0 else 1]
        if b == 0:
            return cols_in.at[0 if c < 0 else 1]
        return corner_in.at[0 if b < 0 else 1, 0 if c < 0 else 1]

    cell_args = (cells_from, cells_to, sent_cells, came_cells)
    mask_args = (
        lambda b, c: mask_ref, lambda b, c: masks_in.at[directions.index((b, c))], sent_mask, came_mask
    )
    flux_args = (
        lambda b, c: flux_ref, lambda b, c: flux_in.at[directions.index((b, c))], sent_flux, came_flux
    )

    def team_copy(source, target, sent, came, step, pick, landing):
        index = member(step)
        chosen = {"whole": lambda: source, "each": lambda: source.at[index]}[pick]()
        place = index if landing else mine
        return pltpu.make_async_remote_copy(
            src_ref=chosen,
            dst_ref=target.at[place],
            send_sem=sent.at[index],
            recv_sem=came.at[place],
            device_id=team_id(index),
            device_id_type=MESH,
        )

    def team_exchange(source, target, sent, came, pick):
        for step in range(1, 4):
            team_copy(source, target, sent, came, step, pick, False).start()

    def team_finish(source, target, sent, came, pick):
        for step in range(1, 4):
            team_copy(source, target, sent, came, step, pick, True).wait()

    def out_copy(block, turn, step, landing):
        index = member(step)
        place = index if landing else mine
        wanted = turn
        if block == 0:
            wanted = lax.rem(1 - (comp if landing else lax.div(index, 2)) + turn, 2)
        return pltpu.make_async_remote_copy(
            src_ref=after.at[lax.rem(index, 2), wanted],
            dst_ref=token.at[block, place, wanted],
            send_sem=sent_out.at[block, turn, index],
            recv_sem=came_out.at[block, turn, place],
            device_id=team_id(index),
            device_id_type=MESH,
        )

    my_x, my_y, my_z = lax.div(me, 16), lax.rem(lax.div(me, 8), 2), lax.rem(me, 8)

    def band_peer(step):
        x = lax.rem(my_x + lax.div(step, 16), bands // 16)
        y = lax.rem(my_y + lax.div(step, 8), 2)
        return x * 16 + y * 8 + lax.rem(my_z + step, 8)

    def band_copy(source, target, sent, came, step, landing):
        index = band_peer(step)
        return pltpu.make_async_remote_copy(
            src_ref=source.at[index],
            dst_ref=target.at[index if landing else me],
            send_sem=sent.at[index],
            recv_sem=came.at[index if landing else me],
            device_id={"band": index},
            device_id_type=MESH,
        )

    def band_exchange(source, target, sent, came, meanwhile):
        source[...] = stage[: bands * 32].astype(jnp.bfloat16).reshape(source.shape)

        def go(step, carry):
            band_copy(source, target, sent, came, step, False).start()
            return carry

        lax.fori_loop(1, bands, go, 0)
        target[me] = source[me]
        meanwhile()

        def widen(index):
            at = pl.multiple_of(index * 32, 32)
            landed[pl.ds(at, 32), :] = target[index].astype(jnp.float32)

        widen(me)

        def come(step, carry):
            band_copy(source, target, sent, came, step, True).wait()
            widen(band_peer(step))
            return carry

        lax.fori_loop(1, bands, come, 0)

    lane = lax.broadcasted_iota(jnp.int32, (1, 128), 1)
    first_half = lane < slot - 128
    sign = jnp.where(first_half, 1.0, -1.0)
    half = longitudes // 2
    counted = jnp.ones((8, slot), jnp.bfloat16)
    which = lax.broadcasted_iota(jnp.int32, (8, longitudes), 0)
    turned = (((1,), (1,)), ((), ()))

    def across_rows(left, right):
        return lax.dot_general(left, right, turned, preferred_element_type=jnp.float32)

    def swap(values):
        return pltpu.roll(values, 64, 1)

    def doubled(tails):
        top = jnp.where(first_half, tails, swap(tails))
        low = jnp.where(first_half, swap(tails), tails)
        return jnp.concatenate([top, low], axis=0)

    def tokens(block, lat):
        if block == 0:
            return turned_ref[lat]
        pieces = [middle_in[s, lat].astype(jnp.float32) for s in range(4)]
        return jnp.concatenate(
            [jnp.concatenate([p[:quarter], doubled(p[quarter:])], axis=1) for p in pieces], axis=0
        )

    def spread(lat, wave, part, values):
        stage[pl.ds(part * 9 + lat * 3 + wave, bands, stride=32), :] = values

    def collect(lat, wave, part):
        return landed[pl.ds(part * 9 + lat * 3 + wave, bands, stride=32), :]

    def spectral_filter(block, while_first, while_second):
        if block == 0:
            total = jnp.zeros((8, longitudes), jnp.float32)
            for lat in range(rows):
                values = x_ref[lat].astype(jnp.float32)
                high, low = split_bf16(values * values)
                total = total + jnp.where(which == lat, times(counted, x_ref[lat]), 0.0)
                total = total + jnp.where(
                    which == rows + lat, times(counted, high) + times(counted, low), 0.0
                )
            sums[...] = total
            pl.semaphore_wait(barrier, bands - 1 + 3 + 4)
            team_exchange(sums, all_sums, sent_sum, came_sum, "whole")
            for copy in near_copies(*mask_args) + near_copies(*cell_args) + sibling_loads:
                copy.start()
            team_exchange(share_ref, shared_ref, sent_share, came_share, "whole")
            shared_ref[mine] = share_ref[...]
            all_sums[mine] = total
            team_finish(sums, all_sums, sent_sum, came_sum, "whole")
            total = all_sums[0] + all_sums[1] + all_sums[2] + all_sums[3]
            columns = jnp.concatenate([total, jnp.zeros((120, longitudes), jnp.float32)], axis=0).T
        else:
            blank = jnp.zeros((120, 128), jnp.float32)
            columns = jnp.concatenate(
                [jnp.concatenate([all_near[s], blank], axis=0).T[:quarter] for s in range(4)], axis=0
            )
        columns = columns * (1.0 / (4 * slot))
        for lat in range(rows):
            average = columns[:, lat : lat + 1]
            power = columns[:, rows + lat : rows + lat + 1]
            scaled = tokens(block, lat) - average
            scaled = scaled * lax.rsqrt(power - average * average + eps_norm)
            scaled = scaled * affine_ref[block, 0:1, :] + affine_ref[block, 2:3, :]
            normed[lat] = scaled
            spectrum = times(forward_ref[...], scaled)
            upper, lower = spectrum[:half], spectrum[half:]
            rest = jnp.where(first_half, upper[:, 128:], lower[:, 128:])
            parts = (upper[:, :128], lower[:, :128], rest)
            for part in range(3):
                for wave in range(each):
                    spread(lat, wave, part, parts[part][wave * bands : (wave + 1) * bands])
        band_exchange(send_a, got_a.at[block], sent_a.at[block], came_a.at[block], while_first)
        pieces = []
        for wave in range(each):
            for part in range(3):
                pieces.append(
                    jnp.concatenate([collect(lat, wave, part) for lat in range(rows)], axis=0)
                )
        spectrum = jnp.concatenate(pieces, axis=1).astype(jnp.bfloat16)
        turned_all = times(across_ref[...], spectrum)

        def combine(both, wave, direction):
            base = wave * 384
            cosine, sine = both[:latitudes, base : base + 384], both[latitudes:, base : base + 384]
            real = cosine[:, :128] + direction * sine[:, 128:256]
            imag = cosine[:, 128:256] - direction * sine[:, :128]
            rest = cosine[:, 256:] + (direction * sign) * swap(sine[:, 256:])
            return real, imag, rest

        rows_mixed = jnp.concatenate(
            [jnp.concatenate(combine(turned_all, wave, 1.0), axis=1) for wave in range(each)], axis=0
        )
        hidden = times(rows_mixed, mix_ref[block, 0])
        hidden = jnp.maximum(hidden + offset_ref[block, 0:1, :], 0.0)
        mixed = times(hidden, mix_ref[block, 1])
        mixed = soft_shrink(mixed + offset_ref[block, 1:2, :])
        mixed = jnp.concatenate(
            [mixed[wave * latitudes : (wave + 1) * latitudes] for wave in range(each)], axis=1
        )
        turned_back = times(back_ref[...], mixed)
        for wave in range(each):
            parts = combine(turned_back, wave, -1.0)
            for part in range(3):
                for lat in range(rows):
                    spread(lat, wave, part, parts[part][lat * bands : (lat + 1) * bands])
        band_exchange(send_b, got_b.at[block], sent_b.at[block], came_b.at[block], while_second)
        for lat in range(rows):
            real, imag, rest = (
                jnp.concatenate([collect(lat, wave, part) for wave in range(each)], axis=0)
                for part in range(3)
            )
            right = jnp.concatenate(
                [
                    jnp.concatenate([real, rest], axis=1),
                    jnp.concatenate([imag, swap(rest)], axis=1),
                ],
                axis=0,
            ).astype(jnp.bfloat16)
            restored = times(inverse_ref[...], right)
            result = tokens(block, lat) + restored + normed[lat]
            for s in range(4):
                piece = result[s * quarter : (s + 1) * quarter]
                tail = piece[:, 128:]
                tail = jnp.where(first_half, tail[:middle], swap(tail[middle:]))
                after[s % 2, s // 2, lat, :quarter] = piece[:, :128].astype(jnp.bfloat16)
                after[s % 2, s // 2, lat, quarter:] = tail.astype(jnp.bfloat16)
        for turn in range(2):
            for step in range(1, 4):
                out_copy(block, turn, step, False).start()
        token[block, mine] = after[tile]
        for i in range(2):
            own_loads[2 * block + i].wait()
            sibling_loads[2 * block + i].wait()

    def pair(left, right):
        return jnp.concatenate(
            [jnp.where(first_half, left, swap(right)), jnp.where(first_half, swap(left), right)], 0
        )

    def unpair(both):
        top, low = both[:middle], both[middle:]
        return jnp.where(first_half, top, swap(low)), jnp.where(first_half, swap(top), low)

    def pack(block_rows, target):
        tails = unpair(block_rows[:, 512:640]) + unpair(block_rows[:, 640:])
        for s in range(4):
            place = target(s)
            place[:quarter] = block_rows[:, s * 128 : (s + 1) * 128].astype(jnp.bfloat16)
            place[quarter:] = tails[s].astype(jnp.bfloat16)

    def lanes_of(slices):
        heads = [p[:quarter] for p in slices]
        tails = [p[quarter:] for p in slices]
        return jnp.concatenate(heads + [pair(*tails[:2]), pair(*tails[2:])], axis=1)

    def reorder(values):
        t = [values[:, i * 128 : (i + 1) * 128] for i in range(6)]

        def inner(a, b):
            return jnp.where(first_half, swap(a), swap(b)), jnp.where(first_half, a, b)

        one, tails_a = inner(t[1], t[2])
        three, tails_b = inner(t[4], t[5])
        return jnp.concatenate([t[0], one, t[3], three, tails_a, tails_b], axis=1)

    row_spans = [(s * slot, 128) for s in range(4)] + [(s * slot + 128, slot - 128) for s in range(4)]

    def mlp(block, which_quarter):
        for lat in range(rows):
            slices = [token[block, s, which_quarter, lat].astype(jnp.float32) for s in range(4)]
            stream[lat * quarter : (lat + 1) * quarter] = lanes_of(slices)
        values = stream[...]
        normal = layer_norm(values, order_ref[block, 1:2, :], order_ref[block, 3:4, :])
        normal = normal.astype(jnp.bfloat16)
        wide = w_in.shape[3]
        for part in range(2):

            def piece(i, carry):
                at = pl.multiple_of(i * 256, 256)
                weight = jnp.concatenate(
                    [w_in[block, part, pl.ds(a, n), pl.ds(at, 256)] for a, n in row_spans], axis=0
                )
                z = jnp.dot(normal, weight, preferred_element_type=jnp.float32)
                hidden_ref[:, pl.ds(part * wide + at, 256)] = gelu(z).astype(jnp.bfloat16)
                return carry

            lax.fori_loop(0, wide // 256, piece, 0)
        total = jnp.dot(hidden_ref[:, :wide], w_out[block, 0], preferred_element_type=jnp.float32)
        total = total + jnp.dot(
            hidden_ref[:, wide:], w_out[block, 1], preferred_element_type=jnp.float32
        )
        total_ref[...] = reorder(total)

    zeros = functools.partial(jnp.zeros, dtype=jnp.float32)
    for block in range(2):
        both = jnp.concatenate([gain_ref[block], shift_ref[block], zeros((4, 4 * slot))], axis=0)
        order_ref[block] = reorder(both)
        head = order_ref[block, :, pl.ds(pl.multiple_of(mine * 128, 128), 128)]
        tail = order_ref[block, :, pl.ds(pl.multiple_of(512 + comp * 128, 128), 128)]
        tail = jnp.where(tile == 0, tail, swap(tail))
        tail = jnp.where(first_half, tail, swap(tail))
        affine_ref[block] = jnp.concatenate([head, tail], axis=1)
    share_ref[...] = zeros(share_ref.shape)
    share_ref[0:8, :slot] = flux_head_ref[...].astype(jnp.float32)
    for lat in range(rows):
        values = x_ref[lat].astype(jnp.float32)
        turned_ref[lat] = jnp.concatenate([values, values[128:]], axis=0).T
    for f in range(4):
        for a in range(2):
            for e in range(2):
                at, row = 8 + e * 16 + a * 8 + f, f * 4 + a * 2 + e
                share_ref[at : at + 1, :slot] = patch_ref[row : row + 1, :]
    mask_ref[...] = zeros(mask_ref.shape)
    mask_ref[: 2 * rows, :cells] = sea_ref[...].astype(jnp.float32)
    ext_rows = 2 * rows + 6

    def prepare_products():
        for block in range(2):
            for sublayer in range(2):

                def placed(weight):
                    width = weight.shape[1]
                    wide = jnp.concatenate([weight, zeros((slot, 128 - width))], axis=1)
                    moved = pltpu.roll(wide[width:], width, 1)
                    low = jnp.where(lane >= width, moved, 0.0)
                    high = jnp.where(first_half, moved, 0.0)
                    return (
                        jnp.concatenate([wide[:width], low], axis=0),
                        jnp.concatenate([zeros((width, 128)), high], axis=0),
                    )

                real, real_tail = placed(weight_ref[block, sublayer, 0])
                imag, imag_tail = placed(weight_ref[block, sublayer, 1])
                upper = jnp.concatenate([real, imag, real_tail + swap(imag_tail)], axis=1)
                lower = jnp.concatenate([-imag, real, swap(real_tail) - imag_tail], axis=1)
                mix_ref[block, sublayer] = jnp.concatenate(
                    [upper[:128], lower[:128], upper[128:], lower[128:]], axis=0
                ).astype(jnp.bfloat16)
                bias = bias_ref[block, sublayer]
                tail = jnp.concatenate([bias[:, 128:], bias[:, 128:]], axis=1)
                offset_ref[block, sublayer : sublayer + 1, :] = jnp.concatenate(
                    [bias[0:1, :128], bias[1:2, :128], jnp.where(first_half, tail[0:1], tail[1:2])], axis=1
                )
        level_ref[...] = zeros(level_ref.shape)
        for level in range(rows + 4):
            level_ref[level * 8 : level * 8 + 8, level * 256 : (level + 1) * 256] = flux_embed_ref[...]
        spread_ref[0], spread_ref[1] = split_bf16(level_ref[...])
        fields = jnp.concatenate([field_head_ref[...], zeros((4, 256))], axis=0)
        field_ref[...] = jnp.concatenate(thirds(fields), axis=0)

    def mask_rows(b, c):
        whole = mask_ref[...] if (b, c) == (0, 0) else masks_in[directions.index((b, c))]
        whole = whole[:, 128:] if c < 0 else whole[:, :128] if c > 0 else whole
        return whole[2 * rows - 3 : 2 * rows] if b < 0 else whole[:3] if b > 0 else whole[: 2 * rows]

    def prepare_masks():
        for copy in near_landings(*mask_args) + near_landings(*cell_args):
            copy.wait()
        masks = jnp.concatenate(
            [jnp.concatenate([mask_rows(b, c) for c in (-1, 0, 1)], axis=1) for b in (-1, 0, 1)]
            + [jnp.zeros((16 - ext_rows, 512), jnp.float32)],
            axis=0,
        )
        seen_masks[...] = across_rows(seen_ref[...], masks.astype(jnp.bfloat16))
        own_masks[...] = jnp.concatenate([mask_ref[...], zeros((120, 256))], axis=0).T

    spectral_filter(0, prepare_products, prepare_masks)
    team_finish(share_ref, shared_ref, sent_share, came_share, "whole")
    copy = pltpu.make_async_remote_copy(
        src_ref=half_out,
        dst_ref=half_in,
        send_sem=sent_half.at[0],
        recv_sem=came_half.at[0],
        device_id={"comp": 1 - comp},
        device_id_type=MESH,
    )

    def halves(i, carry):
        for step in range(1, 4):
            out_copy(0, i, step, True).wait()
        mlp(0, lax.rem(1 - comp + i, 2))

        @pl.when(i == 0)
        def _():
            half_out[...] = total_ref[...].astype(jnp.bfloat16)
            copy.start()

        return carry

    lax.fori_loop(0, 2, halves, 0)
    copy.wait()
    first = stream[...] + total_ref[...] + half_in[...].astype(jnp.float32)
    first = first.astype(jnp.bfloat16)
    stream[...] = first.astype(jnp.float32)

    small = [shared_ref[s] for s in range(4)]
    tails = [s[:, 128:] for s in small]
    whole = jnp.concatenate(
        [s[:, :128] for s in small]
        + [jnp.where(first_half, tails[i], swap(tails[i + 1])) for i in (0, 2)],
        axis=1,
    )
    head, embed = whole[:8].astype(jnp.bfloat16), whole[8:]
    for lat in range(rows):
        flux = across_rows(head, first[lat * quarter : (lat + 1) * quarter])
        flux_ref[lat] = jnp.concatenate([flux, jnp.zeros((8, 128 - quarter), jnp.float32)], axis=1)
    for copy in near_copies(*flux_args):
        copy.start()
    for copy in near_landings(*flux_args):
        copy.wait()

    def flux_at(lat, c):
        b = -1 if lat < 0 else 1 if lat >= rows else 0
        if (b, c) == (0, 0):
            return flux_ref[lat]
        return flux_in[directions.index((b, c)), lat % rows]

    ext_lats = range(-2, rows + 2)
    laid = jnp.concatenate(
        [jnp.concatenate([flux_at(lat, c) for c in (-1, 0, 1)], axis=1) for lat in ext_lats]
        + [jnp.zeros((128 - 8 * len(ext_lats), 384), jnp.float32)],
        axis=0,
    )
    raised = across_rows(pick_ref[...], jnp.concatenate(thirds(laid), axis=0))
    raised = raised[:, :128] + raised[:, 128:256] + raised[:, 256:]
    forcing = product(split_bf16(raised), (spread_ref[0], spread_ref[1]))

    for row in range(ext_rows):
        b = -1 if row < 3 else 1 if row >= 2 * rows + 3 else 0
        at = row if b < 0 else row - 3 if b == 0 else row - 2 * rows - 3
        sources = (
            cols_in[0, at] if b == 0 else corner_in[0 if b < 0 else 1, 0, at],
            ocean_ref[at] if b == 0 else rows_in[0 if b < 0 else 1, at],
            cols_in[1, at] if b == 0 else corner_in[0 if b < 0 else 1, 1, at],
        )
        sources = [s.astype(jnp.float32) for s in sources]
        state = jnp.concatenate([sources[0][8:], sources[1], sources[2][:8]], axis=0)
        level = (row - 3) // 2 + 2
        start = state + seen_masks[:, row : row + 1] * forcing[:, level * 256 : (level + 1) * 256]
        start = start.astype(jnp.bfloat16).astype(jnp.float32)
        if b:
            inside = jnp.where(me > 0, 1.0, 0.0) if b < 0 else jnp.where(me < bands - 1, 1.0, 0.0)
            start = start * inside
        for part in range(2):
            tile_ref[part, row] = start[:, part * 128 : (part + 1) * 128]

    for part in range(2):
        span = slice(part * 128, (part + 1) * 128)

        def strip(i, carry):
            at = pl.multiple_of(i * 16, 16)
            totals = [jnp.zeros((16, 128), jnp.float32) for _ in range(2 * rows)]
            for e in range(7):
                for row in range(ext_rows):
                    values = tile_ref[part, row, pl.ds(at + 5 + e, 16), :]
                    for a in range(7):
                        if 0 <= row - a < 2 * rows:
                            tap = depth_ref[a, e : e + 1, span]
                            totals[row - a] = totals[row - a] + values * tap
            for row in range(2 * rows):
                conv_ref[row, pl.ds(at, 16), span] = totals[row]
            return carry

        lax.fori_loop(0, cells // 16, strip, 0)

    for start_row in range(0, 2 * rows, 2):
        values = conv_ref[start_row : start_row + 2].reshape(2 * cells, 256)
        normal = layer_norm(values, ocean_gain_ref[...], ocean_shift_ref[...])
        normal = normal.astype(jnp.bfloat16)

        def piece(i, carry):
            at = pl.multiple_of(i * 256, 256)
            z = jnp.dot(normal, ocean_in_ref[:, pl.ds(at, 256)], preferred_element_type=jnp.float32)
            wave_ref[:, pl.ds(at, 256)] = gelu(z).astype(jnp.bfloat16)
            return carry

        lax.fori_loop(0, ocean_in_ref.shape[1] // 256, piece, 0)
        update = jnp.dot(wave_ref[...], ocean_out_ref[...], preferred_element_type=jnp.float32)
        update = update * layer_ref[...]
        for row in range(start_row, start_row + 2):
            begin = jnp.concatenate([tile_ref[part, row + 3, 8 : 8 + cells] for part in range(2)], axis=1)
            change = update[(row - start_row) * cells : (row - start_row + 1) * cells]
            fresh = (begin + own_masks[:cells, row : row + 1] * change).astype(jnp.bfloat16)
            next_ref[row] = fresh
            field = across_rows(field_ref[...], fresh)
            field = (field[:8] + field[8:16] + field[16:24]) * mask_ref[row : row + 1, :cells]
            flat_ref[row] = field
            surface_ref[row] = field[:4]

    near = zeros((8, quarter))
    for lat in range(rows):
        both = jnp.concatenate([flat_ref[2 * lat], flat_ref[2 * lat + 1]], axis=0)
        patch = across_rows(split_ref[...], jnp.concatenate(thirds(both), axis=0))
        patch = patch[:, :16] + patch[:, 16:32] + patch[:, 32:48]
        total = stream[lat * quarter : (lat + 1) * quarter]
        for e in range(2):
            total = total + product(
                split_bf16(patch[e * quarter : (e + 1) * quarter]),
                split_bf16(embed[e * 16 : (e + 1) * 16]),
            )
        pack(total, lambda s, lat=lat: middle_out.at[s, lat])
        rounded = total.astype(jnp.bfloat16)
        wide = rounded.astype(jnp.float32)
        high, low = split_bf16(wide * wide)
        every = jnp.ones((8, 4 * slot), jnp.bfloat16)
        plain, power = across_rows(every, rounded), across_rows(every, high) + across_rows(every, low)
        row_index = lax.broadcasted_iota(jnp.int32, (8, quarter), 0)
        near = near + jnp.where(row_index == lat, plain, 0.0)
        near = near + jnp.where(row_index == rows + lat, power, 0.0)
    near_sums[...] = jnp.concatenate([near, zeros((8, 128 - quarter))], axis=1)
    near_args = (near_sums, all_near, sent_near, came_near, "whole")
    team_exchange(*near_args)
    all_near[mine] = near_sums[...]
    args = (middle_out, middle_in, sent_middle, came_middle, "each")
    team_exchange(*args)
    middle_in[mine] = middle_out[mine]
    team_finish(*args)
    team_finish(*near_args)

    spectral_filter(1, lambda: None, lambda: None)

    def quarters(which_quarter, carry):
        for step in range(1, 4):
            out_copy(1, which_quarter, step, True).wait()
        mlp(1, which_quarter)
        for lat in range(rows):
            pack(
                total_ref[lat * quarter : (lat + 1) * quarter],
                lambda s, lat=lat: part_out.at[which_quarter, s, lat],
            )
        team_exchange(
            part_out.at[which_quarter], part_in.at[which_quarter],
            sent_part.at[which_quarter], came_part.at[which_quarter], "each",
        )
        part_in[which_quarter, mine] = part_out[which_quarter, mine]
        return carry

    lax.fori_loop(0, 2, quarters, 0)
    for which_quarter in range(2):
        team_finish(
            part_out.at[which_quarter], part_in.at[which_quarter],
            sent_part.at[which_quarter], came_part.at[which_quarter], "each",
        )
        for half_of in range(2):
            for lat in range(rows):
                piece = after[half_of, which_quarter, lat].astype(jnp.float32)
                piece = piece + part_in[which_quarter, half_of, lat].astype(jnp.float32)
                piece = piece + part_in[which_quarter, 2 + half_of, lat].astype(jnp.float32)
                tail = piece[quarter:]
                at = (2 * which_quarter + half_of) * quarter
                tail = jnp.concatenate([tail, swap(tail)], axis=0)
                atmosphere_ref[lat, at : at + quarter, :128] = piece[:quarter].astype(jnp.bfloat16)
                atmosphere_ref[lat, at : at + quarter, 128:] = tail[:, : slot - 128].astype(
                    jnp.bfloat16
                )


def on_device(
    atmosphere, spec_weight, spec_bias, norm_gain, norm_shift, fc_in, fc_out, flux_head, flux_embed,
    ocean_state, sea_mask, depth_kernel, ocean_gain, ocean_shift, ocean_in, ocean_out, layer_scale,
    field_head, patch_embed,
):
    bands = lax.axis_size("band")
    rows, longitudes, slot = atmosphere.shape
    quarter = longitudes // 4
    count = rows * quarter
    latitudes = rows * bands
    channels, wide = fc_in.shape[1:]
    packed = quarter * slot // 128
    cells, ocean_channels = ocean_state.shape[1:]
    waves = ocean_in.shape[1]

    inside, outside = pl.BlockSpec(memory_space=pltpu.VMEM), pl.BlockSpec(memory_space=pl.ANY)
    arguments = [
        atmosphere.transpose(0, 2, 1), spec_weight, spec_bias, norm_gain, norm_shift, fc_in, fc_out,
        flux_head.T,
        flux_embed, ocean_state, sea_mask, depth_kernel, ocean_gain[None], ocean_shift[None],
        ocean_in, ocean_out, layer_scale[None], field_head.T, patch_embed,
        *transforms(latitudes, longitudes, bands), *ocean_selectors(quarter),
    ]
    specs = [inside] * 5 + [outside] * 2 + [inside] * (len(arguments) - 7)
    levels = (rows + 4) * ocean_channels
    narrow, single = jnp.bfloat16, jnp.float32

    def dma(*shape):
        return pltpu.SemaphoreType.DMA(shape)

    chunks = (bands, 32, 128)
    scratch = [
        pltpu.VMEM((rows, longitudes, 256), single),
        pltpu.VMEM((2, 2, rows, packed, 128), narrow),
        pltpu.VMEM((2, 4, 2, rows, packed, 128), narrow),
        pltpu.VMEM((bands * 32 + 32, 128), single),
        pltpu.VMEM((bands * 32 + 32, 128), single),
        pltpu.VMEM((8, longitudes), single),
        pltpu.VMEM((4, 8, longitudes), single),
        pltpu.VMEM(chunks, narrow),
        pltpu.VMEM((2,) + chunks, narrow),
        pltpu.VMEM(chunks, narrow),
        pltpu.VMEM((2,) + chunks, narrow),
        pltpu.VMEM((2, 2, channels, wide), narrow),
        pltpu.VMEM((2, 2, wide, channels), narrow),
        pltpu.VMEM((count, channels), single),
        pltpu.VMEM((count, 2 * wide), narrow),
        pltpu.VMEM((count, channels), narrow),
        pltpu.VMEM((count, channels), narrow),
        pltpu.VMEM((2, 4, rows, packed, 128), narrow),
        pltpu.VMEM((2, 4, rows, packed, 128), narrow),
        pltpu.VMEM((4, 40, 256), single),
        pltpu.VMEM((2, 3, cells, ocean_channels), narrow),
        pltpu.VMEM((2, 2 * rows, 16, ocean_channels), narrow),
        pltpu.VMEM((2, 2, 3, 16, ocean_channels), narrow),
        pltpu.VMEM((8, 8, 256), single),
        pltpu.VMEM((rows, 8, 128), single),
        pltpu.VMEM((8, rows, 8, 128), single),
        pltpu.VMEM((2, 2 * rows + 6, cells + 16, 128), single),
        pltpu.VMEM((2 * rows, cells, ocean_channels), single),
        pltpu.VMEM((2 * cells, waves), narrow),
        pltpu.VMEM((4, rows, packed, 128), narrow),
        pltpu.VMEM((4, rows, packed, 128), narrow),
        pltpu.VMEM((2, 8, channels), single),
        pltpu.VMEM((2, 8, 256), single),
        pltpu.VMEM((2, 2, 2 * slot, 2 * slot), narrow),
        pltpu.VMEM((2, 8, 2 * slot), single),
        pltpu.VMEM((40, 256), single),
        pltpu.VMEM((8, 256), single),
        pltpu.VMEM((128, levels), single),
        pltpu.VMEM((2, 128, levels), narrow),
        pltpu.VMEM((24, ocean_channels), narrow),
        pltpu.VMEM((count, channels), single),
        pltpu.VMEM((rows, longitudes, 256), single),
        pltpu.VMEM((2 * rows, 8, cells), single),
        pltpu.VMEM((8, 128), single),
        pltpu.VMEM((4, 8, 128), single),
        pltpu.VMEM((cells + 16, 16), single),
        pltpu.VMEM((256, 128), single),
        dma(4), dma(4), dma(2, bands), dma(2, bands), dma(2, bands), dma(2, bands),
        dma(2, 2, 4), dma(2, 2, 4), dma(1), dma(1), dma(2, 4), dma(2, 4), dma(2, 2), dma(2, 2), dma(2, 2),
        dma(4), dma(4), dma(8), dma(8), dma(8), dma(8), dma(8), dma(8), dma(4), dma(4),
        dma(4), dma(4),
    ]
    atmosphere_next, ocean_next, surface = pl.pallas_call(
        functools.partial(step_kernel, bands),
        out_shape=(
            jax.ShapeDtypeStruct(atmosphere.shape, narrow),
            jax.ShapeDtypeStruct(ocean_state.shape, narrow),
            jax.ShapeDtypeStruct((2 * rows, 4, cells), single),
        ),
        in_specs=specs,
        out_specs=(inside,) * 3,
        scratch_shapes=scratch,
        compiler_params=pltpu.CompilerParams(
            collective_id=0, has_side_effects=True, vmem_limit_bytes=63 << 20
        ),
    )(*arguments)
    return (atmosphere_next, ocean_next, surface.transpose(0, 2, 1))


def solution(mesh):
    placed = (
        P("band", None, ("comp", "tile")),
        P(None, None, None, ("comp", "tile"), None),
        P(None, None, None, ("comp", "tile")),
        P(),
        P(),
        P(None, None, ("comp", "tile")),
        P(None, ("comp", "tile"), None),
        P(("comp", "tile"), None),
        P(),
        P("band", ("comp", "tile"), None),
        P("band", ("comp", "tile")),
        P(),
        P(),
        P(),
        P(),
        P(),
        P(),
        P(),
        P(None, ("comp", "tile")),
    )
    return jax.shard_map(
        on_device,
        mesh=mesh,
        in_specs=placed,
        out_specs=(
            P("band", None, ("comp", "tile")),
            P("band", ("comp", "tile"), None),
            P("band", ("comp", "tile"), None),
        ),
        check_vma=False,
    )
```
